128 devices in a mesh: ep: 32 (over x, z, core), tp: 4 (over y).
Axes of the slice: x: 4, y: 4, z: 4, core: 2. Of those that a mesh axis runs over, the one named last changes fastest.
Arguments:
- cache_pages: bfloat16 [2048, 256, 576], P(('ep', 'tp')), may hold values from -6 to 6
- queries: bfloat16 [2048, 128, 576], P(('ep', 'tp')), may hold values from -400 to 400
- lengths: int32 [2048], replicated, may hold values from 2 to 256, as said below
- swap_slot: int32 [128], replicated, may hold values from 0 to 15
- swap_mask: int32 [1], replicated, may hold values from 1 to 31
- hidden: bfloat16 [2048, 3584], P('ep'), may hold values from -6 to 6
- expert_ids: int32 [2048, 8], P('ep'), may hold values from 0 to 95, all different within a row; in each aligned block of 64 rows (0 to 63, 64 to 127, ...) at most 10 rows name the same one
- gate_weights: float32 [2048, 8], P('ep'), may hold values from 0.1 to 0.6
- w_gate: bfloat16 [96, 3584, 1024], P('ep', None, 'tp'), may hold values from -0.09375 to 0.09375
- w_up: bfloat16 [96, 3584, 1024], P('ep', None, 'tp'), may hold values from -0.09375 to 0.09375
- w_down: bfloat16 [96, 1024, 3584], P('ep', 'tp'), may hold values from -0.1875 to 0.1875
Outputs:
- attention_out: bfloat16 [2048, 128, 512], P(('ep', 'tp'))
- moe_out: bfloat16 [2048, 3584], P('ep', 'tp')
The draws below stay inside these ranges and needn't reach their ends.
Inputs may be any that keep to these rules, and one draw needn't show every extreme that they name: `lengths`: each request's cache holds at least 2 tokens; some request holds exactly 256. `expert_ids`: A row's 8 experts are distinct. Among the 64 rows of one ep rank no expert is named by more than 10 rows, a bound that some block reaches.
All inputs are finite; a program needn't handle non-finite values.
Results may differ from the reference program's by a relative error of at most 0.012.
Values may be sent and summed in bfloat16 or wider, within the bound.
A program may use at most 128 MiB of HBM per device.

```python
import math
import jax
import jax.numpy as jnp
import numpy as np
from jax import lax

D = 3584
FF = 1024
HEADS = 128
LAT = 512
KV = 576
TOPK = 8
EXPERTS = 96
REQ_DEV = 64
REQ_LOCAL = 16
REQS = 2048
CTX = 256
CAP = 10
N_EP = 32
N_TP = 4


def trade_slots(key):
    return jax.random.randint(jax.random.fold_in(key, 11), (REQS // REQ_LOCAL,), 0, REQ_LOCAL).astype(jnp.int32)


def full_cache(key):
    full_shape = (REQS, CTX, KV)
    return jax.random.truncated_normal(jax.random.fold_in(key, 21), -5.0, 5.0, full_shape, jnp.float32)


def draw_cache_pages(key, part):
    return full_cache(key).astype(jnp.bfloat16)


def draw_queries(key, part):
    full_shape = (REQS, HEADS, KV)
    base_vals = 2.0 * jax.random.truncated_normal(jax.random.fold_in(key, 31), -5.0, 5.0, full_shape, jnp.float32)
    return base_vals.astype(jnp.bfloat16)


def draw_lengths(key, part):
    group_count = REQS // REQ_LOCAL
    base_vals = jax.random.randint(jax.random.fold_in(key, 41), (REQS,), 0, CTX - 1)
    factor = jax.random.randint(jax.random.fold_in(key, 42), (group_count,), 1, 5)
    spread = jnp.repeat(factor, REQ_LOCAL)
    size_vals = 2 + base_vals * spread // 4
    longest = jax.random.randint(jax.random.fold_in(key, 43), (), 0, REQS)
    return jnp.where(jnp.arange(REQS) == longest, CTX, size_vals).astype(jnp.int32)


def draw_swap_slot(key, part):
    return trade_slots(key)


def block_levels(own_key, shape, split, low, largest):
    def one(axis_at, parts):
        steps = jax.random.uniform(jax.random.fold_in(jax.random.fold_in(own_key, 6), axis_at), (parts,), jnp.float32, low / len(split), largest / len(split))
        return jnp.repeat(jnp.exp(steps), shape[axis_at] // parts).reshape((-1,) + (1,) * (len(shape) - axis_at - 1))

    factor_of = one(*split[0])
    for cut in split[1:]:
        factor_of = factor_of * one(*cut)
    return factor_of


def routed_block(own_key, own, number, rows, count, top, reach, skew):
    order = jax.random.permutation(own_key, count)
    heavy_load, ordinary = shares(count, rows * top, reach, skew, True), shares(count, rows * top, reach, skew, False)
    places = jnp.arange(count)

    def named(tallies, rotation):
        used = int((tallies > 0).sum())
        fixed = max(1, used // 4)
        passed = fixed + (places - fixed + rotation * (used - fixed)) % max(1, count - fixed)
        return jnp.zeros((count,), jnp.int32).at[order[jnp.where(places < fixed, places, passed)]].set(jnp.asarray(tallies, jnp.int32))

    tallies = jnp.where(number % 4 == 0, named(heavy_load, number // 4), named(ordinary, number - number // 4 - 1))
    mixed = jax.random.permutation(jax.random.fold_in(own, 3), count)
    donor, taker = mixed[0:count // 2 * 2:2], mixed[1:count // 2 * 2:2]
    room = jnp.minimum(tallies[donor] - 1, reach - tallies[taker]) // 2
    room = jnp.where((donor == order[0]) | (taker == order[0]) | (tallies[taker] == 0), 0, jnp.maximum(room, 0))
    passed = jax.random.randint(jax.random.fold_in(own, 4), (count // 2,), 0, 1 << 20) % (room + 1)
    tallies = tallies.at[donor].add(-passed).at[taker].add(passed)
    members = jnp.searchsorted(jnp.cumsum(tallies), jnp.arange(rows * top), side="right").astype(jnp.int32)
    table = members.reshape(top, rows).T
    table = table[jax.random.permutation(jax.random.fold_in(own, 1), rows)]
    rotation = jax.random.randint(jax.random.fold_in(own, 2), (rows, 1), 0, top)
    return jnp.take_along_axis(table, (jnp.arange(top)[None, :] + rotation) % top, axis=1)


def shares(count, total, most, lean, full):
    weights = [(1 << 20) // math.isqrt(rank ** lean) + 1 for rank in range(1, count + 1)]
    largest = most if full else min(most, max(-(-total // count), total * weights[0] // sum(weights)))
    least = 1 if total - largest >= count - 1 else 0
    counts, rest = [largest] + [least] * (count - 1), total - largest - least * (count - 1)
    while rest > 0:
        candidates = [i for i in range(1, count) if counts[i] < largest] or [i for i in range(1, count) if counts[i] < most]
        whole, remaining = sum([weights[i] for i in candidates]), rest
        for i in candidates:
            extra = min(most - counts[i], max(1, remaining * weights[i] // whole), rest)
            counts[i] = counts[i] + extra
            rest = rest - extra
    return np.array(counts)


def gaussian(stream_key, shape, scale, bound, pieces=(), kind=jnp.bfloat16):
    drawn = scale * jax.random.normal(stream_key, shape, jnp.float32)
    if pieces:
        drawn = drawn * block_levels(stream_key, shape, pieces, -0.22, 0.18)
    return jnp.clip(drawn, -bound, bound).astype(kind)


def setup_inputs(seed: int = 0) -> dict:
    streams_of = jax.random.split(jax.random.key(seed), 12)
    cache_pages = draw_cache_pages(jax.random.fold_in(streams_of[11], 71), 0)
    queries = draw_queries(jax.random.fold_in(streams_of[11], 71), 0)
    lengths = draw_lengths(jax.random.fold_in(streams_of[11], 71), 0)
    swap_slot = draw_swap_slot(jax.random.fold_in(streams_of[11], 71), 0)
    swap_mask = jax.random.randint(streams_of[4], (1,), 1, N_EP).astype(jnp.int32)
    hidden = gaussian(streams_of[5], (REQS, D), 1.0, 6.0, ((0, 32),))
    expert_ids_keys = jax.random.split(jax.random.fold_in(streams_of[6], 1), REQS // REQ_DEV)
    expert_ids_turns = jax.random.permutation(jax.random.fold_in(streams_of[6], 3), REQS // REQ_DEV)
    expert_ids = jax.vmap(lambda own, number: routed_block(jax.random.fold_in(streams_of[6], 2), own, number, REQ_DEV, EXPERTS, TOPK, CAP, 2))(expert_ids_keys, expert_ids_turns).reshape((REQS, TOPK))
    gate_weights = jnp.clip(0.1 + 0.5 * jax.random.uniform(streams_of[7], (REQS, TOPK), jnp.float32) ** block_levels(streams_of[7], (REQS, TOPK), ((0, 32),), -0.2, 0.2), 0.1, 0.6)
    w_gate = gaussian(streams_of[8], (EXPERTS, D, FF), D ** -0.5, 0.09375, ((0, 32), (2, 4)))
    w_up = gaussian(streams_of[9], (EXPERTS, D, FF), D ** -0.5, 0.09375, ((0, 32), (2, 4)))
    w_down = gaussian(streams_of[10], (EXPERTS, FF, D), FF ** -0.5, 0.1875, ((0, 32), (1, 4)))
    return dict(cache_pages=cache_pages, queries=queries, lengths=lengths, swap_slot=swap_slot, swap_mask=swap_mask, hidden=hidden, expert_ids=expert_ids, gate_weights=gate_weights, w_gate=w_gate, w_up=w_up, w_down=w_down)


SCORE_SCALE = 192.0 ** -0.5
MASK_FLOOR = -1.0e30


def attend(query_row, page_rows, length):
    scores = jnp.dot(query_row, page_rows.T, preferred_element_type=jnp.float32) * SCORE_SCALE
    live_mask = jnp.arange(page_rows.shape[0], dtype=jnp.int32) < length
    scores = jnp.where(live_mask[None, :], scores, MASK_FLOOR)
    top_score = jnp.max(scores, axis=1, keepdims=True)
    weight = jnp.where(live_mask[None, :], jnp.exp(scores - top_score), 0.0)
    totals = jnp.sum(weight, axis=1, keepdims=True)
    weight_low = weight.astype(jnp.bfloat16)
    blended = jnp.dot(weight_low, page_rows[:, :LAT], preferred_element_type=jnp.float32)
    return (blended / totals).astype(jnp.bfloat16)


def reference(cache_pages, queries, lengths, swap_slot, swap_mask, hidden, expert_ids, gate_weights, w_gate, w_up, w_down):
    req_index = jnp.arange(REQS, dtype=jnp.int32)
    device = req_index // REQ_LOCAL
    slot_pos = req_index % REQ_LOCAL
    partner = (jnp.bitwise_xor(device // N_TP, swap_mask[0]) * N_TP + device % N_TP).astype(jnp.int32)
    is_moved = slot_pos == swap_slot[device]
    source = jnp.where(is_moved, partner * REQ_LOCAL + swap_slot[partner], req_index).astype(jnp.int32)

    def single(request):
        anchor = source[request]
        return attend(queries[request], cache_pages[anchor], lengths[anchor])

    attention_out = lax.map(single, req_index)

    pair_count = REQ_DEV * TOPK
    flat_ids = expert_ids.reshape(N_EP, pair_count).astype(jnp.int32)
    onehot = (flat_ids[:, :, None] == jnp.arange(EXPERTS, dtype=jnp.int32)[None, None, :]).astype(jnp.int32)
    pair_rank = jnp.sum(jnp.cumsum(onehot, axis=1) * onehot, axis=2) - 1
    slot_id = (jnp.arange(N_EP, dtype=jnp.int32)[:, None] * CAP + pair_rank).astype(jnp.int32)
    token_ids = (jnp.arange(N_EP, dtype=jnp.int32)[:, None] * REQ_DEV + jnp.arange(pair_count, dtype=jnp.int32)[None, :] // TOPK).astype(jnp.int32)
    slot_table = jnp.full((EXPERTS, N_EP * CAP), -1, jnp.int32).at[flat_ids.reshape(-1), slot_id.reshape(-1)].set(token_ids.reshape(-1))
    share_width = FF // N_TP

    def expert_block(expert):
        row_ids = slot_table[expert]
        inputs = jnp.where((row_ids >= 0)[:, None], hidden[jnp.maximum(row_ids, 0)], jnp.zeros((), jnp.bfloat16))
        gate_act = jnp.dot(inputs, w_gate[expert], preferred_element_type=jnp.float32)
        up_act = jnp.dot(inputs, w_up[expert], preferred_element_type=jnp.float32)
        inner_act = (jax.nn.silu(gate_act) * up_act).astype(jnp.bfloat16)
        down_rows = w_down[expert]
        totals = jnp.zeros((row_ids.shape[0], D), jnp.float32)
        for share_index in range(N_TP):
            lower = share_index * share_width
            share_out = jnp.dot(inner_act[:, lower:lower + share_width], down_rows[lower:lower + share_width], preferred_element_type=jnp.float32).astype(jnp.bfloat16)
            share_out = lax.optimization_barrier(share_out)
            totals = totals + share_out.astype(jnp.float32)
        return totals.astype(jnp.bfloat16)

    expert_out = lax.map(expert_block, jnp.arange(EXPERTS, dtype=jnp.int32))
    picked = expert_out[flat_ids, slot_id]
    weights = gate_weights.reshape(N_EP, pair_count).astype(jnp.float32)
    moe_rows = (picked.astype(jnp.float32) * weights[:, :, None]).reshape(N_EP, REQ_DEV, TOPK, D).sum(axis=2)
    return attention_out, moe_rows.reshape(REQS, D).astype(jnp.bfloat16)
```

```python
import functools

import jax
import jax.numpy as jnp
from jax import lax
from jax.experimental import pallas as pl
from jax.experimental.pallas import tpu as pltpu
from jax.sharding import PartitionSpec as P

MESH = pl.DeviceIdType.MESH
BF = jnp.bfloat16
F32 = jnp.float32
LAT = 512
D = 3584
ROWS = 64
CAP = 10
EXL = 3
META = 256
XW = D + META
GROUP = 512
GSLOT = 80
HALF = D // 2
BLK = D // 4
FFL = 256
SCORE_SCALE = 192.0 ** (-0.5)
MASK_FLOOR = -1e30
VMEM_MAX = 60 * 1024 * 1024


def coords():
    e = lax.axis_index("ep")
    return e // 8, lax.rem(e // 2, 4), lax.rem(e, 2), lax.axis_index("tp")


def wrap(v):
    return lax.rem(v + 4, 4)


def greet(targets):
    barrier = pltpu.get_barrier_semaphore()
    for target in targets:
        pl.semaphore_signal(barrier, inc=1, device_id=target, device_id_type=MESH)
    pl.semaphore_wait(barrier, len(targets))


def gather_kernel(x_ref, wd_ref, xg_ref, wdp_ref, ssem, rsem1, rsem2, dsend, drecv, wsem, lsem):
    x, z, c, y = coords()

    def dev(xx, zz, cc):
        return (xx * 8 + zz * 2 + cc, y)

    other = dev(x, z, 1 - c)
    greet([dev(wrap(x + 1), z, c), dev(wrap(x - 1), z, c), dev(x, wrap(z + 1), c), dev(x, wrap(z - 1), c), other])

    started = []
    count = [0, 0]

    def ship(col, src, dst, target, recv):
        copy = pltpu.make_async_remote_copy(
            src_ref=src,
            dst_ref=dst,
            send_sem=ssem.at[col, count[col]],
            recv_sem=recv,
            device_id=target,
            device_id_type=MESH,
        )
        count[col] += 1
        copy.start()
        started.append(copy)
        return copy

    first = (x, z)
    second = (z, x)

    def place(col, f, s, lo=0, size=32):
        xx, zz = (f, s) if col == 0 else (s, f)
        return xg_ref.at[xx, zz, c, pl.ds(col * 32 + lo, size)]

    def fdev(col, f):
        return dev(f, z, c) if col == 0 else dev(x, f, c)

    def sdev(col, s):
        return dev(x, s, c) if col == 0 else dev(s, z, c)

    def own(col):
        return x_ref.at[pl.ds(col * 32, 32)]

    def expect(ref, sem):
        pltpu.make_async_copy(ref, ref, sem).wait()

    def share(col, f, s, src=None):
        xx, zz = (f, s) if col == 0 else (s, f)
        slot = xx * 4 + zz
        ref = place(col, f, s)
        copy = pltpu.make_async_remote_copy(
            src_ref=ref if src is None else src,
            dst_ref=ref,
            send_sem=dsend.at[col, slot],
            recv_sem=drecv.at[col, slot],
            device_id=other,
            device_id_type=MESH,
        )
        copy.start()
        started.append(copy)

    def fan(col, k, f, src=None):
        s = second[col]
        ref = place(col, f, s)
        src = ref if src is None else src
        ship(col, src, ref, sdev(col, wrap(s + 1)), rsem2.at[col, k, 0])
        ship(col, src, ref, sdev(col, wrap(s - 1)), rsem2.at[col, k, 1])

    def relay2(col, k, f):
        s = second[col]
        back, ahead = place(col, f, wrap(s - 1)), place(col, f, wrap(s + 1))
        expect(back, rsem2.at[col, k, 0])
        ref = place(col, f, wrap(s - 1), 0, 16)
        ship(col, ref, ref, sdev(col, wrap(s + 1)), rsem2.at[col, k, 2])
        share(col, f, wrap(s - 1))
        expect(ahead, rsem2.at[col, k, 1])
        ref = place(col, f, wrap(s + 1), 16, 16)
        ship(col, ref, ref, sdev(col, wrap(s - 1)), rsem2.at[col, k, 3])
        share(col, f, wrap(s + 1))

    def last2(col, k, f):
        s = wrap(second[col] + 2)
        expect(place(col, f, s, 0, 16), rsem2.at[col, k, 2])
        expect(place(col, f, s, 16, 16), rsem2.at[col, k, 3])
        share(col, f, s)

    for col in (0, 1):
        p, s = first[col], second[col]
        ref = place(col, p, s)
        ship(col, own(col), ref, fdev(col, wrap(p + 1)), rsem1.at[col, 0])
        ship(col, own(col), ref, fdev(col, wrap(p - 1)), rsem1.at[col, 1])
    for col in (0, 1):
        fan(col, 0, first[col], own(col))
        share(col, first[col], second[col], own(col))
    local = pltpu.make_async_copy(x_ref, xg_ref.at[x, z, c], lsem)
    local.start()
    far = pl.ds(pl.multiple_of((1 - c) * HALF, HALF), HALF)
    weights = pltpu.make_async_remote_copy(
        src_ref=wd_ref.at[:, :, far],
        dst_ref=wdp_ref,
        send_sem=wsem.at[0],
        recv_sem=wsem.at[1],
        device_id=other,
        device_id_type=MESH,
    )
    weights.start()
    for col in (0, 1):
        p, s = first[col], second[col]
        expect(place(col, wrap(p - 1), s), rsem1.at[col, 0])
        ref = place(col, wrap(p - 1), s, 0, 16)
        ship(col, ref, ref, fdev(col, wrap(p + 1)), rsem1.at[col, 2])
        fan(col, 1, wrap(p - 1))
        share(col, wrap(p - 1), s)
        expect(place(col, wrap(p + 1), s), rsem1.at[col, 1])
        ref = place(col, wrap(p + 1), s, 16, 16)
        ship(col, ref, ref, fdev(col, wrap(p - 1)), rsem1.at[col, 3])
        fan(col, 2, wrap(p + 1))
        share(col, wrap(p + 1), s)
    for col in (0, 1):
        relay2(col, 0, first[col])
    for col in (0, 1):
        p, s = first[col], second[col]
        expect(place(col, wrap(p + 2), s, 0, 16), rsem1.at[col, 2])
        expect(place(col, wrap(p + 2), s, 16, 16), rsem1.at[col, 3])
        fan(col, 3, wrap(p + 2))
        share(col, wrap(p + 2), s)
    for col in (0, 1):
        relay2(col, 1, wrap(first[col] - 1))
        relay2(col, 2, wrap(first[col] + 1))
    for col in (0, 1):
        last2(col, 0, first[col])
    for col in (0, 1):
        relay2(col, 3, wrap(first[col] + 2))
    for col in (0, 1):
        last2(col, 1, wrap(first[col] - 1))
        last2(col, 2, wrap(first[col] + 1))
    for col in (0, 1):
        last2(col, 3, wrap(first[col] + 2))
    for col in (0, 1):
        for slot in range(16):
            expect(xg_ref.at[slot // 4, slot % 4, 1 - c, pl.ds(col * 32, 32)], drecv.at[col, slot])
    weights.wait_recv()
    for copy in started:
        copy.wait_send()
    weights.wait_send()
    local.wait()


def gather_rows(xin, w_down):
    return pl.pallas_call(
        gather_kernel,
        out_shape=(
            jax.ShapeDtypeStruct((4, 4, 2, ROWS, XW), BF),
            jax.ShapeDtypeStruct((EXL, FFL, HALF), BF),
        ),
        in_specs=[pl.BlockSpec(memory_space=pltpu.VMEM), pl.BlockSpec(memory_space=pl.ANY)],
        out_specs=(pl.BlockSpec(memory_space=pl.ANY), pl.BlockSpec(memory_space=pl.ANY)),
        scratch_shapes=[
            pltpu.SemaphoreType.DMA((2, 20)),
            pltpu.SemaphoreType.DMA((2, 4)),
            pltpu.SemaphoreType.DMA((2, 4, 4)),
            pltpu.SemaphoreType.DMA((2, 16)),
            pltpu.SemaphoreType.DMA((2, 16)),
            pltpu.SemaphoreType.DMA((2,)),
            pltpu.SemaphoreType.DMA,
        ],
        compiler_params=pltpu.CompilerParams(
            collective_id=0, has_side_effects=True, vmem_limit_bytes=VMEM_MAX
        ),
        name="gather_rows",
    )(xin, w_down)


def slot_numbers(shape, axis):
    s = lax.broadcasted_iota(jnp.int32, shape, axis)
    g = lax.broadcasted_iota(jnp.int32, shape, 1 - axis)
    expert = jnp.zeros(shape, jnp.int32)
    for k in range(1, shape[axis] // GSLOT):
        expert = expert + (s >= k * GSLOT).astype(jnp.int32)
    u = s - expert * GSLOT
    rank = (u * 205) >> 11
    want = jnp.where((g >> 6) == rank, u - rank * CAP + 1, -1)
    return want.astype(F32)


def expert_lanes(shape, axis, base):
    s = lax.broadcasted_iota(jnp.int32, shape, axis)
    e = lax.broadcasted_iota(jnp.int32, shape, 1 - axis)
    expert = jnp.zeros(shape, jnp.int32)
    for k in range(1, shape[axis] // GSLOT):
        expert = expert + (s >= k * GSLOT).astype(jnp.int32)
    return jnp.where(expert + base == e, 1.0, 0.0).astype(BF)


def up_kernel(base_ref, x_ref, wg_hbm, wu_hbm, out_ref, xc, want, lanes, wg, wu, sem):
    q = pl.program_id(0)
    gate_copy = pltpu.make_async_copy(wg_hbm, wg, sem.at[0])
    up_copy = pltpu.make_async_copy(wu_hbm, wu, sem.at[1])

    @pl.when(q == 0)
    def _():
        gate_copy.start()
        up_copy.start()
        want[...] = slot_numbers((EXL * GSLOT, GROUP), 0)
        lanes[...] = expert_lanes((EXL * GSLOT, 128), 0, base_ref[0])

    table = x_ref[0, :, D : D + 128]
    named = lax.dot_general(lanes[...], table, (((1,), (1,)), ((), ())), preferred_element_type=F32)
    pick = jnp.where(named == want[...], 1.0, 0.0).astype(BF)
    start = pl.multiple_of(q * GSLOT, 16)

    @pl.loop(0, D // 512)
    def _(n):
        cols = pl.ds(pl.multiple_of(n * 512, 512), 512)
        rows = jnp.dot(pick, x_ref[0, :, cols], preferred_element_type=F32).astype(BF)
        for e in range(EXL):
            xc[e, pl.ds(start, GSLOT), cols] = rows[e * GSLOT : (e + 1) * GSLOT]

    @pl.when(q == 3)
    def _():
        gate_copy.wait()
        up_copy.wait()

        @pl.loop(0, EXL)
        def _(e):
            gate = jnp.dot(xc[e], wg[e], preferred_element_type=F32)
            up = jnp.dot(xc[e], wu[e], preferred_element_type=F32)
            out_ref[e] = (gate / (1.0 + jnp.exp(-gate)) * up).astype(BF)


def experts_up(base, xg, w_gate, w_up):
    return pl.pallas_call(
        up_kernel,
        out_shape=jax.ShapeDtypeStruct((EXL, 4 * GSLOT, FFL), BF),
        grid_spec=pltpu.PrefetchScalarGridSpec(
            num_scalar_prefetch=1,
            grid=(4,),
            in_specs=[
                pl.BlockSpec((1, GROUP, XW), lambda q, b: (q, 0, 0)),
                pl.BlockSpec(memory_space=pl.ANY),
                pl.BlockSpec(memory_space=pl.ANY),
            ],
            out_specs=pl.BlockSpec((EXL, 4 * GSLOT, FFL), lambda q, b: (0, 0, 0)),
            scratch_shapes=[
                pltpu.VMEM((EXL, 4 * GSLOT, D), BF),
                pltpu.VMEM((EXL * GSLOT, GROUP), F32),
                pltpu.VMEM((EXL * GSLOT, 128), BF),
                pltpu.VMEM((EXL, D, FFL), BF),
                pltpu.VMEM((EXL, D, FFL), BF),
                pltpu.SemaphoreType.DMA((2,)),
            ],
        ),
        compiler_params=pltpu.CompilerParams(vmem_limit_bytes=VMEM_MAX),
        name="experts_up",
    )(base, xg, w_gate, w_up)


def combine_kernel(
    inner_ref, wd_hbm, wdp_hbm, xg_hbm, out_ref,
    inner2, wdh, meta, outc, want, yp, st1, fin1, st2, fin2, fin3, land,
    lsem, isem, s1, r1, s2, r2, s3, r3, esem,
):
    x, z, c, y = coords()

    def dev(xx, zz, cc, yy):
        return (xx * 8 + zz * 2 + cc, yy)

    other = dev(x, z, 1 - c, y)
    greet(
        [dev(wrap(x + 1), z, c, y), dev(wrap(x - 1), z, c, y), dev(x, wrap(z + 1), c, y), dev(x, wrap(z - 1), c, y)]
        + [other]
        + [dev(x, z, c, wrap(y + k)) for k in (1, 2, 3)]
    )
    waits = []

    def ship(src, dst, target, send, recv):
        copy = pltpu.make_async_remote_copy(
            src_ref=src, dst_ref=dst, send_sem=send, recv_sem=recv, device_id=target, device_id_type=MESH
        )
        copy.start()
        waits.append(copy)
        return copy

    def expect(ref, sem):
        pltpu.make_async_copy(ref, ref, sem).wait()

    swap = ship(inner_ref, inner2, other, isem.at[0], isem.at[1])
    near = pl.ds(pl.multiple_of(c * HALF, HALF), HALF)
    loads = [
        pltpu.make_async_copy(wd_hbm.at[:, :, near], wdh.at[c], lsem.at[0]),
        pltpu.make_async_copy(wdp_hbm, wdh.at[1 - c], lsem.at[1]),
        pltpu.make_async_copy(xg_hbm.at[:, :, pl.ds(D, META)], meta, lsem.at[2]),
    ]
    for load in loads:
        load.start()
    want[...] = slot_numbers((GROUP, 2 * EXL * GSLOT), 1)
    lanes = expert_lanes((128, 2 * EXL * GSLOT), 1, (x * 4 + z) * 2 * EXL)

    def down(core, source):
        @pl.loop(0, EXL)
        def _(e):
            row = pl.multiple_of((core * EXL + e) * GSLOT, 16)
            for n in range(2):
                cols = slice(n * BLK, (n + 1) * BLK)
                part = jnp.dot(source[e], wdh[core, e, :, cols], preferred_element_type=F32).astype(BF)
                for q in range(4):
                    outc[n, q, pl.ds(row, GSLOT), :] = part[q * GSLOT : (q + 1) * GSLOT]

    loads[0].wait()
    down(c, inner_ref)
    loads[1].wait()
    swap.wait_recv()
    down(1 - c, inner2)
    loads[2].wait()

    def scatter(col):
        @pl.loop(0, 4)
        def _(q):
            named = jnp.dot(meta[q, :, 0:128], lanes, preferred_element_type=F32)
            gate = jnp.dot(meta[q, :, 128:256], lanes, preferred_element_type=F32)
            mix = jnp.where(named == want[...], gate, 0.0).astype(BF)
            part = jnp.dot(mix, outc[col, q], preferred_element_type=F32).astype(BF)
            for k in range(4):
                piece = part[k * 128 : (k + 1) * 128]
                if col == 0:
                    yp[0, q, k] = piece
                else:
                    yp[1, k, q] = piece

    first, second = (x, z), (z, x)

    def fdev(col, f):
        return dev(f, z, c, y) if col == 0 else dev(x, f, c, y)

    def sdev(col, s):
        return dev(x, s, c, y) if col == 0 else dev(s, z, c, y)

    def open1(col):
        p = first[col]
        up, dn = fdev(col, wrap(p + 1)), fdev(col, wrap(p - 1))
        ship(yp.at[col, wrap(p + 2), pl.ds(0, 2)], st1.at[col, 0], up, s1.at[col, 0], r1.at[col, 0])
        ship(yp.at[col, wrap(p + 2), pl.ds(2, 2)], st1.at[col, 1], dn, s1.at[col, 1], r1.at[col, 1])
        ship(yp.at[col, wrap(p + 1), pl.ds(2, 2)], fin1.at[col, 0, pl.ds(2, 2)], up, s1.at[col, 2], r1.at[col, 2])
        ship(yp.at[col, wrap(p - 1), pl.ds(0, 2)], fin1.at[col, 1, pl.ds(0, 2)], dn, s1.at[col, 3], r1.at[col, 3])

    def mid1(col):
        p = first[col]
        up, dn = fdev(col, wrap(p + 1)), fdev(col, wrap(p - 1))
        for side, (f, lo, target) in enumerate(((wrap(p + 1), 0, up), (wrap(p - 1), 2, dn))):
            expect(st1.at[col, side], r1.at[col, side])
            for k in range(2):
                acc = yp[col, f, lo + k].astype(F32) + st1[col, side, k].astype(F32)
                yp[col, f, lo + k] = acc.astype(BF)
            ship(
                yp.at[col, f, pl.ds(lo, 2)],
                fin1.at[col, side, pl.ds(lo, 2)],
                target,
                s1.at[col, 4 + side],
                r1.at[col, 4 + side],
            )

    def end1(col):
        p, s = first[col], second[col]
        for side, lo in ((0, 2), (1, 0), (0, 0), (1, 2)):
            expect(
                fin1.at[col, side, pl.ds(lo, 2)],
                r1.at[col, {(0, 2): 2, (1, 0): 3, (0, 0): 4, (1, 2): 5}[(side, lo)]],
            )
        up, dn = sdev(col, wrap(s + 1)), sdev(col, wrap(s - 1))

        def fold(t):
            acc = yp[col, p, t].astype(F32) + fin1[col, 0, t].astype(F32) + fin1[col, 1, t].astype(F32)
            yp[col, p, t] = acc.astype(BF)

        lo, hi = pl.ds(0, 64), pl.ds(64, 64)
        t = wrap(s + 2)
        fold(t)
        ship(yp.at[col, p, t, lo], st2.at[col, 0], up, s2.at[col, 0], r2.at[col, 0])
        ship(yp.at[col, p, t, hi], st2.at[col, 1], dn, s2.at[col, 1], r2.at[col, 1])
        t = wrap(s + 1)
        fold(t)
        ship(yp.at[col, p, t, hi], fin2.at[col, 0, hi], up, s2.at[col, 2], r2.at[col, 2])
        t = wrap(s - 1)
        fold(t)
        ship(yp.at[col, p, t, lo], fin2.at[col, 1, lo], dn, s2.at[col, 3], r2.at[col, 3])
        fold(s)

    def mid2(col):
        p, s = first[col], second[col]
        up, dn = sdev(col, wrap(s + 1)), sdev(col, wrap(s - 1))
        for side, (t, lo, target) in enumerate(((wrap(s + 1), 0, up), (wrap(s - 1), 64, dn))):
            expect(st2.at[col, side], r2.at[col, side])
            acc = yp[col, p, t, lo : lo + 64].astype(F32) + st2[col, side].astype(F32)
            yp[col, p, t, lo : lo + 64] = acc.astype(BF)
            rows = pl.ds(lo, 64)
            ship(
                yp.at[col, p, t, rows], fin2.at[col, side, rows], target, s2.at[col, 4 + side], r2.at[col, 4 + side]
            )

    def end2(col):
        p, s = first[col], second[col]
        for side, lo, k in ((0, 64, 2), (1, 0, 3), (0, 0, 4), (1, 64, 5)):
            expect(fin2.at[col, side, pl.ds(lo, 64)], r2.at[col, k])
        acc = yp[col, p, s].astype(F32) + fin2[col, 0].astype(F32) + fin2[col, 1].astype(F32)
        yp[col, p, s] = acc.astype(BF)
        goal = 2 * c + col
        for k in (1, 2, 3):

            @pl.when(wrap(goal + k) == y)
            def _():
                copy = pltpu.make_async_remote_copy(
                    src_ref=yp.at[col, p, s],
                    dst_ref=fin3.at[k - 1],
                    send_sem=s3.at[col],
                    recv_sem=r3.at[k - 1],
                    device_id=dev(x, z, c, goal),
                    device_id_type=MESH,
                )
                copy.start()

    def end3(col):
        p, s = first[col], second[col]

        @pl.when(y == 2 * c + col)
        def _():
            for k in range(3):
                expect(fin3.at[k], r3.at[k])
            acc = yp[col, p, s].astype(F32)
            for k in range(3):
                acc = acc + fin3[k].astype(F32)
            yp[col, p, s] = acc.astype(BF)
            copy = pltpu.make_async_remote_copy(
                src_ref=yp.at[col, p, s, pl.ds(pl.multiple_of((1 - c) * 64, 64), 64)],
                dst_ref=land,
                send_sem=esem.at[0],
                recv_sem=esem.at[1],
                device_id=other,
                device_id_type=MESH,
            )
            copy.start()
            out_ref[...] = yp[col, p, s, pl.ds(pl.multiple_of(c * 64, 64), 64)]
            copy.wait_send()

        @pl.when(y != 2 * c + col)
        def _():
            expect(yp.at[col, p, s], s3.at[col])

    scatter(0)
    open1(0)
    scatter(1)
    open1(1)
    for step in (mid1, end1, mid2, end2, end3):
        for col in (0, 1):
            step(col)

    @pl.when(y // 2 != c)
    def _():
        expect(land, esem.at[1])
        out_ref[...] = land[...]

    for copy in waits:
        copy.wait_send()


def combine(inner, w_down, wd_far, xg):
    return pl.pallas_call(
        combine_kernel,
        out_shape=jax.ShapeDtypeStruct((ROWS, BLK), BF),
        in_specs=[pl.BlockSpec(memory_space=pltpu.VMEM)] + [pl.BlockSpec(memory_space=pl.ANY)] * 3,
        out_specs=pl.BlockSpec(memory_space=pltpu.VMEM),
        scratch_shapes=[
            pltpu.VMEM((EXL, 4 * GSLOT, FFL), BF),
            pltpu.VMEM((2, EXL, FFL, HALF), BF),
            pltpu.VMEM((4, GROUP, META), BF),
            pltpu.VMEM((2, 4, 2 * EXL * GSLOT, BLK), BF),
            pltpu.VMEM((GROUP, 2 * EXL * GSLOT), F32),
            pltpu.VMEM((2, 4, 4, 128, BLK), BF),
            pltpu.VMEM((2, 2, 2, 128, BLK), BF),
            pltpu.VMEM((2, 2, 4, 128, BLK), BF),
            pltpu.VMEM((2, 2, 64, BLK), BF),
            pltpu.VMEM((2, 2, 128, BLK), BF),
            pltpu.VMEM((3, 128, BLK), BF),
            pltpu.VMEM((64, BLK), BF),
            pltpu.SemaphoreType.DMA((3,)),
            pltpu.SemaphoreType.DMA((2,)),
            pltpu.SemaphoreType.DMA((2, 6)),
            pltpu.SemaphoreType.DMA((2, 6)),
            pltpu.SemaphoreType.DMA((2, 6)),
            pltpu.SemaphoreType.DMA((2, 6)),
            pltpu.SemaphoreType.DMA((2,)),
            pltpu.SemaphoreType.DMA((3,)),
            pltpu.SemaphoreType.DMA((2,)),
        ],
        compiler_params=pltpu.CompilerParams(
            collective_id=1, has_side_effects=True, vmem_limit_bytes=VMEM_MAX
        ),
        name="combine",
    )(inner, w_down, wd_far, xg)


def attend_kernel(slot_ref, lens_ref, q_ref, page_ref, far_ref, out_ref):
    r = pl.program_id(0)
    page = jnp.where(r == slot_ref[0], far_ref[...], page_ref[0])
    scores = lax.dot_general(q_ref[0], page, (((1,), (1,)), ((), ())), preferred_element_type=F32)
    scores = scores * SCORE_SCALE
    live = lax.broadcasted_iota(jnp.int32, scores.shape, 1) < lens_ref[r]
    scores = jnp.where(live, scores, MASK_FLOOR)
    weight = jnp.where(live, jnp.exp(scores - jnp.max(scores, axis=1, keepdims=True)), 0.0)
    total = jnp.sum(weight, axis=1, keepdims=True)
    blended = jnp.dot(weight.astype(BF), page[:, :LAT], preferred_element_type=F32)
    out_ref[0] = (blended / total).astype(BF)


def attend(slot, lens, queries, pages, far):
    count, heads, width = queries.shape
    ctx = pages.shape[1]
    return pl.pallas_call(
        attend_kernel,
        out_shape=jax.ShapeDtypeStruct((count, heads, LAT), BF),
        grid_spec=pltpu.PrefetchScalarGridSpec(
            num_scalar_prefetch=2,
            grid=(count,),
            in_specs=[
                pl.BlockSpec((1, heads, width), lambda r, *_: (r, 0, 0)),
                pl.BlockSpec((1, ctx, width), lambda r, *_: (r, 0, 0)),
                pl.BlockSpec((ctx, width), lambda r, *_: (0, 0)),
            ],
            out_specs=pl.BlockSpec((1, heads, LAT), lambda r, *_: (r, 0, 0)),
        ),
        name="attend",
    )(slot, lens, queries, pages, far)


def trade(page, mask):
    count = lax.axis_size("ep")

    def branch(m):
        return lambda block: lax.ppermute(block, "ep", [(i, i ^ m) for i in range(count)])

    return lax.switch(mask - 1, [branch(m) for m in range(1, count)], page)


def local(
    cache_pages,
    queries,
    lengths,
    swap_slot,
    swap_mask,
    hidden,
    expert_ids,
    gate_weights,
    w_gate,
    w_up,
    w_down,
):
    ep_rank = lax.axis_index("ep")
    groups = lax.axis_size("tp")
    tp_rank = lax.axis_index("tp")

    lane = jnp.arange(128, dtype=jnp.int32)
    hits = expert_ids[:, :, None] == lane[None, None, :]
    chosen = jnp.any(hits, axis=1)
    gates = jnp.sum(jnp.where(hits, gate_weights[:, :, None], 0.0), axis=1)
    upto = jnp.arange(ROWS)[:, None] >= jnp.arange(ROWS)[None, :]
    place = jnp.dot(upto.astype(BF), chosen.astype(BF), preferred_element_type=F32)
    table = jnp.where(chosen, place, 0.0)
    xin = jnp.concatenate([hidden, table.astype(BF), gates.astype(BF)], axis=1)
    xg, wd_far = gather_rows(xin, w_down)
    xg = xg.reshape(4, GROUP, XW)
    base = (ep_rank * EXL).astype(jnp.int32).reshape(1)
    inner = experts_up(base, xg, w_gate, w_up)
    moe_rows = combine(inner, w_down, wd_far, xg)

    count = cache_pages.shape[0]
    device = ep_rank * groups + tp_rank
    partner = jnp.bitwise_xor(ep_rank, swap_mask[0]) * groups + tp_rank
    my_slot = swap_slot[device]
    far_slot = swap_slot[partner]
    own_lengths = lax.dynamic_slice_in_dim(lengths, device * count, count)
    live_lengths = jnp.where(
        jnp.arange(count, dtype=jnp.int32) == my_slot, lengths[partner * count + far_slot], own_lengths
    )
    own_page = lax.dynamic_index_in_dim(cache_pages, my_slot, 0, keepdims=False)
    arrived = trade(own_page, swap_mask[0])
    attended = attend(my_slot.reshape(1), live_lengths, queries, cache_pages, arrived)
    return attended, moe_rows


def solution(mesh):
    in_specs = (
        P(("ep", "tp"), None, None),
        P(("ep", "tp"), None, None),
        P(),
        P(),
        P(),
        P("ep", None),
        P("ep", None),
        P("ep", None),
        P("ep", None, "tp"),
        P("ep", None, "tp"),
        P("ep", "tp", None),
    )
    out_specs = (P(("ep", "tp"), None, None), P("ep", "tp"))
    return jax.shard_map(local, mesh=mesh, in_specs=in_specs, out_specs=out_specs, check_vma=False)
```

```python
import functools

import jax
import jax.numpy as jnp
from jax import lax
from jax.experimental import pallas as pl
from jax.experimental.pallas import tpu as pltpu
from jax.sharding import PartitionSpec as P

MESH = pl.DeviceIdType.MESH
BF = jnp.bfloat16
F32 = jnp.float32
LAT = 512
D = 3584
ROWS = 64
CAP = 10
EXL = 3
META = 256
GROUP = 512
GSLOT = 80
HALF = D // 2
BLK = D // 4
FFL = 256
SCORE_SCALE = 192.0 ** (-0.5)
MASK_FLOOR = -1e30
VMEM_MAX = 60 * 1024 * 1024


def coords():
    e = lax.axis_index("ep")
    return e // 8, lax.rem(e // 2, 4), lax.rem(e, 2), lax.axis_index("tp")


def wrap(v):
    return lax.rem(v + 4, 4)


def greet(targets):
    barrier = pltpu.get_barrier_semaphore()
    for target in targets:
        pl.semaphore_signal(barrier, inc=1, device_id=target, device_id_type=MESH)
    pl.semaphore_wait(barrier, len(targets))


QUARTER = 256
MAIN = D - 4 * QUARTER
WHOLE = MAIN + META


def gather_kernel(
    x_ref, xp_ref, wd_ref, xg_ref, xq_ref, wdp_ref,
    ssem, rsem1, rsem2, dsend, drecv, ysend, yrecv, ydsend, ydrecv, wsem, lsem,
):
    x, z, c, y = coords()

    def dev(xx, zz, cc):
        return (xx * 8 + zz * 2 + cc, y)

    other = dev(x, z, 1 - c)
    above, below = (x * 8 + z * 2 + c, wrap(y + 1)), (x * 8 + z * 2 + c, wrap(y - 1))
    started = []
    count = {}

    def push(src, dst, target, send, recv):
        copy = pltpu.make_async_remote_copy(
            src_ref=src, dst_ref=dst, send_sem=send, recv_sem=recv, device_id=target, device_id_type=MESH
        )
        copy.start()
        started.append(copy)

    def ship(part, col, src, dst, target, recv):
        k = count.get((part, col), 0)
        count[part, col] = k + 1
        push(src, dst, target, ssem.at[part, col, k], recv)

    first = (x, z)
    second = (z, x)

    def place(part, col, f, s, lo=0, size=32):
        xx, zz = (f, s) if col == 0 else (s, f)
        rows = pl.ds(col * 32 + lo, size)
        return xg_ref.at[xx, zz, c, rows] if part else xq_ref.at[y, xx, zz, c, rows]

    def line(col, s, yy, lo=0, size=4, core=c):
        rows = pl.ds(col * 32, 32)
        if col == 0:
            return xq_ref.at[yy, pl.ds(lo, size), s, core, rows]
        return xq_ref.at[yy, s, pl.ds(lo, size), core, rows]

    def fdev(col, f):
        return dev(f, z, c) if col == 0 else dev(x, f, c)

    def sdev(col, s):
        return dev(x, s, c) if col == 0 else dev(s, z, c)

    def own(part, col):
        rows = pl.ds(col * 32, 32)
        return x_ref.at[rows] if part else xp_ref.at[y, rows]

    def expect(ref, sem):
        pltpu.make_async_copy(ref, ref, sem).wait()

    def share(part, col, f, s, src=None):
        if part == 0:
            return
        xx, zz = (f, s) if col == 0 else (s, f)
        slot = xx * 4 + zz
        ref = place(part, col, f, s)
        push(ref if src is None else src, ref, other, dsend.at[col, slot], drecv.at[col, slot])

    def fan(part, col, k, f, src=None):
        s = second[col]
        ref = place(part, col, f, s)
        src = ref if src is None else src
        ship(part, col, src, ref, sdev(col, wrap(s + 1)), rsem2.at[part, col, k, 0])
        ship(part, col, src, ref, sdev(col, wrap(s - 1)), rsem2.at[part, col, k, 1])

    def relay2(part, col, k, f):
        s = second[col]
        expect(place(part, col, f, wrap(s - 1)), rsem2.at[part, col, k, 0])
        ref = place(part, col, f, wrap(s - 1), 0, 16)
        ship(part, col, ref, ref, sdev(col, wrap(s + 1)), rsem2.at[part, col, k, 2])
        share(part, col, f, wrap(s - 1))
        expect(place(part, col, f, wrap(s + 1)), rsem2.at[part, col, k, 1])
        ref = place(part, col, f, wrap(s + 1), 16, 16)
        ship(part, col, ref, ref, sdev(col, wrap(s - 1)), rsem2.at[part, col, k, 3])
        share(part, col, f, wrap(s + 1))

    def last2(part, col, k, f):
        s = wrap(second[col] + 2)
        expect(place(part, col, f, s, 0, 16), rsem2.at[part, col, k, 2])
        expect(place(part, col, f, s, 16, 16), rsem2.at[part, col, k, 3])
        share(part, col, f, s)

    def open1(part):
        for col in (0, 1):
            p, s = first[col], second[col]
            ref = place(part, col, p, s)
            ship(part, col, own(part, col), ref, fdev(col, wrap(p + 1)), rsem1.at[part, col, 0])
            ship(part, col, own(part, col), ref, fdev(col, wrap(p - 1)), rsem1.at[part, col, 1])

    def relay1(part):
        for col in (0, 1):
            p, s = first[col], second[col]
            expect(place(part, col, wrap(p - 1), s), rsem1.at[part, col, 0])
            ref = place(part, col, wrap(p - 1), s, 0, 16)
            ship(part, col, ref, ref, fdev(col, wrap(p + 1)), rsem1.at[part, col, 2])
            expect(place(part, col, wrap(p + 1), s), rsem1.at[part, col, 1])
            ref = place(part, col, wrap(p + 1), s, 16, 16)
            ship(part, col, ref, ref, fdev(col, wrap(p - 1)), rsem1.at[part, col, 3])
            if part:
                for k, f in ((1, wrap(p - 1)), (2, wrap(p + 1))):
                    fan(1, col, k, f)
                    share(1, col, f, s)

    def last1(part, col):
        p, s = first[col], second[col]
        expect(place(part, col, wrap(p + 2), s, 0, 16), rsem1.at[part, col, 2])
        expect(place(part, col, wrap(p + 2), s, 16, 16), rsem1.at[part, col, 3])

    def source(col, k):
        return wrap(first[col] + (0, -1, 1, 2)[k])

    def lines_out(col):
        s = second[col]
        ref = line(col, s, y)
        ship(0, col, ref, ref, sdev(col, wrap(s + 1)), rsem2.at[0, col, 0, 0])
        ship(0, col, ref, ref, sdev(col, wrap(s - 1)), rsem2.at[0, col, 0, 1])

    def lines_on(col):
        s = second[col]
        expect(line(col, wrap(s - 1), y), rsem2.at[0, col, 0, 0])
        ref = line(col, wrap(s - 1), y, 0, 2)
        ship(0, col, ref, ref, sdev(col, wrap(s + 1)), rsem2.at[0, col, 0, 2])
        expect(line(col, wrap(s + 1), y), rsem2.at[0, col, 0, 1])
        ref = line(col, wrap(s + 1), y, 2, 2)
        ship(0, col, ref, ref, sdev(col, wrap(s - 1)), rsem2.at[0, col, 0, 3])

    def lines_in(col):
        s = wrap(second[col] + 2)
        expect(line(col, s, y, 0, 2), rsem2.at[0, col, 0, 2])
        expect(line(col, s, y, 2, 2), rsem2.at[0, col, 0, 3])

    def part_of(yy, lo, size=2, core=c):
        return xq_ref.at[yy, pl.ds(lo, size), :, core]

    def hand(d):
        ref = part_of(wrap(y + d), 0, 4)
        push(ref, ref, other, ydsend.at[d], ydrecv.at[d])

    locals_ = [
        pltpu.make_async_copy(xp_ref.at[y], xq_ref.at[y, x, z, c], lsem.at[0]),
        pltpu.make_async_copy(x_ref, xg_ref.at[x, z, c], lsem.at[1]),
    ]
    for copy in locals_:
        copy.start()
    greet(
        [dev(wrap(x + 1), z, c), dev(wrap(x - 1), z, c), dev(x, wrap(z + 1), c), dev(x, wrap(z - 1), c)]
        + [other, above, below]
    )
    open1(0)
    open1(1)
    far = pl.ds(pl.multiple_of((1 - c) * HALF, HALF), HALF)
    push(wd_ref.at[:, :, far], wdp_ref, other, wsem.at[0], wsem.at[1])
    relay1(0)
    locals_[0].wait()
    for col in (0, 1):
        last1(0, col)
        lines_out(col)
    for col in (0, 1):
        lines_on(col)
    for col in (0, 1):
        fan(1, col, 0, first[col], own(1, col))
        share(1, col, first[col], second[col], own(1, col))
    relay1(1)
    for col in (0, 1):
        lines_in(col)
    for k, lo, target in ((0, 0, above), (2, 2, below), (1, 2, above), (3, 0, below)):
        ref = part_of(y, lo)
        push(ref, ref, target, ysend.at[k], yrecv.at[k])
    hand(0)
    for col in (0, 1):
        relay2(1, col, 0, source(col, 0))
    for col in (0, 1):
        last1(1, col)
        fan(1, col, 3, source(col, 3))
        share(1, col, source(col, 3), second[col])
    ref = part_of(wrap(y - 1), 0)
    expect(ref, yrecv.at[0])
    push(ref, ref, above, ysend.at[4], yrecv.at[4])
    ref = part_of(wrap(y + 1), 2)
    expect(ref, yrecv.at[2])
    push(ref, ref, below, ysend.at[5], yrecv.at[5])
    for k in (1, 2):
        for col in (0, 1):
            relay2(1, col, k, source(col, k))
    for col in (0, 1):
        last2(1, col, 0, source(col, 0))
    expect(part_of(wrap(y - 1), 2), yrecv.at[1])
    hand(3)
    expect(part_of(wrap(y + 1), 0), yrecv.at[3])
    hand(1)
    for col in (0, 1):
        relay2(1, col, 3, source(col, 3))
    expect(part_of(wrap(y + 2), 0), yrecv.at[4])
    expect(part_of(wrap(y + 2), 2), yrecv.at[5])
    hand(2)
    for k in (1, 2, 3):
        for col in (0, 1):
            last2(1, col, k, source(col, k))
    for col in (0, 1):
        for slot in range(16):
            expect(xg_ref.at[slot // 4, slot % 4, 1 - c, pl.ds(col * 32, 32)], drecv.at[col, slot])
    for d in range(4):
        expect(part_of(wrap(y + d), 0, 4, 1 - c), ydrecv.at[d])
    expect(wdp_ref, wsem.at[1])
    locals_[1].wait()
    for copy in started:
        copy.wait_send()


def gather_rows(xmain, xparts, w_down):
    dma = pltpu.SemaphoreType.DMA
    return pl.pallas_call(
        gather_kernel,
        out_shape=(
            jax.ShapeDtypeStruct((4, 4, 2, ROWS, WHOLE), BF),
            jax.ShapeDtypeStruct((4, 4, 4, 2, ROWS, QUARTER), BF),
            jax.ShapeDtypeStruct((EXL, FFL, HALF), BF),
        ),
        in_specs=[pl.BlockSpec(memory_space=pltpu.VMEM)] * 2 + [pl.BlockSpec(memory_space=pl.ANY)],
        out_specs=(pl.BlockSpec(memory_space=pl.ANY),) * 3,
        scratch_shapes=[
            dma((2, 2, 20)),
            dma((2, 2, 4)),
            dma((2, 2, 4, 4)),
            dma((2, 16)),
            dma((2, 16)),
            dma((6,)),
            dma((6,)),
            dma((4,)),
            dma((4,)),
            dma((2,)),
            dma((2,)),
        ],
        compiler_params=pltpu.CompilerParams(
            collective_id=0, has_side_effects=True, vmem_limit_bytes=VMEM_MAX
        ),
        name="gather_rows",
    )(xmain, xparts, w_down)


def slot_numbers(shape, axis):
    s = lax.broadcasted_iota(jnp.int32, shape, axis)
    g = lax.broadcasted_iota(jnp.int32, shape, 1 - axis)
    expert = jnp.zeros(shape, jnp.int32)
    for k in range(1, shape[axis] // GSLOT):
        expert = expert + (s >= k * GSLOT).astype(jnp.int32)
    u = s - expert * GSLOT
    rank = (u * 205) >> 11
    want = jnp.where((g >> 6) == rank, u - rank * CAP + 1, -1)
    return want.astype(F32)


def expert_lanes(shape, axis, base):
    s = lax.broadcasted_iota(jnp.int32, shape, axis)
    e = lax.broadcasted_iota(jnp.int32, shape, 1 - axis)
    expert = jnp.zeros(shape, jnp.int32)
    for k in range(1, shape[axis] // GSLOT):
        expert = expert + (s >= k * GSLOT).astype(jnp.int32)
    return jnp.where(expert + base == e, 1.0, 0.0).astype(BF)


def up_kernel(base_ref, x_ref, xp_ref, wg_hbm, wu_hbm, out_ref, xc, want, lanes, wg, wu, sem):
    q = pl.program_id(0)
    gate_copy = pltpu.make_async_copy(wg_hbm, wg, sem.at[0])
    up_copy = pltpu.make_async_copy(wu_hbm, wu, sem.at[1])

    @pl.when(q == 0)
    def _():
        gate_copy.start()
        up_copy.start()
        want[...] = slot_numbers((EXL * GSLOT, GROUP), 0)
        lanes[...] = expert_lanes((EXL * GSLOT, 128), 0, base_ref[0])

    table = x_ref[0, :, MAIN : MAIN + 128]
    named = lax.dot_general(lanes[...], table, (((1,), (1,)), ((), ())), preferred_element_type=F32)
    pick = jnp.where(named == want[...], 1.0, 0.0).astype(BF)
    start = pl.multiple_of(q * GSLOT, 16)

    def keep(rows, cols):
        for e in range(EXL):
            xc[e, pl.ds(start, GSLOT), cols] = rows[e * GSLOT : (e + 1) * GSLOT].astype(BF)

    @pl.loop(0, MAIN // 512)
    def _(n):
        cols = pl.ds(pl.multiple_of(n * 512, 512), 512)
        keep(jnp.dot(pick, x_ref[0, :, cols], preferred_element_type=F32), cols)

    @pl.loop(0, 4)
    def _(n):
        cols = pl.ds(pl.multiple_of(MAIN + n * QUARTER, 128), QUARTER)
        keep(jnp.dot(pick, xp_ref[n, 0], preferred_element_type=F32), cols)

    @pl.when(q == 3)
    def _():
        gate_copy.wait()
        up_copy.wait()

        @pl.loop(0, EXL)
        def _(e):
            gate = jnp.dot(xc[e], wg[e], preferred_element_type=F32)
            up = jnp.dot(xc[e], wu[e], preferred_element_type=F32)
            out_ref[e] = (gate / (1.0 + jnp.exp(-gate)) * up).astype(BF)


def experts_up(base, xg, xq, w_gate, w_up):
    return pl.pallas_call(
        up_kernel,
        out_shape=jax.ShapeDtypeStruct((EXL, 4 * GSLOT, FFL), BF),
        grid_spec=pltpu.PrefetchScalarGridSpec(
            num_scalar_prefetch=1,
            grid=(4,),
            in_specs=[
                pl.BlockSpec((1, GROUP, WHOLE), lambda q, b: (q, 0, 0)),
                pl.BlockSpec((4, 1, GROUP, QUARTER), lambda q, b: (0, q, 0, 0)),
                pl.BlockSpec(memory_space=pl.ANY),
                pl.BlockSpec(memory_space=pl.ANY),
            ],
            out_specs=pl.BlockSpec((EXL, 4 * GSLOT, FFL), lambda q, b: (0, 0, 0)),
            scratch_shapes=[
                pltpu.VMEM((EXL, 4 * GSLOT, D), BF),
                pltpu.VMEM((EXL * GSLOT, GROUP), F32),
                pltpu.VMEM((EXL * GSLOT, 128), BF),
                pltpu.VMEM((EXL, D, FFL), BF),
                pltpu.VMEM((EXL, D, FFL), BF),
                pltpu.SemaphoreType.DMA((2,)),
            ],
        ),
        cost_estimate=pl.CostEstimate(flops=7_000_000_000, bytes_accessed=30_000_000, transcendentals=0),
        compiler_params=pltpu.CompilerParams(vmem_limit_bytes=VMEM_MAX),
        name="experts_up",
    )(base, xg, xq, w_gate, w_up)


def combine_kernel(
    inner_ref, wd_hbm, wdp_hbm, xg_hbm, out_ref,
    inner2, wdh, meta, outc, want, yp, st1, fin1, st2, fin2, fin3,
    lsem, isem, s1, r1, s2, r2, s3, r3,
):
    x, z, c, y = coords()

    def dev(xx, zz, cc, yy):
        return (xx * 8 + zz * 2 + cc, yy)

    other = dev(x, z, 1 - c, y)
    waits = []

    def ship(src, dst, target, send, recv):
        copy = pltpu.make_async_remote_copy(
            src_ref=src, dst_ref=dst, send_sem=send, recv_sem=recv, device_id=target, device_id_type=MESH
        )
        copy.start()
        waits.append(copy)
        return copy

    def expect(ref, sem):
        pltpu.make_async_copy(ref, ref, sem).wait()

    near = pl.ds(pl.multiple_of(c * HALF, HALF), HALF)
    loads = [
        pltpu.make_async_copy(wd_hbm.at[:, :, near], wdh.at[c], lsem.at[0]),
        pltpu.make_async_copy(wdp_hbm, wdh.at[1 - c], lsem.at[1]),
        pltpu.make_async_copy(xg_hbm.at[:, :, pl.ds(MAIN, META)], meta, lsem.at[2]),
    ]
    for load in loads:
        load.start()
    want[...] = slot_numbers((GROUP, 2 * EXL * GSLOT), 1)
    lanes = expert_lanes((128, 2 * EXL * GSLOT), 1, (x * 4 + z) * 2 * EXL)
    greet(
        [dev(wrap(x + 1), z, c, y), dev(wrap(x - 1), z, c, y), dev(x, wrap(z + 1), c, y), dev(x, wrap(z - 1), c, y)]
        + [other]
        + [dev(x, z, core, wrap(y + k)) for k in (1, 2, 3) for core in (0, 1)]
    )
    swap = ship(inner_ref, inner2, other, isem.at[0], isem.at[1])

    def down(core, source):
        @pl.loop(0, EXL)
        def _(e):
            row = pl.multiple_of((core * EXL + e) * GSLOT, 16)
            for n in range(2):
                cols = slice(n * BLK, (n + 1) * BLK)
                part = jnp.dot(source[e], wdh[core, e, :, cols], preferred_element_type=F32).astype(BF)
                for q in range(4):
                    outc[n, q, pl.ds(row, GSLOT), :] = part[q * GSLOT : (q + 1) * GSLOT]

    loads[0].wait()
    down(c, inner_ref)
    loads[1].wait()
    swap.wait_recv()
    down(1 - c, inner2)
    loads[2].wait()

    def scatter(col):
        @pl.loop(0, 4)
        def _(q):
            named = jnp.dot(meta[q, :, 0:128], lanes, preferred_element_type=F32)
            gate = jnp.dot(meta[q, :, 128:256], lanes, preferred_element_type=F32)
            mix = jnp.where(named == want[...], gate, 0.0).astype(BF)
            part = jnp.dot(mix, outc[col, q], preferred_element_type=F32).astype(BF)
            for k in range(4):
                piece = part[k * 128 : (k + 1) * 128]
                if col == 0:
                    yp[0, q, k] = piece
                else:
                    yp[1, k, q] = piece

    first, second = (x, z), (z, x)

    def fdev(col, f):
        return dev(f, z, c, y) if col == 0 else dev(x, f, c, y)

    def sdev(col, s):
        return dev(x, s, c, y) if col == 0 else dev(s, z, c, y)

    def open1(col):
        p = first[col]
        up, dn = fdev(col, wrap(p + 1)), fdev(col, wrap(p - 1))
        ship(yp.at[col, wrap(p + 2), pl.ds(0, 2)], st1.at[col, 0], up, s1.at[col, 0], r1.at[col, 0])
        ship(yp.at[col, wrap(p + 2), pl.ds(2, 2)], st1.at[col, 1], dn, s1.at[col, 1], r1.at[col, 1])
        ship(yp.at[col, wrap(p + 1), pl.ds(2, 2)], fin1.at[col, 0, pl.ds(2, 2)], up, s1.at[col, 2], r1.at[col, 2])
        ship(yp.at[col, wrap(p - 1), pl.ds(0, 2)], fin1.at[col, 1, pl.ds(0, 2)], dn, s1.at[col, 3], r1.at[col, 3])

    def mid1(col):
        p = first[col]
        up, dn = fdev(col, wrap(p + 1)), fdev(col, wrap(p - 1))
        for side, (f, lo, target) in enumerate(((wrap(p + 1), 0, up), (wrap(p - 1), 2, dn))):
            expect(st1.at[col, side], r1.at[col, side])
            for k in range(2):
                acc = yp[col, f, lo + k].astype(F32) + st1[col, side, k].astype(F32)
                yp[col, f, lo + k] = acc.astype(BF)
            ship(
                yp.at[col, f, pl.ds(lo, 2)],
                fin1.at[col, side, pl.ds(lo, 2)],
                target,
                s1.at[col, 4 + side],
                r1.at[col, 4 + side],
            )

    def end1(col):
        p, s = first[col], second[col]
        for side, lo in ((0, 2), (1, 0), (0, 0), (1, 2)):
            expect(
                fin1.at[col, side, pl.ds(lo, 2)],
                r1.at[col, {(0, 2): 2, (1, 0): 3, (0, 0): 4, (1, 2): 5}[(side, lo)]],
            )
        up, dn = sdev(col, wrap(s + 1)), sdev(col, wrap(s - 1))

        def fold(t):
            acc = yp[col, p, t].astype(F32) + fin1[col, 0, t].astype(F32) + fin1[col, 1, t].astype(F32)
            yp[col, p, t] = acc.astype(BF)

        lo, hi = pl.ds(0, 64), pl.ds(64, 64)
        t = wrap(s + 2)
        fold(t)
        ship(yp.at[col, p, t, lo], st2.at[col, 0], up, s2.at[col, 0], r2.at[col, 0])
        ship(yp.at[col, p, t, hi], st2.at[col, 1], dn, s2.at[col, 1], r2.at[col, 1])
        t = wrap(s + 1)
        fold(t)
        ship(yp.at[col, p, t, hi], fin2.at[col, 0, hi], up, s2.at[col, 2], r2.at[col, 2])
        t = wrap(s - 1)
        fold(t)
        ship(yp.at[col, p, t, lo], fin2.at[col, 1, lo], dn, s2.at[col, 3], r2.at[col, 3])
        fold(s)

    def mid2(col):
        p, s = first[col], second[col]
        up, dn = sdev(col, wrap(s + 1)), sdev(col, wrap(s - 1))
        for side, (t, lo, target) in enumerate(((wrap(s + 1), 0, up), (wrap(s - 1), 64, dn))):
            expect(st2.at[col, side], r2.at[col, side])
            acc = yp[col, p, t, lo : lo + 64].astype(F32) + st2[col, side].astype(F32)
            yp[col, p, t, lo : lo + 64] = acc.astype(BF)
            rows = pl.ds(lo, 64)
            ship(
                yp.at[col, p, t, rows], fin2.at[col, side, rows], target, s2.at[col, 4 + side], r2.at[col, 4 + side]
            )

    def end2(col):
        p, s = first[col], second[col]
        for side, lo, k in ((0, 64, 2), (1, 0, 3), (0, 0, 4), (1, 64, 5)):
            expect(fin2.at[col, side, pl.ds(lo, 64)], r2.at[col, k])
        acc = yp[col, p, s].astype(F32) + fin2[col, 0].astype(F32) + fin2[col, 1].astype(F32)
        yp[col, p, s] = acc.astype(BF)
        goal = 2 * c + col

        def final(core, target, k):
            pltpu.make_async_remote_copy(
                src_ref=yp.at[col, p, s, pl.ds(pl.multiple_of(core * 64, 64), 64)],
                dst_ref=fin3.at[k],
                send_sem=s3.at[col, core],
                recv_sem=r3.at[k],
                device_id=target,
                device_id_type=MESH,
            ).start()

        @pl.when(y == goal)
        def _():
            final(1 - c, other, 0)

        for k in (1, 2, 3):

            @pl.when(wrap(goal + k) == y)
            def _():
                for core in (0, 1):
                    final(core, dev(x, z, core, goal), k)

    def end3(col):
        p, s = first[col], second[col]
        half = yp.at[col, p, s, pl.ds(0, 64)]
        expect(half, s3.at[col, 1 - c])

        @pl.when(y != 2 * c + col)
        def _():
            expect(half, s3.at[col, c])

        @pl.when(y == 2 * c + col)
        def _():
            acc = yp[col, p, s, pl.ds(pl.multiple_of(c * 64, 64), 64)].astype(F32)
            for k in (1, 2, 3):
                acc = acc + fin3[k].astype(F32)
            out_ref[...] = acc.astype(BF)

    scatter(0)
    open1(0)
    scatter(1)
    open1(1)
    for step in (mid1, end1, mid2, end2):
        for col in (0, 1):
            step(col)
    for k in (1, 2, 3):
        expect(fin3.at[k], r3.at[k])
    end3(0)
    end3(1)

    @pl.when(y // 2 != c)
    def _():
        expect(fin3.at[0], r3.at[0])
        acc = fin3[0].astype(F32)
        for k in (1, 2, 3):
            acc = acc + fin3[k].astype(F32)
        out_ref[...] = acc.astype(BF)

    for copy in waits:
        copy.wait_send()


def combine(inner, w_down, wd_far, xg):
    return pl.pallas_call(
        combine_kernel,
        out_shape=jax.ShapeDtypeStruct((ROWS, BLK), BF),
        in_specs=[pl.BlockSpec(memory_space=pltpu.VMEM)] + [pl.BlockSpec(memory_space=pl.ANY)] * 3,
        out_specs=pl.BlockSpec(memory_space=pltpu.VMEM),
        scratch_shapes=[
            pltpu.VMEM((EXL, 4 * GSLOT, FFL), BF),
            pltpu.VMEM((2, EXL, FFL, HALF), BF),
            pltpu.VMEM((4, GROUP, META), BF),
            pltpu.VMEM((2, 4, 2 * EXL * GSLOT, BLK), BF),
            pltpu.VMEM((GROUP, 2 * EXL * GSLOT), F32),
            pltpu.VMEM((2, 4, 4, 128, BLK), BF),
            pltpu.VMEM((2, 2, 2, 128, BLK), BF),
            pltpu.VMEM((2, 2, 4, 128, BLK), BF),
            pltpu.VMEM((2, 2, 64, BLK), BF),
            pltpu.VMEM((2, 2, 128, BLK), BF),
            pltpu.VMEM((4, 64, BLK), BF),
            pltpu.SemaphoreType.DMA((3,)),
            pltpu.SemaphoreType.DMA((2,)),
            pltpu.SemaphoreType.DMA((2, 6)),
            pltpu.SemaphoreType.DMA((2, 6)),
            pltpu.SemaphoreType.DMA((2, 6)),
            pltpu.SemaphoreType.DMA((2, 6)),
            pltpu.SemaphoreType.DMA((2, 2)),
            pltpu.SemaphoreType.DMA((4,)),
        ],
        compiler_params=pltpu.CompilerParams(
            collective_id=1, has_side_effects=True, vmem_limit_bytes=VMEM_MAX
        ),
        name="combine",
    )(inner, w_down, wd_far, xg)


def attend_page(query, page, length):
    scores = lax.dot_general(query, page, (((0,), (0,)), ((), ())), preferred_element_type=F32)
    scores = scores * SCORE_SCALE
    live = lax.broadcasted_iota(jnp.int32, scores.shape, 1) < length
    scores = jnp.where(live, scores, MASK_FLOOR)
    weight = jnp.where(live, jnp.exp(scores - jnp.max(scores, axis=1, keepdims=True)), 0.0)
    total = jnp.sum(weight, axis=1, keepdims=True)
    blended = lax.dot_general(
        weight.astype(BF), page[:LAT], (((1,), (1,)), ((), ())), preferred_element_type=F32
    )
    return (blended / total).astype(BF)


def attend_kernel(dev_ref, lens_ref, q_ref, page_ref, out_ref):
    count = q_ref.shape[0]
    base = dev_ref[0] * 16 + pl.program_id(0) * count
    for k in range(count):
        out_ref[k] = attend_page(q_ref[k], page_ref[k], lens_ref[base + k])


def attend(dev, lens, queries, pages):
    count, width, heads = queries.shape
    ctx = pages.shape[2]
    step = 4
    return pl.pallas_call(
        attend_kernel,
        out_shape=jax.ShapeDtypeStruct((count, heads, LAT), BF),
        grid_spec=pltpu.PrefetchScalarGridSpec(
            num_scalar_prefetch=2,
            grid=(count // step,),
            in_specs=[
                pl.BlockSpec((step, width, heads), lambda r, *_: (r, 0, 0)),
                pl.BlockSpec((step, width, ctx), lambda r, *_: (r, 0, 0)),
            ],
            out_specs=pl.BlockSpec((step, heads, LAT), lambda r, *_: (r, 0, 0)),
        ),
        cost_estimate=pl.CostEstimate(flops=2_400_000_000, bytes_accessed=20_000_000, transcendentals=0),
        name="attend",
    )(dev, lens, queries, pages)


def attend_one_kernel(dev_ref, slot_ref, mask_ref, lens_ref, q_ref, page_ref, all_ref, out_ref):
    partner = jnp.bitwise_xor(dev_ref[0], mask_ref[0] * 4)
    length = lens_ref[partner * 16 + slot_ref[partner]]
    out_ref[0] = attend_page(q_ref[0], page_ref[...], length)


def attend_one(dev, slots, mask, lens, queries, page, attended):
    count, width, heads = queries.shape
    return pl.pallas_call(
        attend_one_kernel,
        out_shape=jax.ShapeDtypeStruct(attended.shape, BF),
        grid_spec=pltpu.PrefetchScalarGridSpec(
            num_scalar_prefetch=4,
            grid=(1,),
            in_specs=[
                pl.BlockSpec((1, width, heads), lambda r, dev, slot, *_: (slot[dev[0]], 0, 0)),
                pl.BlockSpec(page.shape, lambda r, *_: (0, 0)),
                pl.BlockSpec(memory_space=pl.ANY),
            ],
            out_specs=pl.BlockSpec((1, heads, LAT), lambda r, dev, slot, *_: (slot[dev[0]], 0, 0)),
        ),
        input_output_aliases={6: 0},
        name="attend_one",
    )(dev, slots, mask, lens, queries, page, attended)


def trade(page, bits, shift, steps, beside):
    count = lax.axis_size("ep")

    def branch(m):
        def run(block):
            if m:
                block = lax.ppermute(block, "ep", [(i, i ^ (m << shift)) for i in range(count)])
            return block, beside()

        return run

    return lax.switch(bits, [branch(m) for m in range(steps)], page)


def prepare_kernel(dev_ref, slot_ref, x_ref, ids_ref, gates_ref, page_ref, out_ref, parts_ref, own_ref):
    own_ref[...] = page_ref[0]
    top = ids_ref.shape[0]
    expert = lax.broadcasted_iota(jnp.int32, (128, ROWS), 0)
    chosen = jnp.zeros((128, ROWS), F32)
    gates = jnp.zeros((128, ROWS), F32)
    for k in range(top):
        hit = expert == ids_ref[k : k + 1, :]
        chosen = jnp.where(hit, 1.0, chosen)
        gates = jnp.where(hit, gates_ref[k : k + 1, :], gates)
    row = lax.broadcasted_iota(jnp.int32, (ROWS, ROWS), 0)
    col = lax.broadcasted_iota(jnp.int32, (ROWS, ROWS), 1)
    upto = jnp.where(row >= col, 1.0, 0.0).astype(BF)
    same = jnp.where(row == col, 1.0, 0.0).astype(BF)
    flip = functools.partial(
        lax.dot_general, dimension_numbers=(((1,), (1,)), ((), ())), preferred_element_type=F32
    )
    chosen = chosen.astype(BF)
    place = jnp.where(flip(same, chosen) > 0.5, flip(upto, chosen), 0.0)
    out_ref[:, :MAIN] = x_ref[:, :MAIN]
    out_ref[:, MAIN : MAIN + 128] = place.astype(BF)
    out_ref[:, MAIN + 128 :] = flip(same, gates.astype(BF)).astype(BF)
    for k in range(4):
        parts_ref[k] = x_ref[:, MAIN + k * QUARTER : MAIN + (k + 1) * QUARTER]


def prepare(dev, slots, hidden, ids, gates, pages):
    count, width, ctx = pages.shape

    def whole(array):
        return pl.BlockSpec(array.shape, lambda r, *_: (0, 0))

    return pl.pallas_call(
        prepare_kernel,
        out_shape=(
            jax.ShapeDtypeStruct((ROWS, WHOLE), BF),
            jax.ShapeDtypeStruct((4, ROWS, QUARTER), BF),
            jax.ShapeDtypeStruct((width, ctx), BF),
        ),
        grid_spec=pltpu.PrefetchScalarGridSpec(
            num_scalar_prefetch=2,
            grid=(1,),
            in_specs=[
                whole(hidden),
                whole(ids),
                whole(gates),
                pl.BlockSpec((1, width, ctx), lambda r, dev, slot: (slot[dev[0]], 0, 0)),
            ],
            out_specs=(
                pl.BlockSpec((ROWS, WHOLE), lambda r, *_: (0, 0)),
                pl.BlockSpec((4, ROWS, QUARTER), lambda r, *_: (0, 0, 0)),
                pl.BlockSpec((width, ctx), lambda r, *_: (0, 0)),
            ),
        ),
        name="prepare",
    )(dev, slots, hidden, ids, gates, pages)


def local(
    cache_pages,
    queries,
    lengths,
    swap_slot,
    swap_mask,
    hidden,
    expert_ids,
    gate_weights,
    w_gate,
    w_up,
    w_down,
):
    ep_rank = lax.axis_index("ep").astype(jnp.int32)
    groups = lax.axis_size("tp")
    tp_rank = lax.axis_index("tp").astype(jnp.int32)
    device = ep_rank * groups + tp_rank
    mask = swap_mask[0]
    dev = device.reshape(1)
    pages = jnp.swapaxes(cache_pages, 1, 2)
    asked = jnp.swapaxes(queries, 1, 2)
    xmain, xparts, own_page = prepare(dev, swap_slot, hidden, expert_ids.T, gate_weights.T, pages)
    page, attended = trade(
        own_page, jnp.right_shift(mask, 3), 3, 4, lambda: attend(dev, lengths, asked, pages)
    )
    xg, xq, wd_far = gather_rows(xmain, xparts, w_down)
    xg = xg.reshape(4, GROUP, WHOLE)
    xq = xq.reshape(4, 4, GROUP, QUARTER)
    base = (ep_rank * EXL).reshape(1)
    page, inner = trade(
        page, jnp.bitwise_and(mask, 7), 0, 8, lambda: experts_up(base, xg, xq, w_gate, w_up)
    )
    moe_rows = combine(inner, w_down, wd_far, xg)
    attended = attend_one(dev, swap_slot, swap_mask, lengths, asked, page, attended)
    return attended, moe_rows


def solution(mesh):
    in_specs = (
        P(("ep", "tp"), None, None),
        P(("ep", "tp"), None, None),
        P(),
        P(),
        P(),
        P("ep", None),
        P("ep", None),
        P("ep", None),
        P("ep", None, "tp"),
        P("ep", None, "tp"),
        P("ep", "tp", None),
    )
    out_specs = (P(("ep", "tp"), None, None), P("ep", "tp"))
    return jax.shard_map(local, mesh=mesh, in_specs=in_specs, out_specs=out_specs, check_vma=False)
```

```python
import functools

import jax
import jax.numpy as jnp
from jax import lax
from jax.experimental import pallas as pl
from jax.experimental.pallas import tpu as pltpu
from jax.sharding import PartitionSpec as P

MESH = pl.DeviceIdType.MESH
BF = jnp.bfloat16
F32 = jnp.float32
LAT = 512
D = 3584
ROWS = 64
CAP = 10
EXL = 3
META = 256
GROUP = 256
GROUPS = 8
GSLOT = 40
PAIR = 2 * GROUP
PSLOT = 2 * GSLOT
HALF = D // 2
BLK = D // 4
FFL = 256
SCORE_SCALE = 192.0 ** (-0.5)
MASK_FLOOR = -1e30
VMEM_MAX = 60 * 1024 * 1024


def coords():
    e = lax.axis_index("ep")
    return e // 8, lax.rem(e // 2, 4), lax.rem(e, 2), lax.axis_index("tp")


def wrap(v):
    return lax.rem(v + 4, 4)


def greet(targets):
    barrier = pltpu.get_barrier_semaphore()
    for target in targets:
        pl.semaphore_signal(barrier, inc=1, device_id=target, device_id_type=MESH)
    pl.semaphore_wait(barrier, len(targets))


QUARTER = 256
MAIN = D - 4 * QUARTER
WHOLE = MAIN + META


def gather_kernel(
    x_ref, xp_ref, wd_ref, xg_ref, xq_ref, wdp_ref,
    ssem, rsem1, rsem2, dsend, drecv, ysend, yrecv, ydsend, ydrecv, wsem, lsem,
):
    x, z, c, y = coords()

    def dev(xx, zz, cc):
        return (xx * 8 + zz * 2 + cc, y)

    other = dev(x, z, 1 - c)
    above, below = (x * 8 + z * 2 + c, wrap(y + 1)), (x * 8 + z * 2 + c, wrap(y - 1))
    started = []
    count = {}

    def push(src, dst, target, send, recv):
        copy = pltpu.make_async_remote_copy(
            src_ref=src, dst_ref=dst, send_sem=send, recv_sem=recv, device_id=target, device_id_type=MESH
        )
        copy.start()
        started.append(copy)

    def ship(part, col, src, dst, target, recv):
        k = count.get((part, col), 0)
        count[part, col] = k + 1
        push(src, dst, target, ssem.at[part, col, k], recv)

    first = (x, z)
    second = (z, x)

    def place(part, col, f, s, lo=0, size=32):
        xx, zz = (f, s) if col == 0 else (s, f)
        rows = pl.ds(col * 32 + lo, size)
        return xg_ref.at[xx, zz, c, rows] if part else xq_ref.at[y, xx, zz, c, rows]

    def line(col, s, yy, lo=0, size=4, core=c):
        rows = pl.ds(col * 32, 32)
        if col == 0:
            return xq_ref.at[yy, pl.ds(lo, size), s, core, rows]
        return xq_ref.at[yy, s, pl.ds(lo, size), core, rows]

    def fdev(col, f):
        return dev(f, z, c) if col == 0 else dev(x, f, c)

    def sdev(col, s):
        return dev(x, s, c) if col == 0 else dev(s, z, c)

    def own(part, col):
        rows = pl.ds(col * 32, 32)
        return x_ref.at[rows] if part else xp_ref.at[y, rows]

    def expect(ref, sem):
        pltpu.make_async_copy(ref, ref, sem).wait()

    def share(part, col, f, s, src=None):
        if part == 0:
            return
        xx, zz = (f, s) if col == 0 else (s, f)
        slot = xx * 4 + zz
        ref = place(part, col, f, s)
        push(ref if src is None else src, ref, other, dsend.at[col, slot], drecv.at[col, slot])

    def fan(part, col, k, f, src=None):
        s = second[col]
        ref = place(part, col, f, s)
        src = ref if src is None else src
        ship(part, col, src, ref, sdev(col, wrap(s + 1)), rsem2.at[part, col, k, 0])
        ship(part, col, src, ref, sdev(col, wrap(s - 1)), rsem2.at[part, col, k, 1])

    def relay2(part, col, k, f):
        s = second[col]
        expect(place(part, col, f, wrap(s - 1)), rsem2.at[part, col, k, 0])
        ref = place(part, col, f, wrap(s - 1), 0, 16)
        ship(part, col, ref, ref, sdev(col, wrap(s + 1)), rsem2.at[part, col, k, 2])
        share(part, col, f, wrap(s - 1))
        expect(place(part, col, f, wrap(s + 1)), rsem2.at[part, col, k, 1])
        ref = place(part, col, f, wrap(s + 1), 16, 16)
        ship(part, col, ref, ref, sdev(col, wrap(s - 1)), rsem2.at[part, col, k, 3])
        share(part, col, f, wrap(s + 1))

    def last2(part, col, k, f):
        s = wrap(second[col] + 2)
        expect(place(part, col, f, s, 0, 16), rsem2.at[part, col, k, 2])
        expect(place(part, col, f, s, 16, 16), rsem2.at[part, col, k, 3])
        share(part, col, f, s)

    def open1(part):
        for col in (0, 1):
            p, s = first[col], second[col]
            ref = place(part, col, p, s)
            ship(part, col, own(part, col), ref, fdev(col, wrap(p + 1)), rsem1.at[part, col, 0])
            ship(part, col, own(part, col), ref, fdev(col, wrap(p - 1)), rsem1.at[part, col, 1])

    def relay1(part):
        for col in (0, 1):
            p, s = first[col], second[col]
            expect(place(part, col, wrap(p - 1), s), rsem1.at[part, col, 0])
            ref = place(part, col, wrap(p - 1), s, 0, 16)
            ship(part, col, ref, ref, fdev(col, wrap(p + 1)), rsem1.at[part, col, 2])
            expect(place(part, col, wrap(p + 1), s), rsem1.at[part, col, 1])
            ref = place(part, col, wrap(p + 1), s, 16, 16)
            ship(part, col, ref, ref, fdev(col, wrap(p - 1)), rsem1.at[part, col, 3])
            if part:
                for k, f in ((1, wrap(p - 1)), (2, wrap(p + 1))):
                    fan(1, col, k, f)
                    share(1, col, f, s)

    def last1(part, col):
        p, s = first[col], second[col]
        expect(place(part, col, wrap(p + 2), s, 0, 16), rsem1.at[part, col, 2])
        expect(place(part, col, wrap(p + 2), s, 16, 16), rsem1.at[part, col, 3])

    def source(col, k):
        return wrap(first[col] + (0, -1, 1, 2)[k])

    def lines_out(col):
        s = second[col]
        ref = line(col, s, y)
        ship(0, col, ref, ref, sdev(col, wrap(s + 1)), rsem2.at[0, col, 0, 0])
        ship(0, col, ref, ref, sdev(col, wrap(s - 1)), rsem2.at[0, col, 0, 1])

    def lines_on(col):
        s = second[col]
        expect(line(col, wrap(s - 1), y), rsem2.at[0, col, 0, 0])
        ref = line(col, wrap(s - 1), y, 0, 2)
        ship(0, col, ref, ref, sdev(col, wrap(s + 1)), rsem2.at[0, col, 0, 2])
        expect(line(col, wrap(s + 1), y), rsem2.at[0, col, 0, 1])
        ref = line(col, wrap(s + 1), y, 2, 2)
        ship(0, col, ref, ref, sdev(col, wrap(s - 1)), rsem2.at[0, col, 0, 3])

    def lines_in(col):
        s = wrap(second[col] + 2)
        expect(line(col, s, y, 0, 2), rsem2.at[0, col, 0, 2])
        expect(line(col, s, y, 2, 2), rsem2.at[0, col, 0, 3])

    def part_of(yy, lo, size=2, core=c):
        return xq_ref.at[yy, pl.ds(lo, size), :, core]

    def hand(d):
        ref = part_of(wrap(y + d), 0, 4)
        push(ref, ref, other, ydsend.at[d], ydrecv.at[d])

    locals_ = [
        pltpu.make_async_copy(xp_ref.at[y], xq_ref.at[y, x, z, c], lsem.at[0]),
        pltpu.make_async_copy(x_ref, xg_ref.at[x, z, c], lsem.at[1]),
    ]
    for copy in locals_:
        copy.start()
    greet(
        [dev(wrap(x + 1), z, c), dev(wrap(x - 1), z, c), dev(x, wrap(z + 1), c), dev(x, wrap(z - 1), c)]
        + [other, above, below]
    )
    open1(0)
    far = pl.ds(pl.multiple_of((1 - c) * HALF, HALF), HALF)
    push(wd_ref.at[:, :, far], wdp_ref, other, wsem.at[0], wsem.at[1])
    relay1(0)
    open1(1)
    locals_[0].wait()
    for col in (0, 1):
        last1(0, col)
        lines_out(col)
    for col in (0, 1):
        lines_on(col)
    for col in (0, 1):
        fan(1, col, 0, first[col], own(1, col))
        share(1, col, first[col], second[col], own(1, col))
    relay1(1)
    for col in (0, 1):
        lines_in(col)
    for k, lo, target in ((0, 0, above), (2, 2, below), (1, 2, above), (3, 0, below)):
        ref = part_of(y, lo)
        push(ref, ref, target, ysend.at[k], yrecv.at[k])
    hand(0)
    for col in (0, 1):
        relay2(1, col, 0, source(col, 0))
    for col in (0, 1):
        last1(1, col)
        fan(1, col, 3, source(col, 3))
        share(1, col, source(col, 3), second[col])
    ref = part_of(wrap(y - 1), 0)
    expect(ref, yrecv.at[0])
    push(ref, ref, above, ysend.at[4], yrecv.at[4])
    ref = part_of(wrap(y + 1), 2)
    expect(ref, yrecv.at[2])
    push(ref, ref, below, ysend.at[5], yrecv.at[5])
    for k in (1, 2):
        for col in (0, 1):
            relay2(1, col, k, source(col, k))
    for col in (0, 1):
        last2(1, col, 0, source(col, 0))
    expect(part_of(wrap(y - 1), 2), yrecv.at[1])
    hand(3)
    expect(part_of(wrap(y + 1), 0), yrecv.at[3])
    hand(1)
    for col in (0, 1):
        relay2(1, col, 3, source(col, 3))
    expect(part_of(wrap(y + 2), 0), yrecv.at[4])
    expect(part_of(wrap(y + 2), 2), yrecv.at[5])
    hand(2)
    for k in (1, 2, 3):
        for col in (0, 1):
            last2(1, col, k, source(col, k))
    for col in (0, 1):
        for slot in range(16):
            expect(xg_ref.at[slot // 4, slot % 4, 1 - c, pl.ds(col * 32, 32)], drecv.at[col, slot])
    for d in range(4):
        expect(part_of(wrap(y + d), 0, 4, 1 - c), ydrecv.at[d])
    expect(wdp_ref, wsem.at[1])
    for copy in locals_[1:]:
        copy.wait()
    for copy in started:
        copy.wait_send()


def gather_rows(xmain, xparts, w_down):
    dma = pltpu.SemaphoreType.DMA
    return pl.pallas_call(
        gather_kernel,
        out_shape=(
            jax.ShapeDtypeStruct((4, 4, 2, ROWS, WHOLE), BF),
            jax.ShapeDtypeStruct((4, 4, 4, 2, ROWS, QUARTER), BF),
            pltpu.HBM((EXL, FFL, HALF), BF),
        ),
        in_specs=[pl.BlockSpec(memory_space=pltpu.VMEM)] * 2 + [pl.BlockSpec(memory_space=pltpu.HBM)],
        out_specs=(pl.BlockSpec(memory_space=pltpu.VMEM),) * 2
        + (pl.BlockSpec(memory_space=pltpu.HBM),),
        scratch_shapes=[
            dma((2, 2, 20)),
            dma((2, 2, 4)),
            dma((2, 2, 4, 4)),
            dma((2, 16)),
            dma((2, 16)),
            dma((6,)),
            dma((6,)),
            dma((4,)),
            dma((4,)),
            dma((2,)),
            dma((2,)),
        ],
        compiler_params=pltpu.CompilerParams(
            collective_id=0, has_side_effects=True, vmem_limit_bytes=18 * 1024 * 1024
        ),
        name="gather_rows",
    )(xmain, xparts, w_down)


def slot_numbers(shape, axis, gslot):
    s = lax.broadcasted_iota(jnp.int32, shape, axis)
    g = lax.broadcasted_iota(jnp.int32, shape, 1 - axis)
    expert = jnp.zeros(shape, jnp.int32)
    for k in range(1, shape[axis] // gslot):
        expert = expert + (s >= k * gslot).astype(jnp.int32)
    u = s - expert * gslot
    rank = (u * 205) >> 11
    want = jnp.where((g >> 6) == rank, u - rank * CAP + 1, -1)
    return want.astype(F32)


def expert_lanes(shape, axis, base, gslot):
    s = lax.broadcasted_iota(jnp.int32, shape, axis)
    e = lax.broadcasted_iota(jnp.int32, shape, 1 - axis)
    expert = jnp.zeros(shape, jnp.int32)
    for k in range(1, shape[axis] // gslot):
        expert = expert + (s >= k * gslot).astype(jnp.int32)
    return jnp.where(expert + base == e, 1.0, 0.0).astype(BF)


def up_kernel(base_ref, x_ref, xp_ref, wg_ref, wu_hbm, out_ref, tab_ref, xc, wu_ref, sem):
    load = pltpu.make_async_copy(wu_hbm, wu_ref, sem)
    load.start()
    tab_ref[...] = x_ref[:, :, MAIN:WHOLE]
    want = slot_numbers((EXL * PSLOT, PAIR), 0, PSLOT)
    lanes = expert_lanes((EXL * PSLOT, 128), 0, base_ref[0], PSLOT)

    @pl.loop(0, GROUPS // 2)
    def _(q):
        table = x_ref[q, :, MAIN : MAIN + 128]
        named = lax.dot_general(lanes, table, (((1,), (1,)), ((), ())), preferred_element_type=F32)
        pick = jnp.where(named == want, 1.0, 0.0).astype(BF)
        start = pl.multiple_of(q * PSLOT, 16)

        def keep(rows, cols):
            for e in range(EXL):
                xc[e, pl.ds(start, PSLOT), cols] = rows[e * PSLOT : (e + 1) * PSLOT].astype(BF)

        @pl.loop(0, MAIN // 512)
        def _(n):
            cols = pl.ds(pl.multiple_of(n * 512, 512), 512)
            keep(jnp.dot(pick, x_ref[q, :, cols], preferred_element_type=F32), cols)

        @pl.loop(0, 4)
        def _(n):
            cols = pl.ds(pl.multiple_of(MAIN + n * QUARTER, 128), QUARTER)
            keep(jnp.dot(pick, xp_ref[n, q], preferred_element_type=F32), cols)

    load.wait()

    @pl.loop(0, EXL)
    def _(e):
        rows = xc[e]
        gate = jnp.dot(rows, wg_ref[e], preferred_element_type=F32)
        up = jnp.dot(rows, wu_ref[e], preferred_element_type=F32)
        out_ref[e] = (gate / (1.0 + jnp.exp(-gate)) * up).astype(BF)


def experts_up(base, xg, xq, w_gate, w_up):
    return pl.pallas_call(
        up_kernel,
        out_shape=(
            jax.ShapeDtypeStruct((EXL, GROUPS * GSLOT, FFL), BF),
            jax.ShapeDtypeStruct((GROUPS // 2, PAIR, META), BF),
        ),
        in_specs=[pl.BlockSpec(memory_space=pltpu.SMEM)]
        + [pl.BlockSpec(memory_space=pltpu.VMEM)] * 3
        + [pl.BlockSpec(memory_space=pltpu.HBM)],
        out_specs=(pl.BlockSpec(memory_space=pltpu.VMEM),) * 2,
        scratch_shapes=[
            pltpu.VMEM((EXL, GROUPS * GSLOT, D), BF),
            pltpu.VMEM((EXL, D, FFL), BF),
            pltpu.SemaphoreType.DMA,
        ],
        cost_estimate=pl.CostEstimate(flops=7_000_000_000, bytes_accessed=30_000_000, transcendentals=0),
        compiler_params=pltpu.CompilerParams(vmem_limit_bytes=20 * 1024 * 1024),
        name="experts_up",
    )(base, xg, xq, w_gate, w_up)


def combine_kernel(
    inner_ref, meta, wd_hbm, wdp_hbm, out_ref,
    inner2, wdh, outc, want, yp, st1, fin1, st2, fin2, fin3,
    lsem, isem, s1, r1, s2, r2, s3, r3,
):
    x, z, c, y = coords()

    def dev(xx, zz, cc, yy):
        return (xx * 8 + zz * 2 + cc, yy)

    other = dev(x, z, 1 - c, y)
    waits = []

    def ship(src, dst, target, send, recv):
        copy = pltpu.make_async_remote_copy(
            src_ref=src, dst_ref=dst, send_sem=send, recv_sem=recv, device_id=target, device_id_type=MESH
        )
        copy.start()
        waits.append(copy)
        return copy

    def expect(ref, sem):
        pltpu.make_async_copy(ref, ref, sem).wait()

    near = pl.ds(pl.multiple_of(c * HALF, HALF), HALF)
    loads = [
        pltpu.make_async_copy(wd_hbm.at[:, :, near], wdh.at[c], lsem.at[0]),
        pltpu.make_async_copy(wdp_hbm, wdh.at[1 - c], lsem.at[1]),
    ]
    for load in loads:
        load.start()
    want[...] = slot_numbers((GROUP, 2 * EXL * GSLOT), 1, GSLOT)
    lanes = expert_lanes((128, 2 * EXL * GSLOT), 1, (x * 4 + z) * 2 * EXL, GSLOT)
    greet(
        [dev(wrap(x + 1), z, c, y), dev(wrap(x - 1), z, c, y), dev(x, wrap(z + 1), c, y), dev(x, wrap(z - 1), c, y)]
        + [other]
        + [dev(x, z, core, wrap(y + k)) for k in (1, 2, 3) for core in (0, 1)]
    )
    swap = ship(inner_ref, inner2, other, isem.at[0], isem.at[1])

    def down(core, source):
        @pl.loop(0, EXL)
        def _(e):
            row = pl.multiple_of((core * EXL + e) * GSLOT, 8)
            for n in range(2):
                cols = slice(n * BLK, (n + 1) * BLK)
                part = jnp.dot(source[e], wdh[core, e, :, cols], preferred_element_type=F32)
                for q in range(GROUPS):
                    outc[n, q, pl.ds(row, GSLOT), :] = part[q * GSLOT : (q + 1) * GSLOT]

    loads[0].wait()
    down(c, inner_ref)
    loads[1].wait()
    swap.wait_recv()
    down(1 - c, inner2)

    def scatter(col, start, count):
        @pl.loop(0, 2 * count)
        def _(i):
            q = wrap(x + start + i // 2) * 2 + lax.rem(i, 2)
            named = jnp.dot(meta[q, :, 0:128], lanes, preferred_element_type=F32)
            gate = jnp.dot(meta[q, :, 128:256], lanes, preferred_element_type=F32)
            mix = jnp.where(named == want[...], gate, 0.0).astype(BF)
            part = jnp.dot(mix, outc[col, q].astype(BF), preferred_element_type=F32).astype(BF)
            xx = q // 2
            for k in range(2):
                piece = part[k * 128 : (k + 1) * 128]
                zz = lax.rem(q, 2) * 2 + k
                if col == 0:
                    yp[0, xx, zz] = piece
                else:
                    yp[1, zz, xx] = piece

    first, second = (x, z), (z, x)

    def fdev(col, f):
        return dev(f, z, c, y) if col == 0 else dev(x, f, c, y)

    def sdev(col, s):
        return dev(x, s, c, y) if col == 0 else dev(s, z, c, y)

    def open0(col):
        p = first[col]
        up, dn = fdev(col, wrap(p + 1)), fdev(col, wrap(p - 1))
        ship(yp.at[col, wrap(p + 2), pl.ds(0, 2)], st1.at[col, 0], up, s1.at[col, 0], r1.at[col, 0])
        ship(yp.at[col, wrap(p + 2), pl.ds(2, 2)], st1.at[col, 1], dn, s1.at[col, 1], r1.at[col, 1])

    def open1(col):
        p = first[col]
        up, dn = fdev(col, wrap(p + 1)), fdev(col, wrap(p - 1))
        ship(yp.at[col, wrap(p + 1), pl.ds(2, 2)], fin1.at[col, 0, pl.ds(2, 2)], up, s1.at[col, 2], r1.at[col, 2])
        ship(yp.at[col, wrap(p - 1), pl.ds(0, 2)], fin1.at[col, 1, pl.ds(0, 2)], dn, s1.at[col, 3], r1.at[col, 3])

    def mid1(col):
        p = first[col]
        up, dn = fdev(col, wrap(p + 1)), fdev(col, wrap(p - 1))
        for side, (f, lo, target) in enumerate(((wrap(p + 1), 0, up), (wrap(p - 1), 2, dn))):
            expect(st1.at[col, side], r1.at[col, side])
            for k in range(2):
                acc = yp[col, f, lo + k].astype(F32) + st1[col, side, k].astype(F32)
                yp[col, f, lo + k] = acc.astype(BF)
            ship(
                yp.at[col, f, pl.ds(lo, 2)],
                fin1.at[col, side, pl.ds(lo, 2)],
                target,
                s1.at[col, 4 + side],
                r1.at[col, 4 + side],
            )

    def end1(col):
        p, s = first[col], second[col]
        for side, lo in ((0, 2), (1, 0), (0, 0), (1, 2)):
            expect(
                fin1.at[col, side, pl.ds(lo, 2)],
                r1.at[col, {(0, 2): 2, (1, 0): 3, (0, 0): 4, (1, 2): 5}[(side, lo)]],
            )
        up, dn = sdev(col, wrap(s + 1)), sdev(col, wrap(s - 1))

        def fold(t):
            acc = yp[col, p, t].astype(F32) + fin1[col, 0, t].astype(F32) + fin1[col, 1, t].astype(F32)
            yp[col, p, t] = acc.astype(BF)

        lo, hi = pl.ds(0, 64), pl.ds(64, 64)
        t = wrap(s + 2)
        fold(t)
        ship(yp.at[col, p, t, lo], st2.at[col, 0], up, s2.at[col, 0], r2.at[col, 0])
        ship(yp.at[col, p, t, hi], st2.at[col, 1], dn, s2.at[col, 1], r2.at[col, 1])
        t = wrap(s + 1)
        fold(t)
        ship(yp.at[col, p, t, hi], fin2.at[col, 0, hi], up, s2.at[col, 2], r2.at[col, 2])
        t = wrap(s - 1)
        fold(t)
        ship(yp.at[col, p, t, lo], fin2.at[col, 1, lo], dn, s2.at[col, 3], r2.at[col, 3])
        fold(s)

    def mid2(col):
        p, s = first[col], second[col]
        up, dn = sdev(col, wrap(s + 1)), sdev(col, wrap(s - 1))
        for side, (t, lo, target) in enumerate(((wrap(s + 1), 0, up), (wrap(s - 1), 64, dn))):
            expect(st2.at[col, side], r2.at[col, side])
            acc = yp[col, p, t, lo : lo + 64].astype(F32) + st2[col, side].astype(F32)
            yp[col, p, t, lo : lo + 64] = acc.astype(BF)
            rows = pl.ds(lo, 64)
            ship(
                yp.at[col, p, t, rows], fin2.at[col, side, rows], target, s2.at[col, 4 + side], r2.at[col, 4 + side]
            )

    def end2(col):
        p, s = first[col], second[col]
        for side, lo, k in ((0, 64, 2), (1, 0, 3), (0, 0, 4), (1, 64, 5)):
            expect(fin2.at[col, side, pl.ds(lo, 64)], r2.at[col, k])
        acc = yp[col, p, s].astype(F32) + fin2[col, 0].astype(F32) + fin2[col, 1].astype(F32)
        yp[col, p, s] = acc.astype(BF)
        goal = 2 * c + col

        def final(core, target, k):
            pltpu.make_async_remote_copy(
                src_ref=yp.at[col, p, s, pl.ds(pl.multiple_of(core * 64, 64), 64)],
                dst_ref=fin3.at[k],
                send_sem=s3.at[col, core],
                recv_sem=r3.at[k],
                device_id=target,
                device_id_type=MESH,
            ).start()

        @pl.when(y == goal)
        def _():
            final(1 - c, other, 0)

        for k in (1, 2, 3):

            @pl.when(wrap(goal + k) == y)
            def _():
                for core in (0, 1):
                    final(core, dev(x, z, core, goal), k)

    def end3(col):
        p, s = first[col], second[col]
        half = yp.at[col, p, s, pl.ds(0, 64)]
        expect(half, s3.at[col, 1 - c])

        @pl.when(y != 2 * c + col)
        def _():
            expect(half, s3.at[col, c])

        @pl.when(y == 2 * c + col)
        def _():
            acc = yp[col, p, s, pl.ds(pl.multiple_of(c * 64, 64), 64)].astype(F32)
            for k in (1, 2, 3):
                acc = acc + fin3[k].astype(F32)
            out_ref[...] = acc.astype(BF)

    scatter(1, 0, 4)
    open0(1)
    open1(1)
    scatter(0, 2, 1)
    open0(0)
    scatter(0, 3, 3)
    open1(0)
    for step in (mid1, end1, mid2, end2):
        for col in (1, 0):
            step(col)
    for k in (1, 2, 3):
        expect(fin3.at[k], r3.at[k])
    end3(0)
    end3(1)

    @pl.when(y // 2 != c)
    def _():
        expect(fin3.at[0], r3.at[0])
        acc = fin3[0].astype(F32)
        for k in (1, 2, 3):
            acc = acc + fin3[k].astype(F32)
        out_ref[...] = acc.astype(BF)

    for copy in waits:
        copy.wait_send()


def combine(inner, tables, w_down, wd_far):
    return pl.pallas_call(
        combine_kernel,
        out_shape=jax.ShapeDtypeStruct((ROWS, BLK), BF),
        in_specs=[pl.BlockSpec(memory_space=pltpu.VMEM)] * 2 + [pl.BlockSpec(memory_space=pltpu.HBM)] * 2,
        out_specs=pl.BlockSpec(memory_space=pltpu.VMEM),
        scratch_shapes=[
            pltpu.VMEM((EXL, GROUPS * GSLOT, FFL), BF),
            pltpu.VMEM((2, EXL, FFL, HALF), BF),
            pltpu.VMEM((2, GROUPS, 2 * EXL * GSLOT, BLK), F32),
            pltpu.VMEM((GROUP, 2 * EXL * GSLOT), F32),
            pltpu.VMEM((2, 4, 4, 128, BLK), BF),
            pltpu.VMEM((2, 2, 2, 128, BLK), BF),
            pltpu.VMEM((2, 2, 4, 128, BLK), BF),
            pltpu.VMEM((2, 2, 64, BLK), BF),
            pltpu.VMEM((2, 2, 128, BLK), BF),
            pltpu.VMEM((4, 64, BLK), BF),
            pltpu.SemaphoreType.DMA((2,)),
            pltpu.SemaphoreType.DMA((2,)),
            pltpu.SemaphoreType.DMA((2, 6)),
            pltpu.SemaphoreType.DMA((2, 6)),
            pltpu.SemaphoreType.DMA((2, 6)),
            pltpu.SemaphoreType.DMA((2, 6)),
            pltpu.SemaphoreType.DMA((2, 2)),
            pltpu.SemaphoreType.DMA((4,)),
        ],
        compiler_params=pltpu.CompilerParams(
            collective_id=1, has_side_effects=True, vmem_limit_bytes=38 * 1024 * 1024
        ),
        name="combine",
    )(inner, tables, w_down, wd_far)


def attend_page(query, page, length):
    scores = lax.dot_general(query, page, (((0,), (0,)), ((), ())), preferred_element_type=F32)
    scores = scores * SCORE_SCALE
    live = lax.broadcasted_iota(jnp.int32, scores.shape, 1) < length
    scores = jnp.where(live, scores, MASK_FLOOR)
    weight = jnp.exp(scores - jnp.max(scores, axis=1, keepdims=True))
    total = jnp.sum(weight, axis=1, keepdims=True)
    blended = lax.dot_general(
        weight.astype(BF), page[:LAT], (((1,), (1,)), ((), ())), preferred_element_type=F32
    )
    return (blended * (1.0 / total)).astype(BF)


def attend_kernel(dev_ref, lens_ref, q_ref, page_ref, out_ref):
    count = q_ref.shape[0]
    base = dev_ref[0] * 16 + pl.program_id(0) * count
    for k in range(count):
        out_ref[k] = attend_page(q_ref[k], page_ref[k], lens_ref[base + k])


def attend(dev, lens, queries, pages):
    count, width, heads = queries.shape
    ctx = pages.shape[2]
    step = 4
    return pl.pallas_call(
        attend_kernel,
        out_shape=jax.ShapeDtypeStruct((count, heads, LAT), BF),
        grid_spec=pltpu.PrefetchScalarGridSpec(
            num_scalar_prefetch=2,
            grid=(count // step,),
            in_specs=[
                pl.BlockSpec((step, width, heads), lambda r, *_: (r, 0, 0)),
                pl.BlockSpec((step, width, ctx), lambda r, *_: (r, 0, 0)),
            ],
            out_specs=pl.BlockSpec((step, heads, LAT), lambda r, *_: (r, 0, 0)),
        ),
        cost_estimate=pl.CostEstimate(flops=2_400_000_000, bytes_accessed=20_000_000, transcendentals=0),
        name="attend",
    )(dev, lens, queries, pages)


def attend_one_kernel(dev_ref, slot_ref, mask_ref, lens_ref, q_ref, page_ref, all_ref, out_ref):
    partner = jnp.bitwise_xor(dev_ref[0], mask_ref[0] * 4)
    length = lens_ref[partner * 16 + slot_ref[partner]]
    out_ref[0] = attend_page(q_ref[0], page_ref[...], length)


def attend_one(dev, slots, mask, lens, queries, page, attended):
    count, width, heads = queries.shape
    return pl.pallas_call(
        attend_one_kernel,
        out_shape=jax.ShapeDtypeStruct(attended.shape, BF),
        grid_spec=pltpu.PrefetchScalarGridSpec(
            num_scalar_prefetch=4,
            grid=(1,),
            in_specs=[
                pl.BlockSpec((1, width, heads), lambda r, dev, slot, *_: (slot[dev[0]], 0, 0)),
                pl.BlockSpec(page.shape, lambda r, *_: (0, 0)),
                pl.BlockSpec(memory_space=pl.ANY),
            ],
            out_specs=pl.BlockSpec((1, heads, LAT), lambda r, dev, slot, *_: (slot[dev[0]], 0, 0)),
        ),
        input_output_aliases={6: 0},
        name="attend_one",
    )(dev, slots, mask, lens, queries, page, attended)


def trade(page, bits, shift, steps, beside):
    count = lax.axis_size("ep")

    def branch(m):
        def run(block):
            if m:
                block = lax.ppermute(block, "ep", [(i, i ^ (m << shift)) for i in range(count)])
            return block, beside()

        return run

    return lax.switch(bits, [branch(m) for m in range(steps)], page)


def prepare_kernel(dev_ref, slot_ref, x_ref, ids_ref, gates_ref, page_ref, out_ref, parts_ref, own_ref):
    own_ref[...] = page_ref[0]
    top = ids_ref.shape[0]
    expert = lax.broadcasted_iota(jnp.int32, (128, ROWS), 0)
    chosen = jnp.zeros((128, ROWS), F32)
    gates = jnp.zeros((128, ROWS), F32)
    for k in range(top):
        hit = expert == ids_ref[k : k + 1, :]
        chosen = jnp.where(hit, 1.0, chosen)
        gates = jnp.where(hit, gates_ref[k : k + 1, :], gates)
    row = lax.broadcasted_iota(jnp.int32, (ROWS, ROWS), 0)
    col = lax.broadcasted_iota(jnp.int32, (ROWS, ROWS), 1)
    upto = jnp.where(row >= col, 1.0, 0.0).astype(BF)
    same = jnp.where(row == col, 1.0, 0.0).astype(BF)
    flip = functools.partial(
        lax.dot_general, dimension_numbers=(((1,), (1,)), ((), ())), preferred_element_type=F32
    )
    chosen = chosen.astype(BF)
    place = jnp.where(flip(same, chosen) > 0.5, flip(upto, chosen), 0.0)
    out_ref[:, :MAIN] = x_ref[:, :MAIN]
    out_ref[:, MAIN : MAIN + 128] = place.astype(BF)
    out_ref[:, MAIN + 128 :] = flip(same, gates.astype(BF)).astype(BF)
    for k in range(4):
        parts_ref[k] = x_ref[:, MAIN + k * QUARTER : MAIN + (k + 1) * QUARTER]


def prepare(dev, slots, hidden, ids, gates, pages):
    count, width, ctx = pages.shape

    def whole(array):
        return pl.BlockSpec(array.shape, lambda r, *_: (0, 0))

    return pl.pallas_call(
        prepare_kernel,
        out_shape=(
            jax.ShapeDtypeStruct((ROWS, WHOLE), BF),
            jax.ShapeDtypeStruct((4, ROWS, QUARTER), BF),
            jax.ShapeDtypeStruct((width, ctx), BF),
        ),
        grid_spec=pltpu.PrefetchScalarGridSpec(
            num_scalar_prefetch=2,
            grid=(1,),
            in_specs=[
                whole(hidden),
                whole(ids),
                whole(gates),
                pl.BlockSpec((1, width, ctx), lambda r, dev, slot: (slot[dev[0]], 0, 0)),
            ],
            out_specs=(
                pl.BlockSpec((ROWS, WHOLE), lambda r, *_: (0, 0)),
                pl.BlockSpec((4, ROWS, QUARTER), lambda r, *_: (0, 0, 0)),
                pl.BlockSpec((width, ctx), lambda r, *_: (0, 0)),
            ),
        ),
        name="prepare",
    )(dev, slots, hidden, ids, gates, pages)


def local(
    cache_pages,
    queries,
    lengths,
    swap_slot,
    swap_mask,
    hidden,
    expert_ids,
    gate_weights,
    w_gate,
    w_up,
    w_down,
):
    ep_rank = lax.axis_index("ep").astype(jnp.int32)
    groups = lax.axis_size("tp")
    tp_rank = lax.axis_index("tp").astype(jnp.int32)
    device = ep_rank * groups + tp_rank
    mask = swap_mask[0]
    dev = device.reshape(1)
    pages = jnp.swapaxes(cache_pages, 1, 2)
    asked = jnp.swapaxes(queries, 1, 2)
    w_down = pltpu.with_memory_space_constraint(w_down, pltpu.HBM)
    xmain, xparts, own_page = prepare(dev, swap_slot, hidden, expert_ids.T, gate_weights.T, pages)
    page, attended = trade(
        own_page, jnp.right_shift(mask, 3), 3, 4, lambda: attend(dev, lengths, asked, pages)
    )
    xg, xq, wd_far = gather_rows(xmain, xparts, w_down)
    xg = xg.reshape(GROUPS // 2, PAIR, WHOLE)
    xq = xq.reshape(4, GROUPS // 2, PAIR, QUARTER)
    base = (ep_rank * EXL).reshape(1)
    page, (inner, tables) = trade(
        page, jnp.bitwise_and(mask, 7), 0, 8, lambda: experts_up(base, xg, xq, w_gate, w_up)
    )
    moe_rows = combine(inner, tables.reshape(GROUPS, GROUP, META), w_down, wd_far)
    attended = attend_one(dev, swap_slot, swap_mask, lengths, asked, page, attended)
    return attended, moe_rows


def solution(mesh):
    in_specs = (
        P(("ep", "tp"), None, None),
        P(("ep", "tp"), None, None),
        P(),
        P(),
        P(),
        P("ep", None),
        P("ep", None),
        P("ep", None),
        P("ep", None, "tp"),
        P("ep", None, "tp"),
        P("ep", "tp", None),
    )
    out_specs = (P(("ep", "tp"), None, None), P("ep", "tp"))
    return jax.shard_map(local, mesh=mesh, in_specs=in_specs, out_specs=out_specs, check_vma=False)
```

```python
import functools

import jax
import jax.numpy as jnp
from jax import lax
from jax.experimental import pallas as pl
from jax.experimental.pallas import tpu as pltpu
from jax.sharding import PartitionSpec as P

MESH = pl.DeviceIdType.MESH
BF = jnp.bfloat16
F32 = jnp.float32
LAT = 512
D = 3584
ROWS = 64
CAP = 10
EXL = 3
META = 256
GROUP = 256
GROUPS = 8
GSLOT = 40
PAIR = 2 * GROUP
PSLOT = 2 * GSLOT
HALF = D // 2
BLK = D // 4
FFL = 256
SCORE_SCALE = 192.0 ** (-0.5)
MASK_FLOOR = -1e30
VMEM_MAX = 60 * 1024 * 1024


def coords():
    e = lax.axis_index("ep")
    return e // 8, lax.rem(e // 2, 4), lax.rem(e, 2), lax.axis_index("tp")


def wrap(v):
    return lax.rem(v + 4, 4)


def greet(targets):
    barrier = pltpu.get_barrier_semaphore()
    for target in targets:
        pl.semaphore_signal(barrier, inc=1, device_id=target, device_id_type=MESH)
    pl.semaphore_wait(barrier, len(targets))


QUARTER = 256
MAIN = D - 4 * QUARTER
WHOLE = MAIN + META


def gather_kernel(
    x_ref, xp_ref, wd_ref, xg_ref, xq_ref, wdp_ref,
    ssem, rsem1, rsem2, dsend, drecv, ysend, yrecv, ydsend, ydrecv, wsem, lsem,
):
    x, z, c, y = coords()

    def dev(xx, zz, cc):
        return (xx * 8 + zz * 2 + cc, y)

    other = dev(x, z, 1 - c)
    above, below = (x * 8 + z * 2 + c, wrap(y + 1)), (x * 8 + z * 2 + c, wrap(y - 1))
    started = []
    count = {}

    def push(src, dst, target, send, recv):
        copy = pltpu.make_async_remote_copy(
            src_ref=src, dst_ref=dst, send_sem=send, recv_sem=recv, device_id=target, device_id_type=MESH
        )
        copy.start()
        started.append(copy)

    def ship(part, col, src, dst, target, recv):
        k = count.get((part, col), 0)
        count[part, col] = k + 1
        push(src, dst, target, ssem.at[part, col, k], recv)

    first = (x, z)
    second = (z, x)

    def place(part, col, f, s, lo=0, size=32):
        xx, zz = (f, s) if col == 0 else (s, f)
        rows = pl.ds(col * 32 + lo, size)
        return xg_ref.at[xx, zz, c, rows] if part else xq_ref.at[y, xx, zz, c, rows]

    def line(col, s, yy, lo=0, size=4, core=c):
        rows = pl.ds(col * 32, 32)
        if col == 0:
            return xq_ref.at[yy, pl.ds(lo, size), s, core, rows]
        return xq_ref.at[yy, s, pl.ds(lo, size), core, rows]

    def fdev(col, f):
        return dev(f, z, c) if col == 0 else dev(x, f, c)

    def sdev(col, s):
        return dev(x, s, c) if col == 0 else dev(s, z, c)

    def own(part, col):
        rows = pl.ds(col * 32, 32)
        return x_ref.at[rows] if part else xp_ref.at[y, rows]

    def expect(ref, sem):
        pltpu.make_async_copy(ref, ref, sem).wait()

    def share(part, col, f, s, src=None):
        if part == 0:
            return
        xx, zz = (f, s) if col == 0 else (s, f)
        slot = xx * 4 + zz
        ref = place(part, col, f, s)
        push(ref if src is None else src, ref, other, dsend.at[col, slot], drecv.at[col, slot])

    def fan(part, col, k, f, src=None):
        s = second[col]
        ref = place(part, col, f, s)
        src = ref if src is None else src
        ship(part, col, src, ref, sdev(col, wrap(s + 1)), rsem2.at[part, col, k, 0])
        ship(part, col, src, ref, sdev(col, wrap(s - 1)), rsem2.at[part, col, k, 1])

    def relay2(part, col, k, f):
        s = second[col]
        expect(place(part, col, f, wrap(s - 1)), rsem2.at[part, col, k, 0])
        ref = place(part, col, f, wrap(s - 1), 0, 16)
        ship(part, col, ref, ref, sdev(col, wrap(s + 1)), rsem2.at[part, col, k, 2])
        share(part, col, f, wrap(s - 1))
        expect(place(part, col, f, wrap(s + 1)), rsem2.at[part, col, k, 1])
        ref = place(part, col, f, wrap(s + 1), 16, 16)
        ship(part, col, ref, ref, sdev(col, wrap(s - 1)), rsem2.at[part, col, k, 3])
        share(part, col, f, wrap(s + 1))

    def last2(part, col, k, f):
        s = wrap(second[col] + 2)
        expect(place(part, col, f, s, 0, 16), rsem2.at[part, col, k, 2])
        expect(place(part, col, f, s, 16, 16), rsem2.at[part, col, k, 3])
        share(part, col, f, s)

    def open1(part):
        for col in (0, 1):
            p, s = first[col], second[col]
            ref = place(part, col, p, s)
            ship(part, col, own(part, col), ref, fdev(col, wrap(p + 1)), rsem1.at[part, col, 0])
            ship(part, col, own(part, col), ref, fdev(col, wrap(p - 1)), rsem1.at[part, col, 1])

    def relay1(part):
        for col in (0, 1):
            p, s = first[col], second[col]
            expect(place(part, col, wrap(p - 1), s), rsem1.at[part, col, 0])
            ref = place(part, col, wrap(p - 1), s, 0, 16)
            ship(part, col, ref, ref, fdev(col, wrap(p + 1)), rsem1.at[part, col, 2])
            expect(place(part, col, wrap(p + 1), s), rsem1.at[part, col, 1])
            ref = place(part, col, wrap(p + 1), s, 16, 16)
            ship(part, col, ref, ref, fdev(col, wrap(p - 1)), rsem1.at[part, col, 3])
            if part:
                for k, f in ((1, wrap(p - 1)), (2, wrap(p + 1))):
                    fan(1, col, k, f)
                    share(1, col, f, s)

    def last1(part, col):
        p, s = first[col], second[col]
        expect(place(part, col, wrap(p + 2), s, 0, 16), rsem1.at[part, col, 2])
        expect(place(part, col, wrap(p + 2), s, 16, 16), rsem1.at[part, col, 3])

    def source(col, k):
        return wrap(first[col] + (0, -1, 1, 2)[k])

    def lines_out(col):
        s = second[col]
        ref = line(col, s, y)
        ship(0, col, ref, ref, sdev(col, wrap(s + 1)), rsem2.at[0, col, 0, 0])
        ship(0, col, ref, ref, sdev(col, wrap(s - 1)), rsem2.at[0, col, 0, 1])

    def lines_on(col):
        s = second[col]
        expect(line(col, wrap(s - 1), y), rsem2.at[0, col, 0, 0])
        ref = line(col, wrap(s - 1), y, 0, 2)
        ship(0, col, ref, ref, sdev(col, wrap(s + 1)), rsem2.at[0, col, 0, 2])
        expect(line(col, wrap(s + 1), y), rsem2.at[0, col, 0, 1])
        ref = line(col, wrap(s + 1), y, 2, 2)
        ship(0, col, ref, ref, sdev(col, wrap(s - 1)), rsem2.at[0, col, 0, 3])

    def lines_in(col):
        s = wrap(second[col] + 2)
        expect(line(col, s, y, 0, 2), rsem2.at[0, col, 0, 2])
        expect(line(col, s, y, 2, 2), rsem2.at[0, col, 0, 3])

    def part_of(yy, lo, size=2, core=c):
        return xq_ref.at[yy, pl.ds(lo, size), :, core]

    def hand(d):
        ref = part_of(wrap(y + d), 0, 4)
        push(ref, ref, other, ydsend.at[d], ydrecv.at[d])

    locals_ = [
        pltpu.make_async_copy(xp_ref.at[y], xq_ref.at[y, x, z, c], lsem.at[0]),
        pltpu.make_async_copy(x_ref, xg_ref.at[x, z, c], lsem.at[1]),
    ]
    for copy in locals_:
        copy.start()
    greet(
        [dev(wrap(x + 1), z, c), dev(wrap(x - 1), z, c), dev(x, wrap(z + 1), c), dev(x, wrap(z - 1), c)]
        + [other, above, below]
    )
    open1(0)
    far = pl.ds(pl.multiple_of((1 - c) * HALF, HALF), HALF)
    push(wd_ref.at[:, :, far], wdp_ref, other, wsem.at[0], wsem.at[1])
    relay1(0)
    open1(1)
    locals_[0].wait()
    for col in (0, 1):
        last1(0, col)
        lines_out(col)
    for col in (0, 1):
        lines_on(col)
    for col in (0, 1):
        fan(1, col, 0, first[col], own(1, col))
        share(1, col, first[col], second[col], own(1, col))
    relay1(1)
    for col in (0, 1):
        lines_in(col)
    for k, lo, target in ((0, 0, above), (2, 2, below), (1, 2, above), (3, 0, below)):
        ref = part_of(y, lo)
        push(ref, ref, target, ysend.at[k], yrecv.at[k])
    hand(0)
    for col in (0, 1):
        relay2(1, col, 0, source(col, 0))
    for col in (0, 1):
        last1(1, col)
        fan(1, col, 3, source(col, 3))
        share(1, col, source(col, 3), second[col])
    ref = part_of(wrap(y - 1), 0)
    expect(ref, yrecv.at[0])
    push(ref, ref, above, ysend.at[4], yrecv.at[4])
    ref = part_of(wrap(y + 1), 2)
    expect(ref, yrecv.at[2])
    push(ref, ref, below, ysend.at[5], yrecv.at[5])
    for k in (1, 2):
        for col in (0, 1):
            relay2(1, col, k, source(col, k))
    for col in (0, 1):
        last2(1, col, 0, source(col, 0))
    expect(part_of(wrap(y - 1), 2), yrecv.at[1])
    hand(3)
    expect(part_of(wrap(y + 1), 0), yrecv.at[3])
    hand(1)
    for col in (0, 1):
        relay2(1, col, 3, source(col, 3))
    expect(part_of(wrap(y + 2), 0), yrecv.at[4])
    expect(part_of(wrap(y + 2), 2), yrecv.at[5])
    hand(2)
    for k in (1, 2, 3):
        for col in (0, 1):
            last2(1, col, k, source(col, k))
    for col in (0, 1):
        for slot in range(16):
            expect(xg_ref.at[slot // 4, slot % 4, 1 - c, pl.ds(col * 32, 32)], drecv.at[col, slot])
    for d in range(4):
        expect(part_of(wrap(y + d), 0, 4, 1 - c), ydrecv.at[d])
    expect(wdp_ref, wsem.at[1])
    for copy in locals_[1:]:
        copy.wait()
    for copy in started:
        copy.wait_send()


def gather_rows(xmain, xparts, w_down):
    dma = pltpu.SemaphoreType.DMA
    return pl.pallas_call(
        gather_kernel,
        out_shape=(
            jax.ShapeDtypeStruct((4, 4, 2, ROWS, WHOLE), BF),
            jax.ShapeDtypeStruct((4, 4, 4, 2, ROWS, QUARTER), BF),
            pltpu.HBM((EXL, FFL, HALF), BF),
        ),
        in_specs=[pl.BlockSpec(memory_space=pltpu.VMEM)] * 2 + [pl.BlockSpec(memory_space=pltpu.HBM)],
        out_specs=(pl.BlockSpec(memory_space=pltpu.VMEM),) * 2
        + (pl.BlockSpec(memory_space=pltpu.HBM),),
        scratch_shapes=[
            dma((2, 2, 20)),
            dma((2, 2, 4)),
            dma((2, 2, 4, 4)),
            dma((2, 16)),
            dma((2, 16)),
            dma((6,)),
            dma((6,)),
            dma((4,)),
            dma((4,)),
            dma((2,)),
            dma((2,)),
        ],
        compiler_params=pltpu.CompilerParams(
            collective_id=0, has_side_effects=True, vmem_limit_bytes=18 * 1024 * 1024
        ),
        name="gather_rows",
    )(xmain, xparts, w_down)


def slot_numbers(shape, axis, gslot):
    s = lax.broadcasted_iota(jnp.int32, shape, axis)
    g = lax.broadcasted_iota(jnp.int32, shape, 1 - axis)
    expert = jnp.zeros(shape, jnp.int32)
    for k in range(1, shape[axis] // gslot):
        expert = expert + (s >= k * gslot).astype(jnp.int32)
    u = s - expert * gslot
    rank = (u * 205) >> 11
    want = jnp.where((g >> 6) == rank, u - rank * CAP + 1, -1)
    return want.astype(F32)


def expert_lanes(shape, axis, base, gslot):
    s = lax.broadcasted_iota(jnp.int32, shape, axis)
    e = lax.broadcasted_iota(jnp.int32, shape, 1 - axis)
    expert = jnp.zeros(shape, jnp.int32)
    for k in range(1, shape[axis] // gslot):
        expert = expert + (s >= k * gslot).astype(jnp.int32)
    return jnp.where(expert + base == e, 1.0, 0.0).astype(BF)


def up_kernel(base_ref, x_ref, xp_ref, wg_ref, wu_hbm, out_ref, tab_ref, xc, wu_ref, sem):
    load = pltpu.make_async_copy(wu_hbm, wu_ref, sem)
    load.start()
    tab_ref[...] = x_ref[:, :, MAIN:WHOLE]
    want = slot_numbers((EXL * PSLOT, PAIR), 0, PSLOT)
    lanes = expert_lanes((EXL * PSLOT, 128), 0, base_ref[0], PSLOT)

    @pl.loop(0, GROUPS // 2)
    def _(q):
        table = x_ref[q, :, MAIN : MAIN + 128]
        named = lax.dot_general(lanes, table, (((1,), (1,)), ((), ())), preferred_element_type=F32)
        pick = jnp.where(named == want, 1.0, 0.0).astype(BF)
        start = pl.multiple_of(q * PSLOT, 16)

        def keep(rows, cols):
            for e in range(EXL):
                xc[e, pl.ds(start, PSLOT), cols] = rows[e * PSLOT : (e + 1) * PSLOT].astype(BF)

        for n in range(MAIN // 512):
            cols = slice(n * 512, (n + 1) * 512)
            keep(jnp.dot(pick, x_ref[q, :, cols], preferred_element_type=F32), cols)
        for n in range(4):
            cols = slice(MAIN + n * QUARTER, MAIN + (n + 1) * QUARTER)
            keep(jnp.dot(pick, xp_ref[n, q], preferred_element_type=F32), cols)

    load.wait()

    @pl.loop(0, EXL)
    def _(e):
        rows = xc[e]
        gate = jnp.dot(rows, wg_ref[e], preferred_element_type=F32)
        up = jnp.dot(rows, wu_ref[e], preferred_element_type=F32)
        out_ref[e] = (gate / (1.0 + jnp.exp(-gate)) * up).astype(BF)


def experts_up(base, xg, xq, w_gate, w_up):
    return pl.pallas_call(
        up_kernel,
        out_shape=(
            jax.ShapeDtypeStruct((EXL, GROUPS * GSLOT, FFL), BF),
            jax.ShapeDtypeStruct((GROUPS // 2, PAIR, META), BF),
        ),
        in_specs=[pl.BlockSpec(memory_space=pltpu.SMEM)]
        + [pl.BlockSpec(memory_space=pltpu.VMEM)] * 3
        + [pl.BlockSpec(memory_space=pltpu.HBM)],
        out_specs=(pl.BlockSpec(memory_space=pltpu.VMEM),) * 2,
        scratch_shapes=[
            pltpu.VMEM((EXL, GROUPS * GSLOT, D), BF),
            pltpu.VMEM((EXL, D, FFL), BF),
            pltpu.SemaphoreType.DMA,
        ],
        cost_estimate=pl.CostEstimate(flops=7_000_000_000, bytes_accessed=30_000_000, transcendentals=0),
        compiler_params=pltpu.CompilerParams(vmem_limit_bytes=20 * 1024 * 1024),
        name="experts_up",
    )(base, xg, xq, w_gate, w_up)


def combine_kernel(
    inner_ref, meta, wd_hbm, wdp_hbm, out_ref,
    inner2, wdh, outc, want, yp, st1, fin1, st2, fin2, fin3,
    lsem, isem, s1, r1, s2, r2, s3, r3,
):
    x, z, c, y = coords()

    def dev(xx, zz, cc, yy):
        return (xx * 8 + zz * 2 + cc, yy)

    other = dev(x, z, 1 - c, y)
    waits = []

    def ship(src, dst, target, send, recv):
        copy = pltpu.make_async_remote_copy(
            src_ref=src, dst_ref=dst, send_sem=send, recv_sem=recv, device_id=target, device_id_type=MESH
        )
        copy.start()
        waits.append(copy)
        return copy

    def expect(ref, sem):
        pltpu.make_async_copy(ref, ref, sem).wait()

    near = pl.ds(pl.multiple_of(c * HALF, HALF), HALF)
    loads = [
        pltpu.make_async_copy(wd_hbm.at[:, :, near], wdh.at[c], lsem.at[0]),
        pltpu.make_async_copy(wdp_hbm, wdh.at[1 - c], lsem.at[1]),
    ]
    for load in loads:
        load.start()
    want[...] = slot_numbers((GROUP, 2 * EXL * GSLOT), 1, GSLOT)
    lanes = expert_lanes((128, 2 * EXL * GSLOT), 1, (x * 4 + z) * 2 * EXL, GSLOT)
    greet(
        [dev(wrap(x + 1), z, c, y), dev(wrap(x - 1), z, c, y), dev(x, wrap(z + 1), c, y), dev(x, wrap(z - 1), c, y)]
        + [other]
        + [dev(x, z, core, wrap(y + k)) for k in (1, 2, 3) for core in (0, 1)]
    )
    swap = ship(inner_ref, inner2, other, isem.at[0], isem.at[1])

    def down(core, source):
        @pl.loop(0, EXL)
        def _(e):
            row = pl.multiple_of((core * EXL + e) * GSLOT, 8)
            for n in range(2):
                cols = slice(n * BLK, (n + 1) * BLK)
                part = jnp.dot(source[e], wdh[core, e, :, cols], preferred_element_type=F32)
                for q in range(GROUPS):
                    outc[n, q, pl.ds(row, GSLOT), :] = part[q * GSLOT : (q + 1) * GSLOT]

    loads[0].wait()
    down(c, inner_ref)
    loads[1].wait()
    swap.wait_recv()
    down(1 - c, inner2)

    def scatter(col, start, count):
        @pl.loop(0, 2 * count, unroll=2)
        def _(i):
            q = wrap(x + start + i // 2) * 2 + lax.rem(i, 2)
            named = jnp.dot(meta[q, :, 0:128], lanes, preferred_element_type=F32)
            gate = jnp.dot(meta[q, :, 128:256], lanes, preferred_element_type=F32)
            mix = jnp.where(named == want[...], gate, 0.0).astype(BF)
            part = jnp.dot(mix, outc[col, q].astype(BF), preferred_element_type=F32).astype(BF)
            xx = q // 2
            for k in range(2):
                piece = part[k * 128 : (k + 1) * 128]
                zz = lax.rem(q, 2) * 2 + k
                if col == 0:
                    yp[0, xx, zz] = piece
                else:
                    yp[1, zz, xx] = piece

    first, second = (x, z), (z, x)

    def fdev(col, f):
        return dev(f, z, c, y) if col == 0 else dev(x, f, c, y)

    def sdev(col, s):
        return dev(x, s, c, y) if col == 0 else dev(s, z, c, y)

    def open0(col):
        p = first[col]
        up, dn = fdev(col, wrap(p + 1)), fdev(col, wrap(p - 1))
        ship(yp.at[col, wrap(p + 2), pl.ds(0, 2)], st1.at[col, 0], up, s1.at[col, 0], r1.at[col, 0])
        ship(yp.at[col, wrap(p + 2), pl.ds(2, 2)], st1.at[col, 1], dn, s1.at[col, 1], r1.at[col, 1])

    def open1(col):
        p = first[col]
        up, dn = fdev(col, wrap(p + 1)), fdev(col, wrap(p - 1))
        ship(yp.at[col, wrap(p + 1), pl.ds(2, 2)], fin1.at[col, 0, pl.ds(2, 2)], up, s1.at[col, 2], r1.at[col, 2])
        ship(yp.at[col, wrap(p - 1), pl.ds(0, 2)], fin1.at[col, 1, pl.ds(0, 2)], dn, s1.at[col, 3], r1.at[col, 3])

    def mid1(col):
        p = first[col]
        up, dn = fdev(col, wrap(p + 1)), fdev(col, wrap(p - 1))
        for side, (f, lo, target) in enumerate(((wrap(p + 1), 0, up), (wrap(p - 1), 2, dn))):
            expect(st1.at[col, side], r1.at[col, side])
            for k in range(2):
                acc = yp[col, f, lo + k].astype(F32) + st1[col, side, k].astype(F32)
                yp[col, f, lo + k] = acc.astype(BF)
            ship(
                yp.at[col, f, pl.ds(lo, 2)],
                fin1.at[col, side, pl.ds(lo, 2)],
                target,
                s1.at[col, 4 + side],
                r1.at[col, 4 + side],
            )

    def end1(col):
        p, s = first[col], second[col]
        for side, lo in ((0, 2), (1, 0), (0, 0), (1, 2)):
            expect(
                fin1.at[col, side, pl.ds(lo, 2)],
                r1.at[col, {(0, 2): 2, (1, 0): 3, (0, 0): 4, (1, 2): 5}[(side, lo)]],
            )
        up, dn = sdev(col, wrap(s + 1)), sdev(col, wrap(s - 1))

        def fold(t):
            acc = yp[col, p, t].astype(F32) + fin1[col, 0, t].astype(F32) + fin1[col, 1, t].astype(F32)
            yp[col, p, t] = acc.astype(BF)

        lo, hi = pl.ds(0, 64), pl.ds(64, 64)
        t = wrap(s + 2)
        fold(t)
        ship(yp.at[col, p, t, lo], st2.at[col, 0], up, s2.at[col, 0], r2.at[col, 0])
        ship(yp.at[col, p, t, hi], st2.at[col, 1], dn, s2.at[col, 1], r2.at[col, 1])
        t = wrap(s + 1)
        fold(t)
        ship(yp.at[col, p, t, hi], fin2.at[col, 0, hi], up, s2.at[col, 2], r2.at[col, 2])
        t = wrap(s - 1)
        fold(t)
        ship(yp.at[col, p, t, lo], fin2.at[col, 1, lo], dn, s2.at[col, 3], r2.at[col, 3])
        fold(s)

    def mid2(col):
        p, s = first[col], second[col]
        up, dn = sdev(col, wrap(s + 1)), sdev(col, wrap(s - 1))
        for side, (t, lo, target) in enumerate(((wrap(s + 1), 0, up), (wrap(s - 1), 64, dn))):
            expect(st2.at[col, side], r2.at[col, side])
            acc = yp[col, p, t, lo : lo + 64].astype(F32) + st2[col, side].astype(F32)
            yp[col, p, t, lo : lo + 64] = acc.astype(BF)
            rows = pl.ds(lo, 64)
            ship(
                yp.at[col, p, t, rows], fin2.at[col, side, rows], target, s2.at[col, 4 + side], r2.at[col, 4 + side]
            )

    def end2(col):
        p, s = first[col], second[col]
        for side, lo, k in ((0, 64, 2), (1, 0, 3), (0, 0, 4), (1, 64, 5)):
            expect(fin2.at[col, side, pl.ds(lo, 64)], r2.at[col, k])
        acc = yp[col, p, s].astype(F32) + fin2[col, 0].astype(F32) + fin2[col, 1].astype(F32)
        yp[col, p, s] = acc.astype(BF)
        goal = 2 * c + col

        def final(core, target, k):
            pltpu.make_async_remote_copy(
                src_ref=yp.at[col, p, s, pl.ds(pl.multiple_of(core * 64, 64), 64)],
                dst_ref=fin3.at[k],
                send_sem=s3.at[col, core],
                recv_sem=r3.at[k],
                device_id=target,
                device_id_type=MESH,
            ).start()

        @pl.when(y == goal)
        def _():
            final(1 - c, other, 0)

        for k in (1, 2, 3):

            @pl.when(wrap(goal + k) == y)
            def _():
                for core in (0, 1):
                    final(core, dev(x, z, core, goal), k)

    def end3(col):
        p, s = first[col], second[col]
        half = yp.at[col, p, s, pl.ds(0, 64)]
        expect(half, s3.at[col, 1 - c])

        @pl.when(y != 2 * c + col)
        def _():
            expect(half, s3.at[col, c])

        @pl.when(y == 2 * c + col)
        def _():
            acc = yp[col, p, s, pl.ds(pl.multiple_of(c * 64, 64), 64)].astype(F32)
            for k in (1, 2, 3):
                acc = acc + fin3[k].astype(F32)
            out_ref[...] = acc.astype(BF)

    scatter(1, 0, 4)
    open0(1)
    open1(1)
    scatter(0, 2, 1)
    open0(0)
    scatter(0, 3, 3)
    open1(0)
    for step in (mid1, end1, mid2, end2):
        for col in (1, 0):
            step(col)
    for k in (1, 2, 3):
        expect(fin3.at[k], r3.at[k])
    end3(0)
    end3(1)

    @pl.when(y // 2 != c)
    def _():
        expect(fin3.at[0], r3.at[0])
        acc = fin3[0].astype(F32)
        for k in (1, 2, 3):
            acc = acc + fin3[k].astype(F32)
        out_ref[...] = acc.astype(BF)

    for copy in waits:
        copy.wait_send()


def combine(inner, tables, w_down, wd_far):
    return pl.pallas_call(
        combine_kernel,
        out_shape=jax.ShapeDtypeStruct((ROWS, BLK), BF),
        in_specs=[pl.BlockSpec(memory_space=pltpu.VMEM)] * 2 + [pl.BlockSpec(memory_space=pltpu.HBM)] * 2,
        out_specs=pl.BlockSpec(memory_space=pltpu.VMEM),
        scratch_shapes=[
            pltpu.VMEM((EXL, GROUPS * GSLOT, FFL), BF),
            pltpu.VMEM((2, EXL, FFL, HALF), BF),
            pltpu.VMEM((2, GROUPS, 2 * EXL * GSLOT, BLK), F32),
            pltpu.VMEM((GROUP, 2 * EXL * GSLOT), F32),
            pltpu.VMEM((2, 4, 4, 128, BLK), BF),
            pltpu.VMEM((2, 2, 2, 128, BLK), BF),
            pltpu.VMEM((2, 2, 4, 128, BLK), BF),
            pltpu.VMEM((2, 2, 64, BLK), BF),
            pltpu.VMEM((2, 2, 128, BLK), BF),
            pltpu.VMEM((4, 64, BLK), BF),
            pltpu.SemaphoreType.DMA((2,)),
            pltpu.SemaphoreType.DMA((2,)),
            pltpu.SemaphoreType.DMA((2, 6)),
            pltpu.SemaphoreType.DMA((2, 6)),
            pltpu.SemaphoreType.DMA((2, 6)),
            pltpu.SemaphoreType.DMA((2, 6)),
            pltpu.SemaphoreType.DMA((2, 2)),
            pltpu.SemaphoreType.DMA((4,)),
        ],
        compiler_params=pltpu.CompilerParams(
            collective_id=1, has_side_effects=True, vmem_limit_bytes=38 * 1024 * 1024
        ),
        name="combine",
    )(inner, tables, w_down, wd_far)


def attend_page(query, page, length):
    scores = lax.dot_general(query, page, (((0,), (0,)), ((), ())), preferred_element_type=F32)
    scores = scores * SCORE_SCALE
    live = lax.broadcasted_iota(jnp.int32, scores.shape, 1) < length
    scores = jnp.where(live, scores, MASK_FLOOR)
    weight = jnp.exp(scores - jnp.max(scores, axis=1, keepdims=True))
    total = jnp.sum(weight, axis=1, keepdims=True)
    blended = lax.dot_general(
        weight.astype(BF), page[:LAT], (((1,), (1,)), ((), ())), preferred_element_type=F32
    )
    return (blended * (1.0 / total)).astype(BF)


def attend_kernel(dev_ref, lens_ref, q_ref, page_ref, out_ref):
    count = q_ref.shape[0]
    base = dev_ref[0] * 16 + pl.program_id(0) * count
    for k in range(count):
        out_ref[k] = attend_page(q_ref[k], page_ref[k], lens_ref[base + k])


def attend(dev, lens, queries, pages):
    count, width, heads = queries.shape
    ctx = pages.shape[2]
    step = 4
    return pl.pallas_call(
        attend_kernel,
        out_shape=jax.ShapeDtypeStruct((count, heads, LAT), BF),
        grid_spec=pltpu.PrefetchScalarGridSpec(
            num_scalar_prefetch=2,
            grid=(count // step,),
            in_specs=[
                pl.BlockSpec((step, width, heads), lambda r, *_: (r, 0, 0)),
                pl.BlockSpec((step, width, ctx), lambda r, *_: (r, 0, 0)),
            ],
            out_specs=pl.BlockSpec((step, heads, LAT), lambda r, *_: (r, 0, 0)),
        ),
        cost_estimate=pl.CostEstimate(flops=2_400_000_000, bytes_accessed=20_000_000, transcendentals=0),
        name="attend",
    )(dev, lens, queries, pages)


def attend_one_kernel(dev_ref, slot_ref, mask_ref, lens_ref, q_ref, page_ref, all_ref, out_ref):
    partner = jnp.bitwise_xor(dev_ref[0], mask_ref[0] * 4)
    length = lens_ref[partner * 16 + slot_ref[partner]]
    out_ref[0] = attend_page(q_ref[0], page_ref[...], length)


def attend_one(dev, slots, mask, lens, queries, page, attended):
    count, width, heads = queries.shape
    return pl.pallas_call(
        attend_one_kernel,
        out_shape=jax.ShapeDtypeStruct(attended.shape, BF),
        grid_spec=pltpu.PrefetchScalarGridSpec(
            num_scalar_prefetch=4,
            grid=(1,),
            in_specs=[
                pl.BlockSpec((1, width, heads), lambda r, dev, slot, *_: (slot[dev[0]], 0, 0)),
                pl.BlockSpec(page.shape, lambda r, *_: (0, 0)),
                pl.BlockSpec(memory_space=pl.ANY),
            ],
            out_specs=pl.BlockSpec((1, heads, LAT), lambda r, dev, slot, *_: (slot[dev[0]], 0, 0)),
        ),
        input_output_aliases={6: 0},
        name="attend_one",
    )(dev, slots, mask, lens, queries, page, attended)


def trade(page, bits, shift, steps, beside):
    count = lax.axis_size("ep")

    def branch(m):
        def run(block):
            if m:
                block = lax.ppermute(block, "ep", [(i, i ^ (m << shift)) for i in range(count)])
            return block, beside()

        return run

    return lax.switch(bits, [branch(m) for m in range(steps)], page)


def prepare_kernel(dev_ref, slot_ref, x_ref, ids_ref, gates_ref, page_ref, out_ref, parts_ref, own_ref):
    own_ref[...] = page_ref[0]
    top = ids_ref.shape[0]
    expert = lax.broadcasted_iota(jnp.int32, (128, ROWS), 0)
    chosen = jnp.zeros((128, ROWS), F32)
    gates = jnp.zeros((128, ROWS), F32)
    for k in range(top):
        hit = expert == ids_ref[k : k + 1, :]
        chosen = jnp.where(hit, 1.0, chosen)
        gates = jnp.where(hit, gates_ref[k : k + 1, :], gates)
    row = lax.broadcasted_iota(jnp.int32, (ROWS, ROWS), 0)
    col = lax.broadcasted_iota(jnp.int32, (ROWS, ROWS), 1)
    upto = jnp.where(row >= col, 1.0, 0.0).astype(BF)
    same = jnp.where(row == col, 1.0, 0.0).astype(BF)
    flip = functools.partial(
        lax.dot_general, dimension_numbers=(((1,), (1,)), ((), ())), preferred_element_type=F32
    )
    chosen = chosen.astype(BF)
    place = jnp.where(flip(same, chosen) > 0.5, flip(upto, chosen), 0.0)
    out_ref[:, :MAIN] = x_ref[:, :MAIN]
    out_ref[:, MAIN : MAIN + 128] = place.astype(BF)
    out_ref[:, MAIN + 128 :] = flip(same, gates.astype(BF)).astype(BF)
    for k in range(4):
        parts_ref[k] = x_ref[:, MAIN + k * QUARTER : MAIN + (k + 1) * QUARTER]


def prepare(dev, slots, hidden, ids, gates, pages):
    count, width, ctx = pages.shape

    def whole(array):
        return pl.BlockSpec(array.shape, lambda r, *_: (0, 0))

    return pl.pallas_call(
        prepare_kernel,
        out_shape=(
            jax.ShapeDtypeStruct((ROWS, WHOLE), BF),
            jax.ShapeDtypeStruct((4, ROWS, QUARTER), BF),
            jax.ShapeDtypeStruct((width, ctx), BF),
        ),
        grid_spec=pltpu.PrefetchScalarGridSpec(
            num_scalar_prefetch=2,
            grid=(1,),
            in_specs=[
                whole(hidden),
                whole(ids),
                whole(gates),
                pl.BlockSpec((1, width, ctx), lambda r, dev, slot: (slot[dev[0]], 0, 0)),
            ],
            out_specs=(
                pl.BlockSpec((ROWS, WHOLE), lambda r, *_: (0, 0)),
                pl.BlockSpec((4, ROWS, QUARTER), lambda r, *_: (0, 0, 0)),
                pl.BlockSpec((width, ctx), lambda r, *_: (0, 0)),
            ),
        ),
        name="prepare",
    )(dev, slots, hidden, ids, gates, pages)


def local(
    cache_pages,
    queries,
    lengths,
    swap_slot,
    swap_mask,
    hidden,
    expert_ids,
    gate_weights,
    w_gate,
    w_up,
    w_down,
):
    ep_rank = lax.axis_index("ep").astype(jnp.int32)
    groups = lax.axis_size("tp")
    tp_rank = lax.axis_index("tp").astype(jnp.int32)
    device = ep_rank * groups + tp_rank
    mask = swap_mask[0]
    dev = device.reshape(1)
    pages = jnp.swapaxes(cache_pages, 1, 2)
    asked = jnp.swapaxes(queries, 1, 2)
    w_down = pltpu.with_memory_space_constraint(w_down, pltpu.HBM)
    xmain, xparts, own_page = prepare(dev, swap_slot, hidden, expert_ids.T, gate_weights.T, pages)
    page, attended = trade(
        own_page, jnp.right_shift(mask, 3), 3, 4, lambda: attend(dev, lengths, asked, pages)
    )
    xg, xq, wd_far = gather_rows(xmain, xparts, w_down)
    xg = xg.reshape(GROUPS // 2, PAIR, WHOLE)
    xq = xq.reshape(4, GROUPS // 2, PAIR, QUARTER)
    base = (ep_rank * EXL).reshape(1)
    page, (inner, tables) = trade(
        page, jnp.bitwise_and(mask, 7), 0, 8, lambda: experts_up(base, xg, xq, w_gate, w_up)
    )
    moe_rows = combine(inner, tables.reshape(GROUPS, GROUP, META), w_down, wd_far)
    attended = attend_one(dev, swap_slot, swap_mask, lengths, asked, page, attended)
    return attended, moe_rows


def solution(mesh):
    in_specs = (
        P(("ep", "tp"), None, None),
        P(("ep", "tp"), None, None),
        P(),
        P(),
        P(),
        P("ep", None),
        P("ep", None),
        P("ep", None),
        P("ep", None, "tp"),
        P("ep", None, "tp"),
        P("ep", "tp", None),
    )
    out_specs = (P(("ep", "tp"), None, None), P("ep", "tp"))
    return jax.shard_map(local, mesh=mesh, in_specs=in_specs, out_specs=out_specs, check_vma=False)
```

```python
import functools

import jax
import jax.numpy as jnp
from jax import lax
from jax.experimental import pallas as pl
from jax.experimental.pallas import tpu as pltpu
from jax.sharding import PartitionSpec as P

MESH = pl.DeviceIdType.MESH
BF = jnp.bfloat16
F32 = jnp.float32
LAT = 512
D = 3584
ROWS = 64
CAP = 10
EXL = 3
META = 256
GROUP = 256
GROUPS = 8
GSLOT = 40
PAIR = 2 * GROUP
PSLOT = 2 * GSLOT
HALF = D // 2
BLK = D // 4
FFL = 256
SCORE_SCALE = 192.0 ** (-0.5)
MASK_FLOOR = -1e30
VMEM_MAX = 60 * 1024 * 1024


def coords():
    e = lax.axis_index("ep")
    return e // 8, lax.rem(e // 2, 4), lax.rem(e, 2), lax.axis_index("tp")


def wrap(v):
    return lax.rem(v + 4, 4)


def greet(targets):
    barrier = pltpu.get_barrier_semaphore()
    for target in targets:
        pl.semaphore_signal(barrier, inc=1, device_id=target, device_id_type=MESH)
    pl.semaphore_wait(barrier, len(targets))


QUARTER = 256
MAIN = D - 4 * QUARTER
WHOLE = MAIN + META


def gather_kernel(
    x_ref, xp_ref, wd_ref, xg_ref, xq_ref, wdp_ref,
    ssem, rsem1, rsem2, dsend, drecv, ysend, yrecv, ydsend, ydrecv, wsem, lsem,
):
    x, z, c, y = coords()

    def dev(xx, zz, cc):
        return (xx * 8 + zz * 2 + cc, y)

    other = dev(x, z, 1 - c)
    above, below = (x * 8 + z * 2 + c, wrap(y + 1)), (x * 8 + z * 2 + c, wrap(y - 1))
    started = []
    count = {}

    def push(src, dst, target, send, recv):
        copy = pltpu.make_async_remote_copy(
            src_ref=src, dst_ref=dst, send_sem=send, recv_sem=recv, device_id=target, device_id_type=MESH
        )
        copy.start()
        started.append(copy)

    def ship(part, col, src, dst, target, recv):
        k = count.get((part, col), 0)
        count[part, col] = k + 1
        push(src, dst, target, ssem.at[part, col, k], recv)

    first = (x, z)
    second = (z, x)

    def place(part, col, f, s, lo=0, size=32):
        xx, zz = (f, s) if col == 0 else (s, f)
        rows = pl.ds(col * 32 + lo, size)
        return xg_ref.at[xx, zz, c, rows] if part else xq_ref.at[y, xx, zz, c, rows]

    def line(col, s, yy, lo=0, size=4, core=c):
        rows = pl.ds(col * 32, 32)
        if col == 0:
            return xq_ref.at[yy, pl.ds(lo, size), s, core, rows]
        return xq_ref.at[yy, s, pl.ds(lo, size), core, rows]

    def fdev(col, f):
        return dev(f, z, c) if col == 0 else dev(x, f, c)

    def sdev(col, s):
        return dev(x, s, c) if col == 0 else dev(s, z, c)

    def own(part, col):
        rows = pl.ds(col * 32, 32)
        return x_ref.at[rows] if part else xp_ref.at[y, rows]

    def expect(ref, sem):
        pltpu.make_async_copy(ref, ref, sem).wait()

    def share(part, col, f, s, src=None):
        if part == 0:
            return
        xx, zz = (f, s) if col == 0 else (s, f)
        slot = xx * 4 + zz
        ref = place(part, col, f, s)
        push(ref if src is None else src, ref, other, dsend.at[col, slot], drecv.at[col, slot])

    def fan(part, col, k, f, src=None):
        s = second[col]
        ref = place(part, col, f, s)
        src = ref if src is None else src
        ship(part, col, src, ref, sdev(col, wrap(s + 1)), rsem2.at[part, col, k, 0])
        ship(part, col, src, ref, sdev(col, wrap(s - 1)), rsem2.at[part, col, k, 1])

    def relay2(part, col, k, f):
        s = second[col]
        expect(place(part, col, f, wrap(s - 1)), rsem2.at[part, col, k, 0])
        ref = place(part, col, f, wrap(s - 1), 0, 16)
        ship(part, col, ref, ref, sdev(col, wrap(s + 1)), rsem2.at[part, col, k, 2])
        share(part, col, f, wrap(s - 1))
        expect(place(part, col, f, wrap(s + 1)), rsem2.at[part, col, k, 1])
        ref = place(part, col, f, wrap(s + 1), 16, 16)
        ship(part, col, ref, ref, sdev(col, wrap(s - 1)), rsem2.at[part, col, k, 3])
        share(part, col, f, wrap(s + 1))

    def last2(part, col, k, f):
        s = wrap(second[col] + 2)
        expect(place(part, col, f, s, 0, 16), rsem2.at[part, col, k, 2])
        expect(place(part, col, f, s, 16, 16), rsem2.at[part, col, k, 3])
        share(part, col, f, s)

    def open1(part):
        for col in (0, 1):
            p, s = first[col], second[col]
            ref = place(part, col, p, s)
            ship(part, col, own(part, col), ref, fdev(col, wrap(p + 1)), rsem1.at[part, col, 0])
            ship(part, col, own(part, col), ref, fdev(col, wrap(p - 1)), rsem1.at[part, col, 1])

    def relay1(part):
        for col in (0, 1):
            p, s = first[col], second[col]
            expect(place(part, col, wrap(p - 1), s), rsem1.at[part, col, 0])
            ref = place(part, col, wrap(p - 1), s, 0, 16)
            ship(part, col, ref, ref, fdev(col, wrap(p + 1)), rsem1.at[part, col, 2])
            expect(place(part, col, wrap(p + 1), s), rsem1.at[part, col, 1])
            ref = place(part, col, wrap(p + 1), s, 16, 16)
            ship(part, col, ref, ref, fdev(col, wrap(p - 1)), rsem1.at[part, col, 3])
            if part:
                for k, f in ((1, wrap(p - 1)), (2, wrap(p + 1))):
                    fan(1, col, k, f)
                    share(1, col, f, s)

    def last1(part, col):
        p, s = first[col], second[col]
        expect(place(part, col, wrap(p + 2), s, 0, 16), rsem1.at[part, col, 2])
        expect(place(part, col, wrap(p + 2), s, 16, 16), rsem1.at[part, col, 3])

    def source(col, k):
        return wrap(first[col] + (0, -1, 1, 2)[k])

    def lines_out(col):
        s = second[col]
        ref = line(col, s, y)
        ship(0, col, ref, ref, sdev(col, wrap(s + 1)), rsem2.at[0, col, 0, 0])
        ship(0, col, ref, ref, sdev(col, wrap(s - 1)), rsem2.at[0, col, 0, 1])

    def lines_on(col):
        s = second[col]
        expect(line(col, wrap(s - 1), y), rsem2.at[0, col, 0, 0])
        ref = line(col, wrap(s - 1), y, 0, 2)
        ship(0, col, ref, ref, sdev(col, wrap(s + 1)), rsem2.at[0, col, 0, 2])
        expect(line(col, wrap(s + 1), y), rsem2.at[0, col, 0, 1])
        ref = line(col, wrap(s + 1), y, 2, 2)
        ship(0, col, ref, ref, sdev(col, wrap(s - 1)), rsem2.at[0, col, 0, 3])

    def lines_in(col):
        s = wrap(second[col] + 2)
        expect(line(col, s, y, 0, 2), rsem2.at[0, col, 0, 2])
        expect(line(col, s, y, 2, 2), rsem2.at[0, col, 0, 3])

    def part_of(yy, lo, size=2, core=c):
        return xq_ref.at[yy, pl.ds(lo, size), :, core]

    def hand(d):
        ref = part_of(wrap(y + d), 0, 4)
        push(ref, ref, other, ydsend.at[d], ydrecv.at[d])

    locals_ = [
        pltpu.make_async_copy(xp_ref.at[y], xq_ref.at[y, x, z, c], lsem.at[0]),
        pltpu.make_async_copy(x_ref, xg_ref.at[x, z, c], lsem.at[1]),
    ]
    for copy in locals_:
        copy.start()
    greet(
        [dev(wrap(x + 1), z, c), dev(wrap(x - 1), z, c), dev(x, wrap(z + 1), c), dev(x, wrap(z - 1), c)]
        + [other, above, below]
    )
    open1(0)
    far = pl.ds(pl.multiple_of((1 - c) * HALF, HALF), HALF)
    push(wd_ref.at[:, :, far], wdp_ref, other, wsem.at[0], wsem.at[1])
    relay1(0)
    open1(1)
    locals_[0].wait()
    for col in (0, 1):
        last1(0, col)
        lines_out(col)
    for col in (0, 1):
        lines_on(col)
    for col in (0, 1):
        fan(1, col, 0, first[col], own(1, col))
        share(1, col, first[col], second[col], own(1, col))
    relay1(1)
    for col in (0, 1):
        lines_in(col)
    for k, lo, target in ((0, 0, above), (2, 2, below), (1, 2, above), (3, 0, below)):
        ref = part_of(y, lo)
        push(ref, ref, target, ysend.at[k], yrecv.at[k])
    hand(0)
    for col in (0, 1):
        relay2(1, col, 0, source(col, 0))
    for col in (0, 1):
        last1(1, col)
        fan(1, col, 3, source(col, 3))
        share(1, col, source(col, 3), second[col])
    ref = part_of(wrap(y - 1), 0)
    expect(ref, yrecv.at[0])
    push(ref, ref, above, ysend.at[4], yrecv.at[4])
    ref = part_of(wrap(y + 1), 2)
    expect(ref, yrecv.at[2])
    push(ref, ref, below, ysend.at[5], yrecv.at[5])
    for k in (1, 2):
        for col in (0, 1):
            relay2(1, col, k, source(col, k))
    for col in (0, 1):
        last2(1, col, 0, source(col, 0))
    expect(part_of(wrap(y - 1), 2), yrecv.at[1])
    hand(3)
    expect(part_of(wrap(y + 1), 0), yrecv.at[3])
    hand(1)
    for col in (0, 1):
        relay2(1, col, 3, source(col, 3))
    expect(part_of(wrap(y + 2), 0), yrecv.at[4])
    expect(part_of(wrap(y + 2), 2), yrecv.at[5])
    hand(2)
    for k in (1, 2, 3):
        for col in (0, 1):
            last2(1, col, k, source(col, k))
    for col in (0, 1):
        for slot in range(16):
            expect(xg_ref.at[slot // 4, slot % 4, 1 - c, pl.ds(col * 32, 32)], drecv.at[col, slot])
    for d in range(4):
        expect(part_of(wrap(y + d), 0, 4, 1 - c), ydrecv.at[d])
    expect(wdp_ref, wsem.at[1])
    for copy in locals_[1:]:
        copy.wait()
    for copy in started:
        copy.wait_send()


def gather_rows(xmain, xparts, w_down):
    dma = pltpu.SemaphoreType.DMA
    return pl.pallas_call(
        gather_kernel,
        out_shape=(
            jax.ShapeDtypeStruct((4, 4, 2, ROWS, WHOLE), BF),
            jax.ShapeDtypeStruct((4, 4, 4, 2, ROWS, QUARTER), BF),
            pltpu.HBM((EXL, FFL, HALF), BF),
        ),
        in_specs=[pl.BlockSpec(memory_space=pltpu.VMEM)] * 2 + [pl.BlockSpec(memory_space=pltpu.HBM)],
        out_specs=(pl.BlockSpec(memory_space=pltpu.VMEM),) * 2
        + (pl.BlockSpec(memory_space=pltpu.HBM),),
        scratch_shapes=[
            dma((2, 2, 20)),
            dma((2, 2, 4)),
            dma((2, 2, 4, 4)),
            dma((2, 16)),
            dma((2, 16)),
            dma((6,)),
            dma((6,)),
            dma((4,)),
            dma((4,)),
            dma((2,)),
            dma((2,)),
        ],
        compiler_params=pltpu.CompilerParams(
            collective_id=0, has_side_effects=True, vmem_limit_bytes=18 * 1024 * 1024
        ),
        name="gather_rows",
    )(xmain, xparts, w_down)


def slot_numbers(shape, axis, gslot):
    s = lax.broadcasted_iota(jnp.int32, shape, axis)
    g = lax.broadcasted_iota(jnp.int32, shape, 1 - axis)
    expert = jnp.zeros(shape, jnp.int32)
    for k in range(1, shape[axis] // gslot):
        expert = expert + (s >= k * gslot).astype(jnp.int32)
    u = s - expert * gslot
    rank = (u * 205) >> 11
    want = jnp.where((g >> 6) == rank, u - rank * CAP + 1, -1)
    return want.astype(F32)


def expert_lanes(shape, axis, base, gslot):
    s = lax.broadcasted_iota(jnp.int32, shape, axis)
    e = lax.broadcasted_iota(jnp.int32, shape, 1 - axis)
    expert = jnp.zeros(shape, jnp.int32)
    for k in range(1, shape[axis] // gslot):
        expert = expert + (s >= k * gslot).astype(jnp.int32)
    return jnp.where(expert + base == e, 1.0, 0.0).astype(BF)


def up_kernel(base_ref, x_ref, xp_ref, wg_ref, wu_hbm, out_ref, tab_ref, xc, wu_ref, sem):
    load = pltpu.make_async_copy(wu_hbm, wu_ref, sem)
    load.start()
    tab_ref[...] = x_ref[:, :, MAIN:WHOLE]
    want = slot_numbers((EXL * PSLOT, PAIR), 0, PSLOT)
    lanes = expert_lanes((EXL * PSLOT, 128), 0, base_ref[0], PSLOT)

    @pl.loop(0, GROUPS // 2)
    def _(q):
        table = x_ref[q, :, MAIN : MAIN + 128]
        named = lax.dot_general(lanes, table, (((1,), (1,)), ((), ())), preferred_element_type=F32)
        pick = jnp.where(named == want, 1.0, 0.0).astype(BF)
        start = pl.multiple_of(q * PSLOT, 16)

        def keep(rows, cols):
            for e in range(EXL):
                xc[e, pl.ds(start, PSLOT), cols] = rows[e * PSLOT : (e + 1) * PSLOT].astype(BF)

        for n in range(MAIN // 512):
            cols = slice(n * 512, (n + 1) * 512)
            keep(jnp.dot(pick, x_ref[q, :, cols], preferred_element_type=F32), cols)
        for n in range(4):
            cols = slice(MAIN + n * QUARTER, MAIN + (n + 1) * QUARTER)
            keep(jnp.dot(pick, xp_ref[n, q], preferred_element_type=F32), cols)

    load.wait()

    @pl.loop(0, EXL)
    def _(e):
        rows = xc[e]
        gate = jnp.dot(rows, wg_ref[e], preferred_element_type=F32)
        up = jnp.dot(rows, wu_ref[e], preferred_element_type=F32)
        out_ref[e] = (gate / (1.0 + jnp.exp(-gate)) * up).astype(BF)


def experts_up(base, xg, xq, w_gate, w_up):
    return pl.pallas_call(
        up_kernel,
        out_shape=(
            jax.ShapeDtypeStruct((EXL, GROUPS * GSLOT, FFL), BF),
            jax.ShapeDtypeStruct((GROUPS // 2, PAIR, META), BF),
        ),
        in_specs=[pl.BlockSpec(memory_space=pltpu.SMEM)]
        + [pl.BlockSpec(memory_space=pltpu.VMEM)] * 3
        + [pl.BlockSpec(memory_space=pltpu.HBM)],
        out_specs=(pl.BlockSpec(memory_space=pltpu.VMEM),) * 2,
        scratch_shapes=[
            pltpu.VMEM((EXL, GROUPS * GSLOT, D), BF),
            pltpu.VMEM((EXL, D, FFL), BF),
            pltpu.SemaphoreType.DMA,
        ],
        cost_estimate=pl.CostEstimate(flops=7_000_000_000, bytes_accessed=30_000_000, transcendentals=0),
        compiler_params=pltpu.CompilerParams(vmem_limit_bytes=20 * 1024 * 1024),
        name="experts_up",
    )(base, xg, xq, w_gate, w_up)


def combine_kernel(
    inner_ref, meta, wd_hbm, wdp_hbm, out_ref,
    inner2, wdh, outc, want, yp, st1, fin1, st2, fin2, fin3,
    lsem, isem, s1, r1, s2, r2, s3, r3,
):
    x, z, c, y = coords()

    def dev(xx, zz, cc, yy):
        return (xx * 8 + zz * 2 + cc, yy)

    other = dev(x, z, 1 - c, y)
    waits = []

    def ship(src, dst, target, send, recv):
        copy = pltpu.make_async_remote_copy(
            src_ref=src, dst_ref=dst, send_sem=send, recv_sem=recv, device_id=target, device_id_type=MESH
        )
        copy.start()
        waits.append(copy)
        return copy

    def expect(ref, sem):
        pltpu.make_async_copy(ref, ref, sem).wait()

    near = pl.ds(pl.multiple_of(c * HALF, HALF), HALF)
    loads = [
        pltpu.make_async_copy(wd_hbm.at[:, :, near], wdh.at[c], lsem.at[0]),
        pltpu.make_async_copy(wdp_hbm, wdh.at[1 - c], lsem.at[1]),
    ]
    for load in loads:
        load.start()
    want[...] = slot_numbers((GROUP, 2 * EXL * GSLOT), 1, GSLOT)
    lanes = expert_lanes((128, 2 * EXL * GSLOT), 1, (x * 4 + z) * 2 * EXL, GSLOT)
    greet(
        [dev(wrap(x + 1), z, c, y), dev(wrap(x - 1), z, c, y), dev(x, wrap(z + 1), c, y), dev(x, wrap(z - 1), c, y)]
        + [other]
        + [dev(x, z, core, wrap(y + k)) for k in (1, 2, 3) for core in (0, 1)]
    )
    swap = ship(inner_ref, inner2, other, isem.at[0], isem.at[1])

    def down(core, source):
        @pl.loop(0, EXL, unroll=EXL)
        def _(e):
            row = pl.multiple_of((core * EXL + e) * GSLOT, 8)
            for n in range(2):
                cols = slice(n * BLK, (n + 1) * BLK)
                part = jnp.dot(source[e], wdh[core, e, :, cols], preferred_element_type=F32)
                for q in range(GROUPS):
                    outc[n, q, pl.ds(row, GSLOT), :] = part[q * GSLOT : (q + 1) * GSLOT]

    loads[0].wait()
    down(c, inner_ref)
    loads[1].wait()
    swap.wait_recv()
    down(1 - c, inner2)

    def scatter(col, start, count):
        @pl.loop(0, 2 * count, unroll=4 if count == 4 else 2)
        def _(i):
            q = wrap(x + start + i // 2) * 2 + lax.rem(i, 2)
            named = jnp.dot(meta[q, :, 0:128], lanes, preferred_element_type=F32)
            gate = jnp.dot(meta[q, :, 128:256], lanes, preferred_element_type=F32)
            mix = jnp.where(named == want[...], gate, 0.0).astype(BF)
            part = jnp.dot(mix, outc[col, q].astype(BF), preferred_element_type=F32).astype(BF)
            xx = q // 2
            for k in range(2):
                piece = part[k * 128 : (k + 1) * 128]
                zz = lax.rem(q, 2) * 2 + k
                if col == 0:
                    yp[0, xx, zz] = piece
                else:
                    yp[1, zz, xx] = piece

    first, second = (x, z), (z, x)

    def fdev(col, f):
        return dev(f, z, c, y) if col == 0 else dev(x, f, c, y)

    def sdev(col, s):
        return dev(x, s, c, y) if col == 0 else dev(s, z, c, y)

    def open0(col):
        p = first[col]
        up, dn = fdev(col, wrap(p + 1)), fdev(col, wrap(p - 1))
        ship(yp.at[col, wrap(p + 2), pl.ds(0, 2)], st1.at[col, 0], up, s1.at[col, 0], r1.at[col, 0])
        ship(yp.at[col, wrap(p + 2), pl.ds(2, 2)], st1.at[col, 1], dn, s1.at[col, 1], r1.at[col, 1])

    def open1(col):
        p = first[col]
        up, dn = fdev(col, wrap(p + 1)), fdev(col, wrap(p - 1))
        ship(yp.at[col, wrap(p + 1), pl.ds(2, 2)], fin1.at[col, 0, pl.ds(2, 2)], up, s1.at[col, 2], r1.at[col, 2])
        ship(yp.at[col, wrap(p - 1), pl.ds(0, 2)], fin1.at[col, 1, pl.ds(0, 2)], dn, s1.at[col, 3], r1.at[col, 3])

    def mid1(col):
        p = first[col]
        up, dn = fdev(col, wrap(p + 1)), fdev(col, wrap(p - 1))
        for side, (f, lo, target) in enumerate(((wrap(p + 1), 0, up), (wrap(p - 1), 2, dn))):
            expect(st1.at[col, side], r1.at[col, side])
            for k in range(2):
                acc = yp[col, f, lo + k].astype(F32) + st1[col, side, k].astype(F32)
                yp[col, f, lo + k] = acc.astype(BF)
            ship(
                yp.at[col, f, pl.ds(lo, 2)],
                fin1.at[col, side, pl.ds(lo, 2)],
                target,
                s1.at[col, 4 + side],
                r1.at[col, 4 + side],
            )

    def end1(col):
        p, s = first[col], second[col]
        for side, lo in ((0, 2), (1, 0), (0, 0), (1, 2)):
            expect(
                fin1.at[col, side, pl.ds(lo, 2)],
                r1.at[col, {(0, 2): 2, (1, 0): 3, (0, 0): 4, (1, 2): 5}[(side, lo)]],
            )
        up, dn = sdev(col, wrap(s + 1)), sdev(col, wrap(s - 1))

        def fold(t):
            acc = yp[col, p, t].astype(F32) + fin1[col, 0, t].astype(F32) + fin1[col, 1, t].astype(F32)
            yp[col, p, t] = acc.astype(BF)

        lo, hi = pl.ds(0, 64), pl.ds(64, 64)
        t = wrap(s + 2)
        fold(t)
        ship(yp.at[col, p, t, lo], st2.at[col, 0], up, s2.at[col, 0], r2.at[col, 0])
        ship(yp.at[col, p, t, hi], st2.at[col, 1], dn, s2.at[col, 1], r2.at[col, 1])
        t = wrap(s + 1)
        fold(t)
        ship(yp.at[col, p, t, hi], fin2.at[col, 0, hi], up, s2.at[col, 2], r2.at[col, 2])
        t = wrap(s - 1)
        fold(t)
        ship(yp.at[col, p, t, lo], fin2.at[col, 1, lo], dn, s2.at[col, 3], r2.at[col, 3])
        fold(s)

    def mid2(col):
        p, s = first[col], second[col]
        up, dn = sdev(col, wrap(s + 1)), sdev(col, wrap(s - 1))
        for side, (t, lo, target) in enumerate(((wrap(s + 1), 0, up), (wrap(s - 1), 64, dn))):
            expect(st2.at[col, side], r2.at[col, side])
            acc = yp[col, p, t, lo : lo + 64].astype(F32) + st2[col, side].astype(F32)
            yp[col, p, t, lo : lo + 64] = acc.astype(BF)
            rows = pl.ds(lo, 64)
            ship(
                yp.at[col, p, t, rows], fin2.at[col, side, rows], target, s2.at[col, 4 + side], r2.at[col, 4 + side]
            )

    def end2(col):
        p, s = first[col], second[col]
        for side, lo, k in ((0, 64, 2), (1, 0, 3), (0, 0, 4), (1, 64, 5)):
            expect(fin2.at[col, side, pl.ds(lo, 64)], r2.at[col, k])
        acc = yp[col, p, s].astype(F32) + fin2[col, 0].astype(F32) + fin2[col, 1].astype(F32)
        yp[col, p, s] = acc.astype(BF)
        goal = 2 * c + col

        def final(core, target, k):
            pltpu.make_async_remote_copy(
                src_ref=yp.at[col, p, s, pl.ds(pl.multiple_of(core * 64, 64), 64)],
                dst_ref=fin3.at[k],
                send_sem=s3.at[col, core],
                recv_sem=r3.at[k],
                device_id=target,
                device_id_type=MESH,
            ).start()

        @pl.when(y == goal)
        def _():
            final(1 - c, other, 0)

        for k in (1, 2, 3):

            @pl.when(wrap(goal + k) == y)
            def _():
                for core in (0, 1):
                    final(core, dev(x, z, core, goal), k)

    def end3(col):
        p, s = first[col], second[col]
        half = yp.at[col, p, s, pl.ds(0, 64)]
        expect(half, s3.at[col, 1 - c])

        @pl.when(y != 2 * c + col)
        def _():
            expect(half, s3.at[col, c])

        @pl.when(y == 2 * c + col)
        def _():
            acc = yp[col, p, s, pl.ds(pl.multiple_of(c * 64, 64), 64)].astype(F32)
            for k in (1, 2, 3):
                acc = acc + fin3[k].astype(F32)
            out_ref[...] = acc.astype(BF)

    scatter(1, 0, 4)
    open0(1)
    open1(1)
    scatter(0, 2, 1)
    open0(0)
    scatter(0, 3, 3)
    open1(0)
    for step in (mid1, end1, mid2, end2):
        for col in (1, 0):
            step(col)
    for k in (1, 2, 3):
        expect(fin3.at[k], r3.at[k])
    end3(0)
    end3(1)

    @pl.when(y // 2 != c)
    def _():
        expect(fin3.at[0], r3.at[0])
        acc = fin3[0].astype(F32)
        for k in (1, 2, 3):
            acc = acc + fin3[k].astype(F32)
        out_ref[...] = acc.astype(BF)

    for copy in waits:
        copy.wait_send()


def combine(inner, tables, w_down, wd_far):
    return pl.pallas_call(
        combine_kernel,
        out_shape=jax.ShapeDtypeStruct((ROWS, BLK), BF),
        in_specs=[pl.BlockSpec(memory_space=pltpu.VMEM)] * 2 + [pl.BlockSpec(memory_space=pltpu.HBM)] * 2,
        out_specs=pl.BlockSpec(memory_space=pltpu.VMEM),
        scratch_shapes=[
            pltpu.VMEM((EXL, GROUPS * GSLOT, FFL), BF),
            pltpu.VMEM((2, EXL, FFL, HALF), BF),
            pltpu.VMEM((2, GROUPS, 2 * EXL * GSLOT, BLK), F32),
            pltpu.VMEM((GROUP, 2 * EXL * GSLOT), F32),
            pltpu.VMEM((2, 4, 4, 128, BLK), BF),
            pltpu.VMEM((2, 2, 2, 128, BLK), BF),
            pltpu.VMEM((2, 2, 4, 128, BLK), BF),
            pltpu.VMEM((2, 2, 64, BLK), BF),
            pltpu.VMEM((2, 2, 128, BLK), BF),
            pltpu.VMEM((4, 64, BLK), BF),
            pltpu.SemaphoreType.DMA((2,)),
            pltpu.SemaphoreType.DMA((2,)),
            pltpu.SemaphoreType.DMA((2, 6)),
            pltpu.SemaphoreType.DMA((2, 6)),
            pltpu.SemaphoreType.DMA((2, 6)),
            pltpu.SemaphoreType.DMA((2, 6)),
            pltpu.SemaphoreType.DMA((2, 2)),
            pltpu.SemaphoreType.DMA((4,)),
        ],
        compiler_params=pltpu.CompilerParams(
            collective_id=1, has_side_effects=True, vmem_limit_bytes=38 * 1024 * 1024
        ),
        name="combine",
    )(inner, tables, w_down, wd_far)


def attend_page(query, page, length):
    scores = lax.dot_general(query, page, (((0,), (0,)), ((), ())), preferred_element_type=F32)
    scores = scores * SCORE_SCALE
    live = lax.broadcasted_iota(jnp.int32, scores.shape, 1) < length
    scores = jnp.where(live, scores, MASK_FLOOR)
    weight = jnp.exp(scores - jnp.max(scores, axis=1, keepdims=True))
    total = jnp.sum(weight, axis=1, keepdims=True)
    blended = lax.dot_general(
        weight.astype(BF), page[:LAT], (((1,), (1,)), ((), ())), preferred_element_type=F32
    )
    return (blended * (1.0 / total)).astype(BF)


def attend_kernel(dev_ref, lens_ref, q_ref, page_ref, out_ref):
    count = q_ref.shape[0]
    base = dev_ref[0] * 16 + pl.program_id(0) * count
    for k in range(count):
        out_ref[k] = attend_page(q_ref[k], page_ref[k], lens_ref[base + k])


def attend(dev, lens, queries, pages):
    count, width, heads = queries.shape
    ctx = pages.shape[2]
    step = 4
    return pl.pallas_call(
        attend_kernel,
        out_shape=jax.ShapeDtypeStruct((count, heads, LAT), BF),
        grid_spec=pltpu.PrefetchScalarGridSpec(
            num_scalar_prefetch=2,
            grid=(count // step,),
            in_specs=[
                pl.BlockSpec((step, width, heads), lambda r, *_: (r, 0, 0)),
                pl.BlockSpec((step, width, ctx), lambda r, *_: (r, 0, 0)),
            ],
            out_specs=pl.BlockSpec((step, heads, LAT), lambda r, *_: (r, 0, 0)),
        ),
        cost_estimate=pl.CostEstimate(flops=2_400_000_000, bytes_accessed=20_000_000, transcendentals=0),
        name="attend",
    )(dev, lens, queries, pages)


def attend_one_kernel(dev_ref, slot_ref, mask_ref, lens_ref, q_ref, page_ref, all_ref, out_ref):
    partner = jnp.bitwise_xor(dev_ref[0], mask_ref[0] * 4)
    length = lens_ref[partner * 16 + slot_ref[partner]]
    out_ref[0] = attend_page(q_ref[0], page_ref[...], length)


def attend_one(dev, slots, mask, lens, queries, page, attended):
    count, width, heads = queries.shape
    return pl.pallas_call(
        attend_one_kernel,
        out_shape=jax.ShapeDtypeStruct(attended.shape, BF),
        grid_spec=pltpu.PrefetchScalarGridSpec(
            num_scalar_prefetch=4,
            grid=(1,),
            in_specs=[
                pl.BlockSpec((1, width, heads), lambda r, dev, slot, *_: (slot[dev[0]], 0, 0)),
                pl.BlockSpec(page.shape, lambda r, *_: (0, 0)),
                pl.BlockSpec(memory_space=pl.ANY),
            ],
            out_specs=pl.BlockSpec((1, heads, LAT), lambda r, dev, slot, *_: (slot[dev[0]], 0, 0)),
        ),
        input_output_aliases={6: 0},
        name="attend_one",
    )(dev, slots, mask, lens, queries, page, attended)


def trade(page, bits, shift, steps, beside):
    count = lax.axis_size("ep")

    def branch(m):
        def run(block):
            if m:
                block = lax.ppermute(block, "ep", [(i, i ^ (m << shift)) for i in range(count)])
            return block, beside()

        return run

    return lax.switch(bits, [branch(m) for m in range(steps)], page)


def prepare_kernel(dev_ref, slot_ref, x_ref, ids_ref, gates_ref, page_ref, out_ref, parts_ref, own_ref):
    own_ref[...] = page_ref[0]
    top = ids_ref.shape[0]
    expert = lax.broadcasted_iota(jnp.int32, (128, ROWS), 0)
    chosen = jnp.zeros((128, ROWS), F32)
    gates = jnp.zeros((128, ROWS), F32)
    for k in range(top):
        hit = expert == ids_ref[k : k + 1, :]
        chosen = jnp.where(hit, 1.0, chosen)
        gates = jnp.where(hit, gates_ref[k : k + 1, :], gates)
    row = lax.broadcasted_iota(jnp.int32, (ROWS, ROWS), 0)
    col = lax.broadcasted_iota(jnp.int32, (ROWS, ROWS), 1)
    upto = jnp.where(row >= col, 1.0, 0.0).astype(BF)
    same = jnp.where(row == col, 1.0, 0.0).astype(BF)
    flip = functools.partial(
        lax.dot_general, dimension_numbers=(((1,), (1,)), ((), ())), preferred_element_type=F32
    )
    chosen = chosen.astype(BF)
    place = jnp.where(flip(same, chosen) > 0.5, flip(upto, chosen), 0.0)
    out_ref[:, :MAIN] = x_ref[:, :MAIN]
    out_ref[:, MAIN : MAIN + 128] = place.astype(BF)
    out_ref[:, MAIN + 128 :] = flip(same, gates.astype(BF)).astype(BF)
    for k in range(4):
        parts_ref[k] = x_ref[:, MAIN + k * QUARTER : MAIN + (k + 1) * QUARTER]


def prepare(dev, slots, hidden, ids, gates, pages):
    count, width, ctx = pages.shape

    def whole(array):
        return pl.BlockSpec(array.shape, lambda r, *_: (0, 0))

    return pl.pallas_call(
        prepare_kernel,
        out_shape=(
            jax.ShapeDtypeStruct((ROWS, WHOLE), BF),
            jax.ShapeDtypeStruct((4, ROWS, QUARTER), BF),
            jax.ShapeDtypeStruct((width, ctx), BF),
        ),
        grid_spec=pltpu.PrefetchScalarGridSpec(
            num_scalar_prefetch=2,
            grid=(1,),
            in_specs=[
                whole(hidden),
                whole(ids),
                whole(gates),
                pl.BlockSpec((1, width, ctx), lambda r, dev, slot: (slot[dev[0]], 0, 0)),
            ],
            out_specs=(
                pl.BlockSpec((ROWS, WHOLE), lambda r, *_: (0, 0)),
                pl.BlockSpec((4, ROWS, QUARTER), lambda r, *_: (0, 0, 0)),
                pl.BlockSpec((width, ctx), lambda r, *_: (0, 0)),
            ),
        ),
        name="prepare",
    )(dev, slots, hidden, ids, gates, pages)


def local(
    cache_pages,
    queries,
    lengths,
    swap_slot,
    swap_mask,
    hidden,
    expert_ids,
    gate_weights,
    w_gate,
    w_up,
    w_down,
):
    ep_rank = lax.axis_index("ep").astype(jnp.int32)
    groups = lax.axis_size("tp")
    tp_rank = lax.axis_index("tp").astype(jnp.int32)
    device = ep_rank * groups + tp_rank
    mask = swap_mask[0]
    dev = device.reshape(1)
    pages = jnp.swapaxes(cache_pages, 1, 2)
    asked = jnp.swapaxes(queries, 1, 2)
    w_down = pltpu.with_memory_space_constraint(w_down, pltpu.HBM)
    xmain, xparts, own_page = prepare(dev, swap_slot, hidden, expert_ids.T, gate_weights.T, pages)
    page, attended = trade(
        own_page, jnp.right_shift(mask, 3), 3, 4, lambda: attend(dev, lengths, asked, pages)
    )
    xg, xq, wd_far = gather_rows(xmain, xparts, w_down)
    xg = xg.reshape(GROUPS // 2, PAIR, WHOLE)
    xq = xq.reshape(4, GROUPS // 2, PAIR, QUARTER)
    base = (ep_rank * EXL).reshape(1)
    page, (inner, tables) = trade(
        page, jnp.bitwise_and(mask, 7), 0, 8, lambda: experts_up(base, xg, xq, w_gate, w_up)
    )
    moe_rows = combine(inner, tables.reshape(GROUPS, GROUP, META), w_down, wd_far)
    attended = attend_one(dev, swap_slot, swap_mask, lengths, asked, page, attended)
    return attended, moe_rows


def solution(mesh):
    in_specs = (
        P(("ep", "tp"), None, None),
        P(("ep", "tp"), None, None),
        P(),
        P(),
        P(),
        P("ep", None),
        P("ep", None),
        P("ep", None),
        P("ep", None, "tp"),
        P("ep", None, "tp"),
        P("ep", "tp", None),
    )
    out_specs = (P(("ep", "tp"), None, None), P("ep", "tp"))
    return jax.shard_map(local, mesh=mesh, in_specs=in_specs, out_specs=out_specs, check_vma=False)
```

```python
import functools

import jax
import jax.numpy as jnp
from jax import lax
from jax.experimental import pallas as pl
from jax.experimental.pallas import tpu as pltpu
from jax.sharding import PartitionSpec as P

MESH = pl.DeviceIdType.MESH
BF = jnp.bfloat16
F32 = jnp.float32
LAT = 512
D = 3584
ROWS = 64
CAP = 10
EXL = 3
META = 256
GROUP = 256
GROUPS = 8
GSLOT = 40
PAIR = 2 * GROUP
PSLOT = 2 * GSLOT
HALF = D // 2
BLK = D // 4
FFL = 256
SCORE_SCALE = 192.0 ** (-0.5)
MASK_FLOOR = -1e30
VMEM_MAX = 60 * 1024 * 1024


def coords():
    e = lax.axis_index("ep")
    return e // 8, lax.rem(e // 2, 4), lax.rem(e, 2), lax.axis_index("tp")


def wrap(v):
    return lax.rem(v + 4, 4)


def greet(targets):
    barrier = pltpu.get_barrier_semaphore()
    for target in targets:
        pl.semaphore_signal(barrier, inc=1, device_id=target, device_id_type=MESH)
    pl.semaphore_wait(barrier, len(targets))


QUARTER = 256
MAIN = D - 4 * QUARTER
WHOLE = MAIN + META


def gather_kernel(
    x_ref, xp_ref, wd_ref, xg_ref, xq_ref, wdp_ref,
    ssem, rsem1, rsem2, dsend, drecv, ysend, yrecv, ydsend, ydrecv, wsem, lsem,
):
    x, z, c, y = coords()

    def dev(xx, zz, cc):
        return (xx * 8 + zz * 2 + cc, y)

    other = dev(x, z, 1 - c)
    above, below = (x * 8 + z * 2 + c, wrap(y + 1)), (x * 8 + z * 2 + c, wrap(y - 1))
    started = []
    count = {}

    def push(src, dst, target, send, recv):
        copy = pltpu.make_async_remote_copy(
            src_ref=src, dst_ref=dst, send_sem=send, recv_sem=recv, device_id=target, device_id_type=MESH
        )
        copy.start()
        started.append(copy)

    def ship(part, col, src, dst, target, recv):
        k = count.get((part, col), 0)
        count[part, col] = k + 1
        push(src, dst, target, ssem.at[part, col, k], recv)

    first = (x, z)
    second = (z, x)

    def place(part, col, f, s, lo=0, size=32):
        xx, zz = (f, s) if col == 0 else (s, f)
        rows = pl.ds(col * 32 + lo, size)
        return xg_ref.at[xx, zz, c, rows] if part else xq_ref.at[y, xx, zz, c, rows]

    def line(col, s, yy, lo=0, size=4, core=c):
        rows = pl.ds(col * 32, 32)
        if col == 0:
            return xq_ref.at[yy, pl.ds(lo, size), s, core, rows]
        return xq_ref.at[yy, s, pl.ds(lo, size), core, rows]

    def fdev(col, f):
        return dev(f, z, c) if col == 0 else dev(x, f, c)

    def sdev(col, s):
        return dev(x, s, c) if col == 0 else dev(s, z, c)

    def own(part, col):
        rows = pl.ds(col * 32, 32)
        return x_ref.at[rows] if part else xp_ref.at[y, rows]

    def expect(ref, sem):
        pltpu.make_async_copy(ref, ref, sem).wait()

    def share(part, col, f, s, src=None):
        if part == 0:
            return
        xx, zz = (f, s) if col == 0 else (s, f)
        slot = xx * 4 + zz
        ref = place(part, col, f, s)
        push(ref if src is None else src, ref, other, dsend.at[col, slot], drecv.at[col, slot])

    def fan(part, col, k, f, src=None):
        s = second[col]
        ref = place(part, col, f, s)
        src = ref if src is None else src
        ship(part, col, src, ref, sdev(col, wrap(s + 1)), rsem2.at[part, col, k, 0])
        ship(part, col, src, ref, sdev(col, wrap(s - 1)), rsem2.at[part, col, k, 1])

    def relay2(part, col, k, f):
        s = second[col]
        expect(place(part, col, f, wrap(s - 1)), rsem2.at[part, col, k, 0])
        ref = place(part, col, f, wrap(s - 1), 0, 16)
        ship(part, col, ref, ref, sdev(col, wrap(s + 1)), rsem2.at[part, col, k, 2])
        share(part, col, f, wrap(s - 1))
        expect(place(part, col, f, wrap(s + 1)), rsem2.at[part, col, k, 1])
        ref = place(part, col, f, wrap(s + 1), 16, 16)
        ship(part, col, ref, ref, sdev(col, wrap(s - 1)), rsem2.at[part, col, k, 3])
        share(part, col, f, wrap(s + 1))

    def last2(part, col, k, f):
        s = wrap(second[col] + 2)
        expect(place(part, col, f, s, 0, 16), rsem2.at[part, col, k, 2])
        expect(place(part, col, f, s, 16, 16), rsem2.at[part, col, k, 3])
        share(part, col, f, s)

    def open1(part):
        for col in (0, 1):
            p, s = first[col], second[col]
            ref = place(part, col, p, s)
            ship(part, col, own(part, col), ref, fdev(col, wrap(p + 1)), rsem1.at[part, col, 0])
            ship(part, col, own(part, col), ref, fdev(col, wrap(p - 1)), rsem1.at[part, col, 1])

    def relay1(part):
        for col in (0, 1):
            p, s = first[col], second[col]
            expect(place(part, col, wrap(p - 1), s), rsem1.at[part, col, 0])
            ref = place(part, col, wrap(p - 1), s, 0, 16)
            ship(part, col, ref, ref, fdev(col, wrap(p + 1)), rsem1.at[part, col, 2])
            expect(place(part, col, wrap(p + 1), s), rsem1.at[part, col, 1])
            ref = place(part, col, wrap(p + 1), s, 16, 16)
            ship(part, col, ref, ref, fdev(col, wrap(p - 1)), rsem1.at[part, col, 3])
            if part:
                for k, f in ((1, wrap(p - 1)), (2, wrap(p + 1))):
                    fan(1, col, k, f)
                    share(1, col, f, s)

    def last1(part, col):
        p, s = first[col], second[col]
        expect(place(part, col, wrap(p + 2), s, 0, 16), rsem1.at[part, col, 2])
        expect(place(part, col, wrap(p + 2), s, 16, 16), rsem1.at[part, col, 3])

    def source(col, k):
        return wrap(first[col] + (0, -1, 1, 2)[k])

    def lines_out(col):
        s = second[col]
        ref = line(col, s, y)
        ship(0, col, ref, ref, sdev(col, wrap(s + 1)), rsem2.at[0, col, 0, 0])
        ship(0, col, ref, ref, sdev(col, wrap(s - 1)), rsem2.at[0, col, 0, 1])

    def lines_on(col):
        s = second[col]
        expect(line(col, wrap(s - 1), y), rsem2.at[0, col, 0, 0])
        ref = line(col, wrap(s - 1), y, 0, 2)
        ship(0, col, ref, ref, sdev(col, wrap(s + 1)), rsem2.at[0, col, 0, 2])
        expect(line(col, wrap(s + 1), y), rsem2.at[0, col, 0, 1])
        ref = line(col, wrap(s + 1), y, 2, 2)
        ship(0, col, ref, ref, sdev(col, wrap(s - 1)), rsem2.at[0, col, 0, 3])

    def lines_in(col):
        s = wrap(second[col] + 2)
        expect(line(col, s, y, 0, 2), rsem2.at[0, col, 0, 2])
        expect(line(col, s, y, 2, 2), rsem2.at[0, col, 0, 3])

    def part_of(yy, lo, size=2, core=c):
        return xq_ref.at[yy, pl.ds(lo, size), :, core]

    def hand(d):
        ref = part_of(wrap(y + d), 0, 4)
        push(ref, ref, other, ydsend.at[d], ydrecv.at[d])

    locals_ = [
        pltpu.make_async_copy(xp_ref.at[y], xq_ref.at[y, x, z, c], lsem.at[0]),
        pltpu.make_async_copy(x_ref, xg_ref.at[x, z, c], lsem.at[1]),
    ]
    for copy in locals_:
        copy.start()
    greet(
        [dev(wrap(x + 1), z, c), dev(wrap(x - 1), z, c), dev(x, wrap(z + 1), c), dev(x, wrap(z - 1), c)]
        + [other, above, below]
    )
    open1(0)
    far = pl.ds(pl.multiple_of((1 - c) * HALF, HALF), HALF)
    push(wd_ref.at[:, :, far], wdp_ref, other, wsem.at[0], wsem.at[1])
    relay1(0)
    open1(1)
    locals_[0].wait()
    for col in (0, 1):
        last1(0, col)
        lines_out(col)
    for col in (0, 1):
        lines_on(col)
    for col in (0, 1):
        fan(1, col, 0, first[col], own(1, col))
        share(1, col, first[col], second[col], own(1, col))
    relay1(1)
    for col in (0, 1):
        lines_in(col)
    for k, lo, target in ((0, 0, above), (2, 2, below), (1, 2, above), (3, 0, below)):
        ref = part_of(y, lo)
        push(ref, ref, target, ysend.at[k], yrecv.at[k])
    hand(0)
    for col in (0, 1):
        relay2(1, col, 0, source(col, 0))
    for col in (0, 1):
        last1(1, col)
        fan(1, col, 3, source(col, 3))
        share(1, col, source(col, 3), second[col])
    ref = part_of(wrap(y - 1), 0)
    expect(ref, yrecv.at[0])
    push(ref, ref, above, ysend.at[4], yrecv.at[4])
    ref = part_of(wrap(y + 1), 2)
    expect(ref, yrecv.at[2])
    push(ref, ref, below, ysend.at[5], yrecv.at[5])
    for k in (1, 2):
        for col in (0, 1):
            relay2(1, col, k, source(col, k))
    for col in (0, 1):
        last2(1, col, 0, source(col, 0))
    expect(part_of(wrap(y - 1), 2), yrecv.at[1])
    hand(3)
    expect(part_of(wrap(y + 1), 0), yrecv.at[3])
    hand(1)
    for col in (0, 1):
        relay2(1, col, 3, source(col, 3))
    expect(part_of(wrap(y + 2), 0), yrecv.at[4])
    expect(part_of(wrap(y + 2), 2), yrecv.at[5])
    hand(2)
    for k in (1, 2, 3):
        for col in (0, 1):
            last2(1, col, k, source(col, k))
    for col in (0, 1):
        for slot in range(16):
            expect(xg_ref.at[slot // 4, slot % 4, 1 - c, pl.ds(col * 32, 32)], drecv.at[col, slot])
    for d in range(4):
        expect(part_of(wrap(y + d), 0, 4, 1 - c), ydrecv.at[d])
    expect(wdp_ref, wsem.at[1])
    for copy in locals_[1:]:
        copy.wait()
    for copy in started:
        copy.wait_send()


def gather_rows(xmain, xparts, w_down):
    dma = pltpu.SemaphoreType.DMA
    return pl.pallas_call(
        gather_kernel,
        out_shape=(
            jax.ShapeDtypeStruct((4, 4, 2, ROWS, WHOLE), BF),
            jax.ShapeDtypeStruct((4, 4, 4, 2, ROWS, QUARTER), BF),
            pltpu.HBM((EXL, FFL, HALF), BF),
        ),
        in_specs=[pl.BlockSpec(memory_space=pltpu.VMEM)] * 2 + [pl.BlockSpec(memory_space=pltpu.HBM)],
        out_specs=(pl.BlockSpec(memory_space=pltpu.VMEM),) * 2
        + (pl.BlockSpec(memory_space=pltpu.HBM),),
        scratch_shapes=[
            dma((2, 2, 20)),
            dma((2, 2, 4)),
            dma((2, 2, 4, 4)),
            dma((2, 16)),
            dma((2, 16)),
            dma((6,)),
            dma((6,)),
            dma((4,)),
            dma((4,)),
            dma((2,)),
            dma((2,)),
        ],
        compiler_params=pltpu.CompilerParams(
            collective_id=0, has_side_effects=True, vmem_limit_bytes=18 * 1024 * 1024
        ),
        name="gather_rows",
    )(xmain, xparts, w_down)


def slot_numbers(shape, axis, gslot):
    s = lax.broadcasted_iota(jnp.int32, shape, axis)
    g = lax.broadcasted_iota(jnp.int32, shape, 1 - axis)
    expert = jnp.zeros(shape, jnp.int32)
    for k in range(1, shape[axis] // gslot):
        expert = expert + (s >= k * gslot).astype(jnp.int32)
    u = s - expert * gslot
    rank = (u * 205) >> 11
    want = jnp.where((g >> 6) == rank, u - rank * CAP + 1, -1)
    return want.astype(F32)


def expert_lanes(shape, axis, base, gslot):
    s = lax.broadcasted_iota(jnp.int32, shape, axis)
    e = lax.broadcasted_iota(jnp.int32, shape, 1 - axis)
    expert = jnp.zeros(shape, jnp.int32)
    for k in range(1, shape[axis] // gslot):
        expert = expert + (s >= k * gslot).astype(jnp.int32)
    return jnp.where(expert + base == e, 1.0, 0.0).astype(BF)


def up_kernel(base_ref, x_ref, xp_ref, wg_ref, wu_hbm, out_ref, tab_ref, xc, wu_ref, sem):
    load = pltpu.make_async_copy(wu_hbm, wu_ref, sem)
    load.start()
    tab_ref[...] = x_ref[:, :, MAIN:WHOLE]
    want = slot_numbers((EXL * PSLOT, PAIR), 0, PSLOT)
    lanes = expert_lanes((EXL * PSLOT, 128), 0, base_ref[0], PSLOT)

    @pl.loop(0, GROUPS // 2, unroll=2)
    def _(q):
        table = x_ref[q, :, MAIN : MAIN + 128]
        named = lax.dot_general(lanes, table, (((1,), (1,)), ((), ())), preferred_element_type=F32)
        pick = jnp.where(named == want, 1.0, 0.0).astype(BF)
        start = pl.multiple_of(q * PSLOT, 16)

        def keep(rows, cols):
            for e in range(EXL):
                xc[e, pl.ds(start, PSLOT), cols] = rows[e * PSLOT : (e + 1) * PSLOT].astype(BF)

        for n in range(MAIN // 512):
            cols = slice(n * 512, (n + 1) * 512)
            keep(jnp.dot(pick, x_ref[q, :, cols], preferred_element_type=F32), cols)
        for n in range(4):
            cols = slice(MAIN + n * QUARTER, MAIN + (n + 1) * QUARTER)
            keep(jnp.dot(pick, xp_ref[n, q], preferred_element_type=F32), cols)

    load.wait()

    @pl.loop(0, EXL)
    def _(e):
        rows = xc[e]
        gate = jnp.dot(rows, wg_ref[e], preferred_element_type=F32)
        up = jnp.dot(rows, wu_ref[e], preferred_element_type=F32)
        out_ref[e] = (gate / (1.0 + jnp.exp(-gate)) * up).astype(BF)


def experts_up(base, xg, xq, w_gate, w_up):
    return pl.pallas_call(
        up_kernel,
        out_shape=(
            jax.ShapeDtypeStruct((EXL, GROUPS * GSLOT, FFL), BF),
            jax.ShapeDtypeStruct((GROUPS // 2, PAIR, META), BF),
        ),
        in_specs=[pl.BlockSpec(memory_space=pltpu.SMEM)]
        + [pl.BlockSpec(memory_space=pltpu.VMEM)] * 3
        + [pl.BlockSpec(memory_space=pltpu.HBM)],
        out_specs=(pl.BlockSpec(memory_space=pltpu.VMEM),) * 2,
        scratch_shapes=[
            pltpu.VMEM((EXL, GROUPS * GSLOT, D), BF),
            pltpu.VMEM((EXL, D, FFL), BF),
            pltpu.SemaphoreType.DMA,
        ],
        cost_estimate=pl.CostEstimate(flops=7_000_000_000, bytes_accessed=30_000_000, transcendentals=0),
        compiler_params=pltpu.CompilerParams(vmem_limit_bytes=20 * 1024 * 1024),
        name="experts_up",
    )(base, xg, xq, w_gate, w_up)


def combine_kernel(
    inner_ref, meta, wd_hbm, wdp_hbm, out_ref,
    inner2, wdh, outc, want, yp, st1, fin1, st2, fin2, fin3,
    lsem, isem, s1, r1, s2, r2, s3, r3,
):
    x, z, c, y = coords()

    def dev(xx, zz, cc, yy):
        return (xx * 8 + zz * 2 + cc, yy)

    other = dev(x, z, 1 - c, y)
    waits = []

    def ship(src, dst, target, send, recv):
        copy = pltpu.make_async_remote_copy(
            src_ref=src, dst_ref=dst, send_sem=send, recv_sem=recv, device_id=target, device_id_type=MESH
        )
        copy.start()
        waits.append(copy)
        return copy

    def expect(ref, sem):
        pltpu.make_async_copy(ref, ref, sem).wait()

    near = pl.ds(pl.multiple_of(c * HALF, HALF), HALF)
    loads = [
        pltpu.make_async_copy(wd_hbm.at[:, :, near], wdh.at[c], lsem.at[0]),
        pltpu.make_async_copy(wdp_hbm, wdh.at[1 - c], lsem.at[1]),
    ]
    for load in loads:
        load.start()
    want[...] = slot_numbers((GROUP, 2 * EXL * GSLOT), 1, GSLOT)
    lanes = expert_lanes((128, 2 * EXL * GSLOT), 1, (x * 4 + z) * 2 * EXL, GSLOT)
    greet(
        [dev(wrap(x + 1), z, c, y), dev(wrap(x - 1), z, c, y), dev(x, wrap(z + 1), c, y), dev(x, wrap(z - 1), c, y)]
        + [other]
        + [dev(x, z, core, wrap(y + k)) for k in (1, 2, 3) for core in (0, 1)]
    )
    swap = ship(inner_ref, inner2, other, isem.at[0], isem.at[1])

    def down(core, source):
        @pl.loop(0, EXL, unroll=EXL)
        def _(e):
            row = pl.multiple_of((core * EXL + e) * GSLOT, 8)
            for n in range(2):
                cols = slice(n * BLK, (n + 1) * BLK)
                part = jnp.dot(source[e], wdh[core, e, :, cols], preferred_element_type=F32)
                for q in range(GROUPS):
                    outc[n, q, pl.ds(row, GSLOT), :] = part[q * GSLOT : (q + 1) * GSLOT]

    loads[0].wait()
    down(c, inner_ref)
    loads[1].wait()
    swap.wait_recv()
    down(1 - c, inner2)

    def scatter(col, start, count):
        @pl.loop(0, 2 * count, unroll=4 if count == 4 else 2)
        def _(i):
            q = wrap(x + start + i // 2) * 2 + lax.rem(i, 2)
            named = jnp.dot(meta[q, :, 0:128], lanes, preferred_element_type=F32)
            gate = jnp.dot(meta[q, :, 128:256], lanes, preferred_element_type=F32)
            mix = jnp.where(named == want[...], gate, 0.0).astype(BF)
            part = jnp.dot(mix, outc[col, q].astype(BF), preferred_element_type=F32).astype(BF)
            xx = q // 2
            for k in range(2):
                piece = part[k * 128 : (k + 1) * 128]
                zz = lax.rem(q, 2) * 2 + k
                if col == 0:
                    yp[0, xx, zz] = piece
                else:
                    yp[1, zz, xx] = piece

    first, second = (x, z), (z, x)

    def fdev(col, f):
        return dev(f, z, c, y) if col == 0 else dev(x, f, c, y)

    def sdev(col, s):
        return dev(x, s, c, y) if col == 0 else dev(s, z, c, y)

    def open0(col):
        p = first[col]
        up, dn = fdev(col, wrap(p + 1)), fdev(col, wrap(p - 1))
        ship(yp.at[col, wrap(p + 2), pl.ds(0, 2)], st1.at[col, 0], up, s1.at[col, 0], r1.at[col, 0])
        ship(yp.at[col, wrap(p + 2), pl.ds(2, 2)], st1.at[col, 1], dn, s1.at[col, 1], r1.at[col, 1])

    def open1(col):
        p = first[col]
        up, dn = fdev(col, wrap(p + 1)), fdev(col, wrap(p - 1))
        ship(yp.at[col, wrap(p + 1), pl.ds(2, 2)], fin1.at[col, 0, pl.ds(2, 2)], up, s1.at[col, 2], r1.at[col, 2])
        ship(yp.at[col, wrap(p - 1), pl.ds(0, 2)], fin1.at[col, 1, pl.ds(0, 2)], dn, s1.at[col, 3], r1.at[col, 3])

    def mid1(col):
        p = first[col]
        up, dn = fdev(col, wrap(p + 1)), fdev(col, wrap(p - 1))
        for side, (f, lo, target) in enumerate(((wrap(p + 1), 0, up), (wrap(p - 1), 2, dn))):
            expect(st1.at[col, side], r1.at[col, side])
            for k in range(2):
                acc = yp[col, f, lo + k].astype(F32) + st1[col, side, k].astype(F32)
                yp[col, f, lo + k] = acc.astype(BF)
            ship(
                yp.at[col, f, pl.ds(lo, 2)],
                fin1.at[col, side, pl.ds(lo, 2)],
                target,
                s1.at[col, 4 + side],
                r1.at[col, 4 + side],
            )

    def end1(col):
        p, s = first[col], second[col]
        for side, lo in ((0, 2), (1, 0), (0, 0), (1, 2)):
            expect(
                fin1.at[col, side, pl.ds(lo, 2)],
                r1.at[col, {(0, 2): 2, (1, 0): 3, (0, 0): 4, (1, 2): 5}[(side, lo)]],
            )
        up, dn = sdev(col, wrap(s + 1)), sdev(col, wrap(s - 1))

        def fold(t):
            acc = yp[col, p, t].astype(F32) + fin1[col, 0, t].astype(F32) + fin1[col, 1, t].astype(F32)
            yp[col, p, t] = acc.astype(BF)

        lo, hi = pl.ds(0, 64), pl.ds(64, 64)
        t = wrap(s + 2)
        fold(t)
        ship(yp.at[col, p, t, lo], st2.at[col, 0], up, s2.at[col, 0], r2.at[col, 0])
        ship(yp.at[col, p, t, hi], st2.at[col, 1], dn, s2.at[col, 1], r2.at[col, 1])
        t = wrap(s + 1)
        fold(t)
        ship(yp.at[col, p, t, hi], fin2.at[col, 0, hi], up, s2.at[col, 2], r2.at[col, 2])
        t = wrap(s - 1)
        fold(t)
        ship(yp.at[col, p, t, lo], fin2.at[col, 1, lo], dn, s2.at[col, 3], r2.at[col, 3])
        fold(s)

    def mid2(col):
        p, s = first[col], second[col]
        up, dn = sdev(col, wrap(s + 1)), sdev(col, wrap(s - 1))
        for side, (t, lo, target) in enumerate(((wrap(s + 1), 0, up), (wrap(s - 1), 64, dn))):
            expect(st2.at[col, side], r2.at[col, side])
            acc = yp[col, p, t, lo : lo + 64].astype(F32) + st2[col, side].astype(F32)
            yp[col, p, t, lo : lo + 64] = acc.astype(BF)
            rows = pl.ds(lo, 64)
            ship(
                yp.at[col, p, t, rows], fin2.at[col, side, rows], target, s2.at[col, 4 + side], r2.at[col, 4 + side]
            )

    def end2(col):
        p, s = first[col], second[col]
        for side, lo, k in ((0, 64, 2), (1, 0, 3), (0, 0, 4), (1, 64, 5)):
            expect(fin2.at[col, side, pl.ds(lo, 64)], r2.at[col, k])
        acc = yp[col, p, s].astype(F32) + fin2[col, 0].astype(F32) + fin2[col, 1].astype(F32)
        yp[col, p, s] = acc.astype(BF)
        goal = 2 * c + col

        def final(core, target, k):
            pltpu.make_async_remote_copy(
                src_ref=yp.at[col, p, s, pl.ds(pl.multiple_of(core * 64, 64), 64)],
                dst_ref=fin3.at[k],
                send_sem=s3.at[col, core],
                recv_sem=r3.at[k],
                device_id=target,
                device_id_type=MESH,
            ).start()

        @pl.when(y == goal)
        def _():
            final(1 - c, other, 0)

        for k in (1, 2, 3):

            @pl.when(wrap(goal + k) == y)
            def _():
                for core in (0, 1):
                    final(core, dev(x, z, core, goal), k)

    def end3(col):
        p, s = first[col], second[col]
        half = yp.at[col, p, s, pl.ds(0, 64)]
        expect(half, s3.at[col, 1 - c])

        @pl.when(y != 2 * c + col)
        def _():
            expect(half, s3.at[col, c])

        @pl.when(y == 2 * c + col)
        def _():
            acc = yp[col, p, s, pl.ds(pl.multiple_of(c * 64, 64), 64)].astype(F32)
            for k in (1, 2, 3):
                acc = acc + fin3[k].astype(F32)
            out_ref[...] = acc.astype(BF)

    scatter(1, 0, 4)
    open0(1)
    open1(1)
    scatter(0, 2, 1)
    open0(0)
    scatter(0, 3, 3)
    open1(0)
    for step in (mid1, end1, mid2, end2):
        for col in (1, 0):
            step(col)
    for k in (1, 2, 3):
        expect(fin3.at[k], r3.at[k])
    end3(0)
    end3(1)

    @pl.when(y // 2 != c)
    def _():
        expect(fin3.at[0], r3.at[0])
        acc = fin3[0].astype(F32)
        for k in (1, 2, 3):
            acc = acc + fin3[k].astype(F32)
        out_ref[...] = acc.astype(BF)

    for copy in waits:
        copy.wait_send()


def combine(inner, tables, w_down, wd_far):
    return pl.pallas_call(
        combine_kernel,
        out_shape=jax.ShapeDtypeStruct((ROWS, BLK), BF),
        in_specs=[pl.BlockSpec(memory_space=pltpu.VMEM)] * 2 + [pl.BlockSpec(memory_space=pltpu.HBM)] * 2,
        out_specs=pl.BlockSpec(memory_space=pltpu.VMEM),
        scratch_shapes=[
            pltpu.VMEM((EXL, GROUPS * GSLOT, FFL), BF),
            pltpu.VMEM((2, EXL, FFL, HALF), BF),
            pltpu.VMEM((2, GROUPS, 2 * EXL * GSLOT, BLK), F32),
            pltpu.VMEM((GROUP, 2 * EXL * GSLOT), F32),
            pltpu.VMEM((2, 4, 4, 128, BLK), BF),
            pltpu.VMEM((2, 2, 2, 128, BLK), BF),
            pltpu.VMEM((2, 2, 4, 128, BLK), BF),
            pltpu.VMEM((2, 2, 64, BLK), BF),
            pltpu.VMEM((2, 2, 128, BLK), BF),
            pltpu.VMEM((4, 64, BLK), BF),
            pltpu.SemaphoreType.DMA((2,)),
            pltpu.SemaphoreType.DMA((2,)),
            pltpu.SemaphoreType.DMA((2, 6)),
            pltpu.SemaphoreType.DMA((2, 6)),
            pltpu.SemaphoreType.DMA((2, 6)),
            pltpu.SemaphoreType.DMA((2, 6)),
            pltpu.SemaphoreType.DMA((2, 2)),
            pltpu.SemaphoreType.DMA((4,)),
        ],
        compiler_params=pltpu.CompilerParams(
            collective_id=1, has_side_effects=True, vmem_limit_bytes=38 * 1024 * 1024
        ),
        name="combine",
    )(inner, tables, w_down, wd_far)


def attend_page(query, page, length):
    scores = lax.dot_general(query, page, (((0,), (0,)), ((), ())), preferred_element_type=F32)
    scores = scores * SCORE_SCALE
    live = lax.broadcasted_iota(jnp.int32, scores.shape, 1) < length
    scores = jnp.where(live, scores, MASK_FLOOR)
    weight = jnp.exp(scores - jnp.max(scores, axis=1, keepdims=True))
    total = jnp.sum(weight, axis=1, keepdims=True)
    blended = lax.dot_general(
        weight.astype(BF), page[:LAT], (((1,), (1,)), ((), ())), preferred_element_type=F32
    )
    return (blended * (1.0 / total)).astype(BF)


def attend_kernel(dev_ref, lens_ref, q_ref, page_ref, out_ref):
    count = q_ref.shape[0]
    base = dev_ref[0] * 16 + pl.program_id(0) * count
    for k in range(count):
        out_ref[k] = attend_page(q_ref[k], page_ref[k], lens_ref[base + k])


def attend(dev, lens, queries, pages):
    count, width, heads = queries.shape
    ctx = pages.shape[2]
    step = 4
    return pl.pallas_call(
        attend_kernel,
        out_shape=jax.ShapeDtypeStruct((count, heads, LAT), BF),
        grid_spec=pltpu.PrefetchScalarGridSpec(
            num_scalar_prefetch=2,
            grid=(count // step,),
            in_specs=[
                pl.BlockSpec((step, width, heads), lambda r, *_: (r, 0, 0)),
                pl.BlockSpec((step, width, ctx), lambda r, *_: (r, 0, 0)),
            ],
            out_specs=pl.BlockSpec((step, heads, LAT), lambda r, *_: (r, 0, 0)),
        ),
        cost_estimate=pl.CostEstimate(flops=2_400_000_000, bytes_accessed=20_000_000, transcendentals=0),
        name="attend",
    )(dev, lens, queries, pages)


def attend_one_kernel(dev_ref, slot_ref, mask_ref, lens_ref, q_ref, page_ref, all_ref, out_ref):
    partner = jnp.bitwise_xor(dev_ref[0], mask_ref[0] * 4)
    length = lens_ref[partner * 16 + slot_ref[partner]]
    out_ref[0] = attend_page(q_ref[0], page_ref[...], length)


def attend_one(dev, slots, mask, lens, queries, page, attended):
    count, width, heads = queries.shape
    return pl.pallas_call(
        attend_one_kernel,
        out_shape=jax.ShapeDtypeStruct(attended.shape, BF),
        grid_spec=pltpu.PrefetchScalarGridSpec(
            num_scalar_prefetch=4,
            grid=(1,),
            in_specs=[
                pl.BlockSpec((1, width, heads), lambda r, dev, slot, *_: (slot[dev[0]], 0, 0)),
                pl.BlockSpec(page.shape, lambda r, *_: (0, 0)),
                pl.BlockSpec(memory_space=pl.ANY),
            ],
            out_specs=pl.BlockSpec((1, heads, LAT), lambda r, dev, slot, *_: (slot[dev[0]], 0, 0)),
        ),
        input_output_aliases={6: 0},
        name="attend_one",
    )(dev, slots, mask, lens, queries, page, attended)


def trade(page, bits, shift, steps, beside):
    count = lax.axis_size("ep")

    def branch(m):
        def run(block):
            if m:
                block = lax.ppermute(block, "ep", [(i, i ^ (m << shift)) for i in range(count)])
            return block, beside()

        return run

    return lax.switch(bits, [branch(m) for m in range(steps)], page)


def prepare_kernel(dev_ref, slot_ref, x_ref, ids_ref, gates_ref, page_ref, out_ref, parts_ref, own_ref):
    own_ref[...] = page_ref[0]
    top = ids_ref.shape[0]
    expert = lax.broadcasted_iota(jnp.int32, (128, ROWS), 0)
    chosen = jnp.zeros((128, ROWS), F32)
    gates = jnp.zeros((128, ROWS), F32)
    for k in range(top):
        hit = expert == ids_ref[k : k + 1, :]
        chosen = jnp.where(hit, 1.0, chosen)
        gates = jnp.where(hit, gates_ref[k : k + 1, :], gates)
    row = lax.broadcasted_iota(jnp.int32, (ROWS, ROWS), 0)
    col = lax.broadcasted_iota(jnp.int32, (ROWS, ROWS), 1)
    upto = jnp.where(row >= col, 1.0, 0.0).astype(BF)
    same = jnp.where(row == col, 1.0, 0.0).astype(BF)
    flip = functools.partial(
        lax.dot_general, dimension_numbers=(((1,), (1,)), ((), ())), preferred_element_type=F32
    )
    chosen = chosen.astype(BF)
    place = jnp.where(flip(same, chosen) > 0.5, flip(upto, chosen), 0.0)
    out_ref[:, :MAIN] = x_ref[:, :MAIN]
    out_ref[:, MAIN : MAIN + 128] = place.astype(BF)
    out_ref[:, MAIN + 128 :] = flip(same, gates.astype(BF)).astype(BF)
    for k in range(4):
        parts_ref[k] = x_ref[:, MAIN + k * QUARTER : MAIN + (k + 1) * QUARTER]


def prepare(dev, slots, hidden, ids, gates, pages):
    count, width, ctx = pages.shape

    def whole(array):
        return pl.BlockSpec(array.shape, lambda r, *_: (0, 0))

    return pl.pallas_call(
        prepare_kernel,
        out_shape=(
            jax.ShapeDtypeStruct((ROWS, WHOLE), BF),
            jax.ShapeDtypeStruct((4, ROWS, QUARTER), BF),
            jax.ShapeDtypeStruct((width, ctx), BF),
        ),
        grid_spec=pltpu.PrefetchScalarGridSpec(
            num_scalar_prefetch=2,
            grid=(1,),
            in_specs=[
                whole(hidden),
                whole(ids),
                whole(gates),
                pl.BlockSpec((1, width, ctx), lambda r, dev, slot: (slot[dev[0]], 0, 0)),
            ],
            out_specs=(
                pl.BlockSpec((ROWS, WHOLE), lambda r, *_: (0, 0)),
                pl.BlockSpec((4, ROWS, QUARTER), lambda r, *_: (0, 0, 0)),
                pl.BlockSpec((width, ctx), lambda r, *_: (0, 0)),
            ),
        ),
        name="prepare",
    )(dev, slots, hidden, ids, gates, pages)


def local(
    cache_pages,
    queries,
    lengths,
    swap_slot,
    swap_mask,
    hidden,
    expert_ids,
    gate_weights,
    w_gate,
    w_up,
    w_down,
):
    ep_rank = lax.axis_index("ep").astype(jnp.int32)
    groups = lax.axis_size("tp")
    tp_rank = lax.axis_index("tp").astype(jnp.int32)
    device = ep_rank * groups + tp_rank
    mask = swap_mask[0]
    dev = device.reshape(1)
    pages = jnp.swapaxes(cache_pages, 1, 2)
    asked = jnp.swapaxes(queries, 1, 2)
    w_down = pltpu.with_memory_space_constraint(w_down, pltpu.HBM)
    xmain, xparts, own_page = prepare(dev, swap_slot, hidden, expert_ids.T, gate_weights.T, pages)
    page, attended = trade(
        own_page, jnp.right_shift(mask, 3), 3, 4, lambda: attend(dev, lengths, asked, pages)
    )
    xg, xq, wd_far = gather_rows(xmain, xparts, w_down)
    xg = xg.reshape(GROUPS // 2, PAIR, WHOLE)
    xq = xq.reshape(4, GROUPS // 2, PAIR, QUARTER)
    base = (ep_rank * EXL).reshape(1)
    page, (inner, tables) = trade(
        page, jnp.bitwise_and(mask, 7), 0, 8, lambda: experts_up(base, xg, xq, w_gate, w_up)
    )
    moe_rows = combine(inner, tables.reshape(GROUPS, GROUP, META), w_down, wd_far)
    attended = attend_one(dev, swap_slot, swap_mask, lengths, asked, page, attended)
    return attended, moe_rows


def solution(mesh):
    in_specs = (
        P(("ep", "tp"), None, None),
        P(("ep", "tp"), None, None),
        P(),
        P(),
        P(),
        P("ep", None),
        P("ep", None),
        P("ep", None),
        P("ep", None, "tp"),
        P("ep", None, "tp"),
        P("ep", "tp", None),
    )
    out_specs = (P(("ep", "tp"), None, None), P("ep", "tp"))
    return jax.shard_map(local, mesh=mesh, in_specs=in_specs, out_specs=out_specs, check_vma=False)
```
